128 devices in a mesh: blk: 4 (over x), tok: 32 (over y, z, core).
Axes of the slice: x: 4, y: 4, z: 4, core: 2. Of those that a mesh axis runs over, the one named last changes fastest.
Arguments:
- tokens: bfloat16 [32, 1024, 1664], P('tok', 'blk'), may hold values from -6 to 6
- segment_ids: int32 [32, 1024], P('tok'), may hold values from 0 to 31, as said below
- merge_index: int32 [32, 256, 4], P('tok'), may hold values from 0 to 1023, as said below
- segment_owner: int32 [32, 32], P('tok'), may hold values from 0 to 31, each once within a row
- ln1_gain: float32 [1664], replicated, may hold values from 0.1 to 1.9
- ln1_bias: float32 [1664], replicated, may hold values from -4 to 4
- w_qkv: bfloat16 [3, 1664, 1664], P(None, 'tok', 'blk'), may hold values from -0.15625 to 0.15625
- qkv_bias: float32 [3, 1664], P(None, 'blk'), may hold values from -6 to 6
- w_out: bfloat16 [1664, 1664], P('blk', 'tok'), may hold values from -0.15625 to 0.15625
- out_bias: float32 [1664], replicated, may hold values from -6 to 6
- ln2_gain: float32 [1664], replicated, may hold values from 0.1 to 1.9
- ln2_bias: float32 [1664], replicated, may hold values from -4 to 4
- w_fc1: bfloat16 [1664, 8192], P(None, 'blk'), may hold values from -0.15625 to 0.15625
- fc1_bias: float32 [8192], P('blk'), may hold values from -6 to 6
- w_fc2: bfloat16 [8192, 1664], P('blk'), may hold values from -0.0625 to 0.0625
- fc2_bias: float32 [1664], replicated, may hold values from -6 to 6
- ln3_gain: float32 [1664], replicated, may hold values from 0.1 to 1.9
- ln3_bias: float32 [1664], replicated, may hold values from -4 to 4
- w_proj: bfloat16 [6656, 1664], P('tok', 'blk'), may hold values from -0.078125 to 0.078125
- proj_bias: float32 [1664], P('blk'), may hold values from -6 to 6
Outputs:
- returned: bfloat16 [32, 32, 16, 1664], P('tok', None, None, 'blk')
The draws below stay inside these ranges and needn't reach their ends.
Inputs may be any that keep to these rules, and one draw needn't show every extreme that they name: `segment_ids`: within a block each segment holds 4 to 64 tokens, one exactly 64; the four tokens of one row of merge_index share a segment. `merge_index`: the rows of one block name each token of the block exactly once. `segment_owner`: each block's row is a permutation of the owners.
All inputs are finite; a program needn't handle non-finite values.
Results may differ from the reference program's by a relative error of at most 0.015.
Values may be sent and summed in bfloat16 or wider, within the bound.
A program may use at most 128 MiB of HBM per device.

```python
import jax
import jax.numpy as jnp
from jax import lax

D = 1664
HEADS = 16
HD = 104
FF = 8192
TOK_DEV = 1024
MERGED_DEV = 256
SEG_DEV = 32
SLOT = 16
N_TOK = 32


def block_layout(key):
    others_count = SEG_DEV - 1
    spare_units = MERGED_DEV - SLOT - others_count
    base_length = spare_units // others_count
    surplus_units = spare_units - base_length * others_count
    reach_max = max(0, min(base_length, SLOT - 2 - base_length))
    half_count = others_count // 2
    key_order, key_shift, key_pairs, key_place, key_tokens = jax.random.split(key, 5)
    token_shuffle = jax.random.permutation(key_order, others_count)
    extra_allotment = (token_shuffle < surplus_units).astype(jnp.int32)
    shifts = jax.random.randint(key_shift, (half_count,), 0, reach_max + 1).astype(jnp.int32)
    pair_grouped = jnp.zeros((others_count,), jnp.int32)
    pair_grouped = pair_grouped.at[0:2 * half_count:2].set(shifts)
    pair_grouped = pair_grouped.at[1:2 * half_count:2].set(-shifts)
    pair_grouped = pair_grouped[jax.random.permutation(key_pairs, others_count)]
    remaining_length = 1 + base_length + extra_allotment + pair_grouped
    special = jax.random.randint(key_place, (), 0, SEG_DEV).astype(jnp.int32)
    seg_index = jnp.arange(SEG_DEV, dtype=jnp.int32)
    source = jnp.clip(seg_index - (seg_index > special).astype(jnp.int32), 0, others_count - 1)
    lengths = jnp.where(seg_index == special, SLOT, remaining_length[source]).astype(jnp.int32)
    seg_ends = jnp.cumsum(lengths)
    quad_index = jnp.arange(MERGED_DEV, dtype=jnp.int32)
    quad_seg = jnp.sum((quad_index[:, None] >= seg_ends[None, :]).astype(jnp.int32), axis=1).astype(jnp.int32)
    token_order = jax.random.permutation(key_tokens, TOK_DEV).astype(jnp.int32)
    merge_rows = token_order.reshape(MERGED_DEV, 4)
    segment_row = jnp.zeros((TOK_DEV,), jnp.int32).at[token_order].set(jnp.repeat(quad_seg, 4))
    return (segment_row, merge_rows)


def all_layouts(key):
    block_keys = jax.random.split(jax.random.fold_in(key, 11), N_TOK)
    return jax.vmap(block_layout)(block_keys)


def draw_segment_ids(key, part):
    return all_layouts(key)[0]


def draw_merge_index(key, part):
    return all_layouts(key)[1]


def level_of(own_key, extent, shards, least, high):
    loudness, own = 1.0, jax.random.fold_in(own_key, 6)
    for dim, shards_of in shards:
        heights = jnp.exp(jax.random.uniform(jax.random.fold_in(own, dim), (shards_of,), jnp.float32, least / len(shards), high / len(shards)))
        loudness = loudness * jnp.repeat(heights, extent[dim] // shards_of).reshape([-1 if axis == dim else 1 for axis in range(len(extent))])
    return loudness


def noise(stream_key, extent, scale, limit, pieces=(), kind=jnp.bfloat16):
    level = level_of(stream_key, extent, pieces, -0.22, 0.18) if pieces else 1.0
    result = jax.random.normal(stream_key, extent, jnp.float32) * scale * level
    return jnp.minimum(jnp.maximum(result, -limit), limit).astype(kind)


def setup_inputs(seed: int = 0) -> dict:
    streams_of = jax.random.split(jax.random.key(seed), 21)
    tokens = noise(streams_of[0], (N_TOK, TOK_DEV, D), 1.0, 6.0, ((0, 32), (1, 4)))
    segment_ids = draw_segment_ids(jax.random.fold_in(streams_of[20], 71), 0)
    merge_index = draw_merge_index(jax.random.fold_in(streams_of[20], 71), 0)
    segment_owner = jax.vmap(lambda own: jax.random.permutation(own, N_TOK))(jax.random.split(streams_of[3], N_TOK)).reshape((N_TOK, SEG_DEV)).astype(jnp.int32)
    ln1_gain = jnp.clip(1.0 + 0.18 * jax.random.normal(streams_of[4], (D,), jnp.float32), 0.1, 1.9)
    ln1_bias = noise(streams_of[5], (D,), 0.3, 4.0, (), jnp.float32)
    w_qkv = noise(streams_of[6], (3, D, D), D ** -0.5, 0.15625, ((1, 32), (2, 4)))
    qkv_bias = noise(streams_of[7], (3, D), 0.5, 6.0, ((1, 4),), jnp.float32)
    w_out = noise(streams_of[8], (D, D), D ** -0.5, 0.15625, ((0, 4), (1, 32)))
    out_bias = noise(streams_of[9], (D,), 0.5, 6.0, (), jnp.float32)
    ln2_gain = jnp.clip(1.0 + 0.18 * jax.random.normal(streams_of[10], (D,), jnp.float32), 0.1, 1.9)
    ln2_bias = noise(streams_of[11], (D,), 0.3, 4.0, (), jnp.float32)
    w_fc1 = noise(streams_of[12], (D, FF), D ** -0.5, 0.15625, ((1, 4),))
    fc1_bias = noise(streams_of[13], (FF,), 0.5, 6.0, ((0, 4),), jnp.float32)
    w_fc2 = noise(streams_of[14], (FF, D), FF ** -0.5, 0.0625, ((0, 4),))
    fc2_bias = noise(streams_of[15], (D,), 0.5, 6.0, (), jnp.float32)
    ln3_gain = jnp.clip(1.0 + 0.18 * jax.random.normal(streams_of[16], (D,), jnp.float32), 0.1, 1.9)
    ln3_bias = noise(streams_of[17], (D,), 0.3, 4.0, (), jnp.float32)
    w_proj = noise(streams_of[18], (4 * D, D), (4 * D) ** -0.5, 0.078125, ((0, 32), (1, 4)))
    proj_bias = noise(streams_of[19], (D,), 0.5, 6.0, ((0, 4),), jnp.float32)
    return {"tokens": tokens, "segment_ids": segment_ids, "merge_index": merge_index, "segment_owner": segment_owner, "ln1_gain": ln1_gain, "ln1_bias": ln1_bias, "w_qkv": w_qkv, "qkv_bias": qkv_bias, "w_out": w_out, "out_bias": out_bias, "ln2_gain": ln2_gain, "ln2_bias": ln2_bias, "w_fc1": w_fc1, "fc1_bias": fc1_bias, "w_fc2": w_fc2, "fc2_bias": fc2_bias, "ln3_gain": ln3_gain, "ln3_bias": ln3_bias, "w_proj": w_proj, "proj_bias": proj_bias}


EPS = 1e-06

def layer_norm(input_tensors, scales, offset):
    input_tensors = input_tensors.astype(jnp.float32)
    center = input_tensors - lax.optimization_barrier(jnp.mean(input_tensors, axis=-1, keepdims=True))
    spread = lax.optimization_barrier(jnp.mean(center * center, axis=-1, keepdims=True))
    return center * lax.rsqrt(spread + EPS) * scales + offset

def rounded(input_tensors):
    return lax.optimization_barrier(input_tensors.astype(jnp.bfloat16)).astype(jnp.float32)

def reference(tokens, segment_ids, merge_index, segment_owner, ln1_gain, ln1_bias, w_qkv, qkv_bias, w_out, out_bias, ln2_gain, ln2_bias, w_fc1, fc1_bias, w_fc2, fc2_bias, ln3_gain, ln3_bias, w_proj, proj_bias):
    score_scale = 1.0 / HD ** 0.5

    def encode_block(input_tensors):
        tok_block, segment_row, merge_rows, owners_here = input_tensors
        normed_one = rounded(layer_norm(tok_block, ln1_gain, ln1_bias))
        projected_qkv = jnp.einsum('td,cde->cte', normed_one, w_qkv.astype(jnp.float32)) + qkv_bias[:, None, :]
        projected_qkv = rounded(projected_qkv).reshape(3, TOK_DEV, HEADS, HD)
        queries, key_rows, values = (projected_qkv[0], projected_qkv[1], projected_qkv[2])
        scores = jnp.einsum('qhe,khe->hqk', queries, key_rows) * score_scale
        allowed = segment_row[:, None] == segment_row[None, :]
        weights = jnp.where(allowed[None], jnp.exp(scores), 0.0)
        attn_probs = rounded(weights / lax.optimization_barrier(jnp.sum(weights, axis=-1, keepdims=True)))
        attended = jnp.einsum('hqk,khe->qhe', attn_probs, values).reshape(TOK_DEV, D)
        attended = attended.astype(jnp.bfloat16)
        after_attn = tok_block.astype(jnp.float32) + jnp.dot(attended, w_out, preferred_element_type=jnp.float32) + out_bias
        normed_two = layer_norm(after_attn, ln2_gain, ln2_bias).astype(jnp.bfloat16)
        pre_act = jnp.dot(normed_two, w_fc1, preferred_element_type=jnp.float32) + fc1_bias
        hidden_act = jax.nn.gelu(pre_act, approximate=False).astype(jnp.bfloat16)
        layer_out = (after_attn + jnp.dot(hidden_act, w_fc2, preferred_element_type=jnp.float32) + fc2_bias).astype(jnp.bfloat16)
        final_norm = layer_norm(layer_out, ln3_gain, ln3_bias).astype(jnp.bfloat16)
        merged = jnp.take(final_norm, merge_rows.reshape(-1), axis=0).reshape(MERGED_DEV, 4 * D)
        projected = (jnp.dot(merged, w_proj, preferred_element_type=jnp.float32) + proj_bias).astype(jnp.bfloat16)
        seg_rows = jnp.take(segment_row, merge_rows[:, 0])
        seg_match = (seg_rows[:, None] == jnp.arange(SEG_DEV, dtype=jnp.int32)[None, :]).astype(jnp.int32)
        owner_rows = lax.optimization_barrier(jnp.sum(seg_match * owners_here[None, :], axis=1)).astype(jnp.int32)
        segment_matches = (owner_rows[:, None] == jnp.arange(N_TOK, dtype=jnp.int32)[None, :]).astype(jnp.int32)
        before = jnp.cumsum(segment_matches, axis=0) - segment_matches
        order_in = lax.optimization_barrier(jnp.sum(before * segment_matches, axis=1)).astype(jnp.int32)
        return (projected, owner_rows, order_in)
    projected, owner_rows, order_in = lax.map(encode_block, (tokens, segment_ids, merge_index, segment_owner))
    source = jnp.broadcast_to(jnp.arange(N_TOK, dtype=jnp.int32)[:, None], owner_rows.shape)
    returned = jnp.zeros((N_TOK, N_TOK, SLOT, D), jnp.bfloat16)
    return returned.at[owner_rows, source, order_in].set(projected)
```

```python
import math

import jax
import jax.numpy as jnp
from jax import lax
from jax.experimental import pallas as pl
from jax.experimental.pallas import tpu as pltpu
from jax.sharding import PartitionSpec as P

HD = 104
HPAD = 128
EPS = 1e-06
BF = jnp.bfloat16
F32 = jnp.float32
MESH_ID = pl.DeviceIdType.MESH
VLIM = 65000 * 1024
VM = pl.BlockSpec(memory_space=pltpu.VMEM)
ANY = pl.BlockSpec(memory_space=pl.ANY)


def position():
    x = lax.axis_index("blk")
    t = lax.axis_index("tok")
    return x, t // 8, (t // 2) % 4, t % 2


def tok_of(y, z, c):
    return ((y % 4) * 4 + z % 4) * 2 + c


def rcopy(src, dst, ssem, rsem, dev):
    return pltpu.make_async_remote_copy(
        src_ref=src, dst_ref=dst, send_sem=ssem, recv_sem=rsem, device_id=dev, device_id_type=MESH_ID
    )


def x_dev(x, off):
    return {"blk": (x + off) % 4}


def meet(peers):
    bar = pltpu.get_barrier_semaphore()
    for dev in peers:
        pl.semaphore_signal(bar, inc=1, device_id=dev, device_id_type=MESH_ID)
    pl.semaphore_wait(bar, len(peers))


def x_peers():
    x, y, z, c = position()
    return [x_dev(x, 1), x_dev(x, 3)]


def tok_peers():
    x, y, z, c = position()
    return [
        {"tok": tok_of(y, z + 1, c)},
        {"tok": tok_of(y, z + 3, c)},
        {"tok": tok_of(y + 1, z, c)},
        {"tok": tok_of(y + 3, z, c)},
        {"tok": tok_of(y, z, 1 - c)},
    ]


class RingGather:
    def __init__(self, own, half, ss, rs):
        x = lax.axis_index("blk")
        right, left = x_dev(x, 1), x_dev(x, 3)

        def send(view, src, i, k, dev):
            return rcopy(view, half(src, i), ss(k), rs(k), dev)

        me, lo, hi = x, (x + 3) % 4, (x + 1) % 4
        self.c = [
            send(own(0), me, 0, 0, right),
            send(own(1), me, 1, 1, right),
            send(own(1), me, 1, 2, left),
            send(own(0), me, 0, 3, left),
            send(half(lo, 0), lo, 0, 4, right),
            send(half(hi, 1), hi, 1, 5, left),
        ]

    def start(self):
        for k in (0, 2, 1, 3):
            self.c[k].start()

    def relay(self):
        self.c[0].wait_recv()
        self.c[4].start()
        self.c[2].wait_recv()
        self.c[5].start()

    def wait_near(self):
        self.c[1].wait_recv()
        self.c[3].wait_recv()

    def wait_far(self):
        self.c[4].wait_recv()
        self.c[5].wait_recv()

    def finish(self):
        for c in self.c:
            c.wait_send()


class TokGather:
    OFF = (0, 3, 1, 2)

    def __init__(self, own, slots, half, zs, zr, ys, yr, cs, cr):
        x, y, z, c = position()
        self.slots, self.half = slots, half
        self.pos = (y, z, c)
        me = tok_of(y, z, c)

        def dev(yy, zz, cc):
            return {"tok": tok_of(yy, zz, cc)}

        def slot(yy, zz):
            return slots.at[tok_of(yy, zz, c)]

        zp, zm = dev(y, z + 1, c), dev(y, z + 3, c)
        yp, ym = dev(y + 1, z, c), dev(y + 3, z, c)
        sib = dev(y, z, 1 - c)
        self.zc = [
            rcopy(own, slots.at[me], zs.at[0], zr.at[0], zp),
            rcopy(own, slots.at[me], zs.at[1], zr.at[1], zm),
            rcopy(half(slot(y, z + 3), 0), half(slot(y, z + 3), 0), zs.at[2], zr.at[2], zp),
            rcopy(half(slot(y, z + 1), 1), half(slot(y, z + 1), 1), zs.at[3], zr.at[3], zm),
        ]
        self.yc = []
        for i, o in enumerate(self.OFF):
            src = own if i == 0 else slot(y, z + o)
            here = slot(y, z + o)
            up, dn = slot(y + 3, z + o), slot(y + 1, z + o)
            self.yc.append(
                [
                    rcopy(src, here, ys.at[i, 0], yr.at[i, 0], yp),
                    rcopy(src, here, ys.at[i, 1], yr.at[i, 1], ym),
                    rcopy(half(up, 0), half(up, 0), ys.at[i, 2], yr.at[i, 2], yp),
                    rcopy(half(dn, 1), half(dn, 1), ys.at[i, 3], yr.at[i, 3], ym),
                ]
            )
        self.cc = []
        for dy in range(4):
            row = []
            for i, o in enumerate(self.OFF):
                s = slot(y + self.OFF[dy], z + o)
                src = own if (i == 0 and dy == 0) else s
                row.append(rcopy(src, s, cs.at[dy, i], cr.at[dy, i], sib))
            self.cc.append(row)

    def start(self):
        self.zc[0].start()
        self.zc[1].start()
        self._fan(0)

    def _fan(self, i):
        self.yc[i][0].start()
        self.yc[i][1].start()
        self.cc[0][i].start()

    def z_near(self):
        self.zc[0].wait_recv()
        self.zc[2].start()
        self._fan(1)
        self.zc[1].wait_recv()
        self.zc[3].start()
        self._fan(2)

    def z_far(self):
        self.zc[2].wait_recv()
        self.zc[3].wait_recv()
        self._fan(3)

    def y_near(self, i):
        self.yc[i][0].wait_recv()
        self.yc[i][2].start()
        self.cc[1][i].start()
        self.yc[i][1].wait_recv()
        self.yc[i][3].start()
        self.cc[2][i].start()

    def y_far(self, i):
        self.yc[i][2].wait_recv()
        self.yc[i][3].wait_recv()
        self.cc[3][i].start()

    def wait_all(self):
        for row in self.cc:
            for d in row:
                d.wait_recv()

    def finish(self):
        for d in self.zc:
            d.wait_send()
        for row in self.yc + self.cc:
            for d in row:
                d.wait_send()


TOK_SEMS = [pltpu.SemaphoreType.DMA((4,))] * 2 + [pltpu.SemaphoreType.DMA((4, 4))] * 4


def norm_rows(src, dst, gain, bias, rows, step=32):
    @pl.loop(0, rows // step)
    def _(i):
        at = pl.ds(pl.multiple_of(i * step, step), step)
        v = src[at, :].astype(F32)
        mean = jnp.mean(v, axis=-1, keepdims=True)
        center = v - mean
        spread = jnp.mean(center * center, axis=-1, keepdims=True)
        dst[at, :] = (center * lax.rsqrt(spread + EPS) * gain[...] + bias[...]).astype(dst.dtype)


def k_qkv(tok, wl, wo, gain, bias, qb, toks, qkv, wo4, slots, wf, hb, lsem, xs, xr, ws, wr, *gs):
    x, y, z, c = position()
    t = lax.axis_index("tok")
    meet(x_peers() + [x_dev(x, 2)] + tok_peers())
    ring = RingGather(
        lambda i: tok.at[pl.ds(128 * i, 128)],
        lambda s, i: toks.at[s, pl.ds(128 * i, 128)],
        lambda k: xs.at[k],
        lambda k: xr.at[k],
    )
    wide = wl.shape[1] // 2
    gath = TokGather(wl, slots, lambda r, i: r.at[:, pl.ds(wide * i, wide)], *gs)
    gath.start()
    ring.start()
    wo_send = [rcopy(wo, wo4.at[x], ws.at[k], wr.at[k], x_dev(x, k + 1)) for k in range(3)]
    for d in wo_send:
        d.start()
    local = [
        pltpu.make_async_copy(tok, toks.at[x], lsem.at[0]),
        pltpu.make_async_copy(wl, slots.at[t], lsem.at[1]),
        pltpu.make_async_copy(wo, wo4.at[x], lsem.at[2]),
    ]
    for d in local:
        d.start()
    norm_rows(tok, hb.at[x], gain, bias, 256)
    gath.z_near()
    gath.z_far()
    gath.y_near(0)
    ring.relay()
    for i in range(1, 4):
        gath.y_near(i)
    ring.wait_near()
    for o in (1, 3):
        s = (x + o) % 4
        norm_rows(toks.at[s], hb.at[s], gain, bias, 256)
    for i in range(4):
        gath.y_far(i)
    for d in local:
        d.wait()
    gath.wait_all()

    @pl.loop(0, 8)
    def _(g):
        parts = [slots[4 * g + j] for j in range(4)]
        wf[pl.ds(pl.multiple_of(g * 208, 16), 208), :] = jnp.concatenate(parts, axis=0)

    def project(s):
        @pl.loop(0, wf.shape[1] // 256)
        def _(j):
            cols = pl.ds(pl.multiple_of(j * 256, 256), 256)
            v = jnp.dot(hb[s], wf[:, cols], preferred_element_type=F32) + qb[:, cols]
            v = v.astype(BF)
            rows = pl.ds(pl.multiple_of(s * 256, 256), 256)
            qkv[2 * j, rows, :] = v[:, :128]
            qkv[2 * j + 1, rows, :] = v[:, 128:]

    @pl.loop(0, 3)
    def _(i):
        project((x + i + i // 2) % 4)

    ring.wait_far()
    far = (x + 2) % 4
    norm_rows(toks.at[far], hb.at[far], gain, bias, 256)
    project(far)
    for d in wo_send:
        d.wait()
    ring.finish()
    gath.finish()


def k_att(qkv, segc, segr, wo4, att, wof, oh, slots, lsem, xs, xr, *gs):
    x, y, z, c = position()
    t = lax.axis_index("tok")
    meet(x_peers() + tok_peers())
    gath = TokGather(wo4, slots, lambda r, i: r.at[pl.ds(2 * i, 2)], *gs)
    gath.start()
    local = pltpu.make_async_copy(wo4, slots.at[t], lsem)
    local.start()
    scale = 1.0 / math.sqrt(HD)

    def attend(r):
        @pl.loop(0, 8)
        def _(i):
            h, sub = i // 2, i % 2
            rows = pl.ds(pl.multiple_of(r * 256 + sub * 128, 128), 128)
            s = lax.dot_general(
                qkv[h, rows, :], qkv[4 + h], (((1,), (1,)), ((), ())), preferred_element_type=F32
            )
            p = jnp.where(segc[rows, :] == segr[...], jnp.exp(s * scale), 0.0)
            total = jnp.sum(p, axis=-1, keepdims=True)
            o = jnp.dot(p.astype(BF), qkv[8 + h], preferred_element_type=F32) / total
            oh[h, pl.ds(pl.multiple_of(sub * 128, 128), 128), :] = o.astype(BF)

        att[x, pl.ds(r * 256, 256), :] = jnp.concatenate([oh[h][:, :HD] for h in range(4)], axis=1)

    rings = []
    for r in range(4):

        def part(s, i, r=r):
            return att.at[s, pl.ds(r * 256 + 128 * i, 128)]

        rings.append(
            RingGather(
                lambda i, part=part: part(x, i),
                part,
                lambda k, r=r: xs.at[r, k],
                lambda k, r=r: xr.at[r, k],
            )
        )
    attend(0)
    rings[0].start()
    gath.z_near()
    gath.z_far()
    attend(1)
    rings[1].start()
    rings[0].relay()
    gath.y_near(0)
    attend(2)
    rings[2].start()
    gath.y_near(1)
    attend(3)
    rings[3].start()
    rings[1].relay()
    gath.y_near(2)
    gath.y_near(3)
    rings[2].relay()
    for i in range(4):
        gath.y_far(i)
    rings[3].relay()
    local.wait()
    gath.wait_all()

    @pl.loop(0, 8)
    def _(g):
        for b in range(4):
            parts = [slots[4 * g + j, b] for j in range(4)]
            wof[b, pl.ds(pl.multiple_of(g * 208, 16), 208), :] = jnp.concatenate(parts, axis=0)

    for ring in rings:
        ring.wait_near()
        ring.wait_far()
        ring.finish()
    gath.finish()


class RingReduce:
    def __init__(self, sbuf, far_in, main_in, ss, rs, half):
        x = lax.axis_index("blk")
        self.hi, self.lo, self.far = (x + 1) % 4, (x + 3) % 4, (x + 2) % 4
        self.sbuf, self.far_in, self.main_in = sbuf, far_in, main_in
        right, left = x_dev(x, 1), x_dev(x, 3)
        self.a, self.b = pl.ds(0, half), pl.ds(half, half)
        a, b = self.a, self.b
        self.c = [
            rcopy(sbuf.at[self.far, a], far_in.at[0], ss(0), rs(0), right),
            rcopy(sbuf.at[self.far, b], far_in.at[1], ss(1), rs(1), left),
            rcopy(sbuf.at[self.hi, b], main_in.at[0, b], ss(2), rs(2), right),
            rcopy(sbuf.at[self.lo, a], main_in.at[1, a], ss(3), rs(3), left),
            rcopy(sbuf.at[self.hi, a], main_in.at[0, a], ss(4), rs(4), right),
            rcopy(sbuf.at[self.lo, b], main_in.at[1, b], ss(5), rs(5), left),
        ]

    def start(self):
        for k in range(4):
            self.c[k].start()

    def relay(self):
        self.c[0].wait_recv()
        s = self.sbuf[self.hi, self.a].astype(F32) + self.far_in[0].astype(F32)
        self.sbuf[self.hi, self.a] = s.astype(BF)
        self.c[1].wait_recv()
        s = self.sbuf[self.lo, self.b].astype(F32) + self.far_in[1].astype(F32)
        self.sbuf[self.lo, self.b] = s.astype(BF)
        self.c[4].start()
        self.c[5].start()

    def wait(self):
        for k in range(2, 6):
            self.c[k].wait_recv()

    def finish(self):
        for d in self.c:
            d.wait_send()


def gelu(v):
    return 0.5 * v * (1.0 + lax.erf(v * (1.0 / math.sqrt(2.0))))


def k_mlp(
    att, wof, toks, ob, gain, bias, fc1, b1, fc2, b2, wp, lo, wpg,
    w1, w2, after, h2, hid, part, own, sbuf, far_in, main_in, lsem, xs, xr, *gs
):
    x, y, z, c = position()
    t = lax.axis_index("tok")
    load = [
        pltpu.make_async_copy(fc1, w1, lsem.at[0]),
        pltpu.make_async_copy(fc2, w2, lsem.at[1]),
        pltpu.make_async_copy(wp, wpg.at[t], lsem.at[2]),
    ]
    for d in load:
        d.start()
    meet(x_peers() + tok_peers())
    gath = TokGather(wp, wpg, lambda r, i: r.at[pl.ds(96 * i, 96 + 16 * i)], *gs)
    gath.start()
    tiles = [(n, min(256, 1664 - n)) for n in range(0, 1664, 256)]

    def ring(r):
        return RingReduce(
            sbuf.at[r],
            far_in.at[r],
            main_in.at[r],
            lambda k: xs.at[r, k],
            lambda k: xr.at[r, k],
            128,
        )

    @pl.loop(0, 6)
    def _(r):
        @pl.when(r < 4)
        def _():
            rows = pl.ds(pl.multiple_of(r * 256, 256), 256)
            for n, w in tiles:
                acc = toks[r, :, n : n + w].astype(F32) + ob[:, n : n + w]
                for b in range(4):
                    acc += lax.dot_general(
                        att[b, rows, :],
                        wof[b, n : n + w, :],
                        (((1,), (1,)), ((), ())),
                        preferred_element_type=F32,
                    )
                after[:, n : n + w] = acc
            norm_rows(after, h2, gain, bias, 256)
            for j in range(4):

                @pl.when(x == j)
                def _():
                    own[r] = after[:, 416 * j : 416 * j + 416] + b2[...]

            @pl.when(r == 0)
            def _():
                load[0].wait()

            @pl.loop(0, 8)
            def _(j):
                cols = pl.ds(pl.multiple_of(j * 256, 256), 256)
                v = jnp.dot(h2[...], w1[:, cols], preferred_element_type=F32) + b1[:, cols]
                hid[:, cols] = gelu(v).astype(BF)

            @pl.when(r == 0)
            def _():
                load[1].wait()
                gath.z_near()
                gath.z_far()

            for n, w in tiles:
                part[:, n : n + w] = jnp.dot(hid[...], w2[:, n : n + w], preferred_element_type=F32)
            for j in range(4):
                piece = part[:, 416 * j : 416 * j + 416]
                sbuf[r, j] = piece.astype(BF)

                @pl.when(x == j)
                def _():
                    own[r] += piece

            @pl.when(r == 1)
            def _():
                gath.y_near(0)
                gath.y_near(1)

            @pl.when(r == 2)
            def _():
                gath.y_near(2)
                gath.y_near(3)

            ring(r).start()

        @pl.when((r > 0) & (r < 5))
        def _():
            ring(r - 1).relay()

        @pl.when(r > 1)
        def _():
            q = r - 2
            rg = ring(q)
            rg.wait()
            total = own[q] + main_in[q, 0].astype(F32) + main_in[q, 1].astype(F32)
            lo[pl.ds(pl.multiple_of(q * 256, 256), 256), :] = total.astype(BF)
            rg.finish()

        @pl.when(r == 3)
        def _():
            for i in range(4):
                gath.y_far(i)

    load[2].wait()
    gath.wait_all()
    gath.finish()


def k_proj(
    lo, gain, bias, mi, wpg, pb, out, fin, sbuf, own, far_in, main_in, st, ss, sr, xs, xr
):
    x, y, z, c = position()
    meet(x_peers() + [x_dev(x, 2)])
    n_loc = lo.shape[1]

    @pl.loop(0, 8)
    def _(i):
        rows = pl.ds(pl.multiple_of(i * 128, 128), 128)
        v = lo[rows, :].astype(F32)
        mean = jnp.mean(v, axis=-1, keepdims=True)
        d = v - mean
        m2 = jnp.sum(d * d, axis=-1, keepdims=True)
        lane = lax.broadcasted_iota(jnp.int32, (128, 128), 1)
        both = jnp.where(lane == 0, mean, jnp.where(lane == 1, m2, 0.0))
        st[x, :, rows] = both.T[:8]

    sends = [rcopy(st.at[x], st.at[x], ss.at[k], sr.at[k], x_dev(x, k + 1)) for k in range(3)]
    for d in sends:
        d.start()
    for d in sends:
        d.wait_recv()
    means = [st[s, 0:1, :] for s in range(4)]
    mean = 0.25 * (means[0] + means[1] + means[2] + means[3])
    m2 = st[0, 1:2, :] + st[1, 1:2, :] + st[2, 1:2, :] + st[3, 1:2, :]
    for s in range(4):
        d = means[s] - mean
        m2 = m2 + n_loc * (d * d)
    rstd = lax.rsqrt(m2 * (1.0 / (4 * n_loc)) + EPS)
    for i in range(8):
        sl = slice(128 * i, 128 * i + 128)
        row = lax.broadcasted_iota(jnp.int32, (128, 128), 0)
        cols = jnp.where(row == 0, mean[:, sl], jnp.where(row == 1, rstd[:, sl], 0.0)).T
        v = lo[sl, :].astype(F32)
        fin[sl, :] = ((v - cols[:, 0:1]) * cols[:, 1:2] * gain[...] + bias[...]).astype(BF)
    own[...] = jnp.zeros_like(own)

    @pl.loop(0, 4)
    def _(k):
        pick = (mi[k] == lax.broadcasted_iota(jnp.int32, (256, 1024), 1)).astype(BF)
        got = jnp.dot(pick, fin[...], preferred_element_type=F32).astype(BF)

        @pl.loop(0, 4)
        def _(j):
            own[j] += jnp.dot(got, wpg[k * 4 + j], preferred_element_type=F32)

    @pl.loop(0, 4)
    def _(j):
        sbuf[j] = own[j].astype(BF)

    rg = RingReduce(sbuf, far_in, main_in, lambda k: xs.at[k], lambda k: xr.at[k], 128)
    rg.start()
    rg.relay()
    rg.wait()
    total = own[x] + main_in[0].astype(F32) + main_in[1].astype(F32) + pb[...]
    out[...] = total.astype(BF)
    rg.finish()
    for d in sends:
        d.wait_send()


def kernel_call(body, name, cid, ins, outs, scratch, args):
    return pl.pallas_call(
        body,
        name=name,
        out_shape=outs,
        in_specs=ins,
        out_specs=[VM] * len(outs),
        scratch_shapes=scratch,
        compiler_params=pltpu.CompilerParams(
            collective_id=cid, has_side_effects=True, vmem_limit_bytes=VLIM
        ),
    )(*args)


def sds(shape, dtype):
    return jax.ShapeDtypeStruct(shape, dtype)


DMA = pltpu.SemaphoreType.DMA


def body(
    tokens,
    segment_ids,
    merge_index,
    segment_owner,
    ln1_gain,
    ln1_bias,
    w_qkv,
    qkv_bias,
    w_out,
    out_bias,
    ln2_gain,
    ln2_bias,
    w_fc1,
    fc1_bias,
    w_fc2,
    fc2_bias,
    ln3_gain,
    ln3_bias,
    w_proj,
    proj_bias,
):
    x = lax.axis_index("blk")
    tok = tokens[0]
    width = tok.shape[1]
    part_w = w_qkv.shape[2]
    depth = w_qkv.shape[1]
    heads = part_w // HD
    cols = 3 * heads * HPAD
    pad = ((0, 0), (0, 0), (0, 0), (0, HPAD - HD))
    wl = jnp.pad(w_qkv.transpose(1, 0, 2).reshape(depth, 3, heads, HD), pad).reshape(depth, cols)
    qb = jnp.pad(qkv_bias.reshape(1, 3, heads, HD), pad).reshape(1, cols)
    wo = w_out.T
    perm = []
    for bx in range(4):
        for t in range(32):
            ty, tz, tc = t // 8, (t // 2) % 4, t % 2
            perm.append((bx * 32 + t, tz * 32 + (ty * 4 + bx) * 2 + tc))
    wp = lax.ppermute(w_proj, ("blk", "tok"), perm)

    def row(v):
        return v.reshape(1, -1)

    toks, qkv, wo4 = kernel_call(
        k_qkv,
        "qkv",
        1,
        [VM] * 6,
        [sds((4, 256, width), BF), sds((3 * heads, 1024, HPAD), BF), sds((4, depth, part_w), BF)],
        [
            pltpu.VMEM((32, depth, cols), BF),
            pltpu.VMEM((width, cols), BF),
            pltpu.VMEM((4, 256, width), BF),
            DMA((3,)),
            DMA((6,)),
            DMA((6,)),
            DMA((3,)),
            DMA((3,)),
        ]
        + TOK_SEMS,
        (tok, wl, wo, row(ln1_gain), row(ln1_bias), qb),
    )
    seg = segment_ids[0]
    att, wof = kernel_call(
        k_att,
        "attention",
        2,
        [VM] * 4,
        [sds((4, 1024, part_w), BF), sds((4, width, part_w), BF)],
        [
            pltpu.VMEM((heads, 256, HPAD), BF),
            pltpu.VMEM((32, 4, depth, part_w), BF),
            DMA,
            DMA((4, 6)),
            DMA((4, 6)),
        ]
        + TOK_SEMS,
        (qkv, seg.reshape(-1, 1), seg.reshape(1, -1), wo4),
    )
    hidden = w_fc1.shape[1]

    def mine(v):
        return lax.dynamic_slice_in_dim(v, x * part_w, part_w, 0).reshape(1, -1)

    lo, wpg = kernel_call(
        k_mlp,
        "mlp",
        3,
        [VM, VM, VM, VM, VM, VM, ANY, VM, ANY, VM, VM],
        [sds((1024, part_w), BF), sds((32, 208, part_w), BF)],
        [
            pltpu.VMEM((width, hidden), BF),
            pltpu.VMEM((hidden, width), BF),
            pltpu.VMEM((256, width), F32),
            pltpu.VMEM((256, width), BF),
            pltpu.VMEM((256, hidden), BF),
            pltpu.VMEM((256, width), F32),
            pltpu.VMEM((4, 256, part_w), F32),
            pltpu.VMEM((4, 4, 256, part_w), BF),
            pltpu.VMEM((4, 2, 128, part_w), BF),
            pltpu.VMEM((4, 2, 256, part_w), BF),
            DMA((3,)),
            DMA((4, 6)),
            DMA((4, 6)),
        ]
        + TOK_SEMS,
        (
            att, wof, toks, row(out_bias), row(ln2_gain), row(ln2_bias),
            w_fc1, row(fc1_bias), w_fc2, mine(fc2_bias), wp,
        ),
    )
    merge_rows = merge_index[0]
    merged_count = merge_rows.shape[0]
    projected = kernel_call(
        k_proj,
        "merge",
        4,
        [VM] * 6,
        [sds((merged_count, part_w), BF)],
        [
            pltpu.VMEM((1024, part_w), BF),
            pltpu.VMEM((4, 256, part_w), BF),
            pltpu.VMEM((4, 256, part_w), F32),
            pltpu.VMEM((2, 128, part_w), BF),
            pltpu.VMEM((2, 256, part_w), BF),
            pltpu.VMEM((4, 8, 1024), F32),
            DMA((3,)),
            DMA((3,)),
            DMA((6,)),
            DMA((6,)),
        ],
        (
            lo,
            mine(ln3_gain),
            mine(ln3_bias),
            merge_rows.T.reshape(4, merged_count, 1),
            wpg.reshape(16, part_w, part_w),
            row(proj_bias),
        ),
    )[0]
    tok_count = lax.axis_size("tok")
    slot_cap = 2 * merged_count // tok_count
    owners_here = segment_owner[0]
    seg_rows = jnp.take(seg, merge_rows[:, 0])
    seg_match = (
        seg_rows[:, None] == jnp.arange(owners_here.shape[0], dtype=jnp.int32)[None, :]
    ).astype(jnp.int32)
    owner_rows = jnp.sum(seg_match * owners_here[None, :], axis=1)
    segment_matches = (
        owner_rows[:, None] == jnp.arange(tok_count, dtype=jnp.int32)[None, :]
    ).astype(jnp.int32)
    before = jnp.cumsum(segment_matches, axis=0) - segment_matches
    order_in = jnp.sum(before * segment_matches, axis=1)
    target = owner_rows * slot_cap + order_in
    placed = (jnp.arange(tok_count * slot_cap, dtype=jnp.int32)[:, None] == target[None, :]).astype(BF)
    outgoing = jnp.dot(placed, projected, preferred_element_type=F32).astype(BF)
    outgoing = outgoing.reshape(tok_count, slot_cap, projected.shape[1])
    arrived = lax.all_to_all(outgoing, "tok", split_axis=0, concat_axis=0, tiled=True)
    return arrived[None]


def solution(mesh):
    placed = (
        P("tok", "blk", None),
        P("tok", None),
        P("tok", None, None),
        P("tok", None),
        P(),
        P(),
        P(None, "tok", "blk"),
        P(None, "blk"),
        P("blk", "tok"),
        P(),
        P(),
        P(),
        P(None, "blk"),
        P("blk"),
        P("blk", None),
        P(),
        P(),
        P(),
        P("tok", "blk"),
        P("blk"),
    )
    return jax.shard_map(
        body, mesh=mesh, in_specs=placed, out_specs=P("tok", None, None, "blk"), check_vma=False
    )
```

```python
import math

import jax
import jax.numpy as jnp
from jax import lax
from jax.experimental import pallas as pl
from jax.experimental.pallas import tpu as pltpu
from jax.sharding import PartitionSpec as P

HD = 104
HPAD = 128
EPS = 1e-06
BF = jnp.bfloat16
F32 = jnp.float32
MESH_ID = pl.DeviceIdType.MESH
VLIM = 65000 * 1024
VM = pl.BlockSpec(memory_space=pltpu.VMEM)
ANY = pl.BlockSpec(memory_space=pl.ANY)


def position():
    x = lax.axis_index("blk")
    t = lax.axis_index("tok")
    return x, t // 8, (t // 2) % 4, t % 2


def tok_of(y, z, c):
    return ((y % 4) * 4 + z % 4) * 2 + c


def rcopy(src, dst, ssem, rsem, dev):
    return pltpu.make_async_remote_copy(
        src_ref=src, dst_ref=dst, send_sem=ssem, recv_sem=rsem, device_id=dev, device_id_type=MESH_ID
    )


def x_dev(x, off):
    return {"blk": (x + off) % 4}


def meet(peers):
    bar = pltpu.get_barrier_semaphore()
    for dev in peers:
        pl.semaphore_signal(bar, inc=1, device_id=dev, device_id_type=MESH_ID)
    pl.semaphore_wait(bar, len(peers))


def x_peers():
    x, y, z, c = position()
    return [x_dev(x, 1), x_dev(x, 3)]


def tok_peers():
    x, y, z, c = position()
    return [
        {"tok": tok_of(y, z + 1, c)},
        {"tok": tok_of(y, z + 3, c)},
        {"tok": tok_of(y + 1, z, c)},
        {"tok": tok_of(y + 3, z, c)},
        {"tok": tok_of(y, z, 1 - c)},
    ]


class RingGather:
    def __init__(self, own, half, ss, rs):
        x = lax.axis_index("blk")
        right, left = x_dev(x, 1), x_dev(x, 3)

        def send(view, src, i, k, dev):
            return rcopy(view, half(src, i), ss(k), rs(k), dev)

        me, lo, hi = x, (x + 3) % 4, (x + 1) % 4
        self.c = [
            send(own(0), me, 0, 0, right),
            send(own(1), me, 1, 1, right),
            send(own(1), me, 1, 2, left),
            send(own(0), me, 0, 3, left),
            send(half(lo, 0), lo, 0, 4, right),
            send(half(hi, 1), hi, 1, 5, left),
        ]

    def start(self):
        for k in (0, 2, 1, 3):
            self.c[k].start()

    def relay(self):
        self.c[0].wait_recv()
        self.c[4].start()
        self.c[2].wait_recv()
        self.c[5].start()

    def wait_near(self):
        self.c[1].wait_recv()
        self.c[3].wait_recv()

    def wait_far(self):
        self.c[4].wait_recv()
        self.c[5].wait_recv()

    def finish(self):
        for c in self.c:
            c.wait_send()


class TokGather:
    OFF = (0, 3, 1, 2)

    def __init__(self, own, slots, view, fs, fr, ss, sr, cs, cr):
        x, y, z, c = position()
        self.first, self.second, self.cross = [], [], []
        sib = {"tok": tok_of(y, z, 1 - c)}
        for h in range(2):

            def tok(d1, d2, h=h):
                return tok_of(y + d2, z + d1, c) if h == 0 else tok_of(y + d1, z + d2, c)

            def slot(d1, d2, tok=tok):
                return slots.at[tok(d1, d2)]

            def half(r, h=h):
                return view(r, h, None)

            def quarter(r, q, h=h):
                return view(r, h, q)

            me = slot(0, 0)
            p1, m1 = {"tok": tok(1, 0)}, {"tok": tok(3, 0)}
            p2, m2 = {"tok": tok(0, 1)}, {"tok": tok(0, 3)}
            self.first.append(
                [
                    rcopy(half(own), half(me), fs.at[h, 0], fr.at[h, 0], p1),
                    rcopy(half(own), half(me), fs.at[h, 1], fr.at[h, 1], m1),
                    rcopy(quarter(slot(3, 0), 0), quarter(slot(3, 0), 0), fs.at[h, 2], fr.at[h, 2], p1),
                    rcopy(quarter(slot(1, 0), 1), quarter(slot(1, 0), 1), fs.at[h, 3], fr.at[h, 3], m1),
                ]
            )
            second = []
            for i, o in enumerate(self.OFF):
                src = half(own) if i == 0 else half(slot(o, 0))
                here, up, dn = half(slot(o, 0)), slot(o, 3), slot(o, 1)
                second.append(
                    [
                        rcopy(src, here, ss.at[h, i, 0], sr.at[h, i, 0], p2),
                        rcopy(src, here, ss.at[h, i, 1], sr.at[h, i, 1], m2),
                        rcopy(quarter(up, 0), quarter(up, 0), ss.at[h, i, 2], sr.at[h, i, 2], p2),
                        rcopy(quarter(dn, 1), quarter(dn, 1), ss.at[h, i, 3], sr.at[h, i, 3], m2),
                    ]
                )
            self.second.append(second)
            cross = []
            for k in range(4):
                row = []
                for i, o in enumerate(self.OFF):
                    dst = half(slot(o, self.OFF[k]))
                    src = half(own) if (i == 0 and k == 0) else dst
                    row.append(rcopy(src, dst, cs.at[h, k, i], cr.at[h, k, i], sib))
                cross.append(row)
            self.cross.append(cross)

    def start(self):
        for h in range(2):
            self.first[h][0].start()
            self.first[h][1].start()
        for h in range(2):
            self._fan(h, 0)

    def _fan(self, h, i):
        self.second[h][i][0].start()
        self.second[h][i][1].start()
        self.cross[h][0][i].start()

    def first_near(self):
        for h in range(2):
            f = self.first[h]
            f[0].wait_recv()
            f[2].start()
            self._fan(h, 1)
            f[1].wait_recv()
            f[3].start()
            self._fan(h, 2)

    def first_far(self):
        for h in range(2):
            self.first[h][2].wait_recv()
            self.first[h][3].wait_recv()
            self._fan(h, 3)

    def second_near(self, i):
        for h in range(2):
            f = self.second[h][i]
            f[0].wait_recv()
            f[2].start()
            self.cross[h][1][i].start()
            f[1].wait_recv()
            f[3].start()
            self.cross[h][2][i].start()

    def second_far(self, i):
        for h in range(2):
            f = self.second[h][i]
            f[2].wait_recv()
            f[3].wait_recv()
            self.cross[h][3][i].start()

    def _all(self):
        for h in range(2):
            for row in self.cross[h]:
                yield from row

    def wait_all(self):
        for d in self._all():
            d.wait_recv()

    def finish(self):
        for h in range(2):
            for d in self.first[h]:
                d.wait_send()
            for row in self.second[h]:
                for d in row:
                    d.wait_send()
        for d in self._all():
            d.wait_send()


TOK_SEMS = [pltpu.SemaphoreType.DMA((2, 4))] * 2 + [pltpu.SemaphoreType.DMA((2, 4, 4))] * 4


def norm_rows(src, dst, gain, bias, rows, step=32):
    @pl.loop(0, rows // step)
    def _(i):
        at = pl.ds(pl.multiple_of(i * step, step), step)
        v = src[at, :].astype(F32)
        mean = jnp.mean(v, axis=-1, keepdims=True)
        center = v - mean
        spread = jnp.mean(center * center, axis=-1, keepdims=True)
        dst[at, :] = (center * lax.rsqrt(spread + EPS) * gain[...] + bias[...]).astype(dst.dtype)


def view_cols(r, h, q):
    return r.at[:, pl.ds(768 * h, 768)] if q is None else r.at[:, pl.ds(768 * h + 384 * q, 384)]


def view_lead(r, h, q):
    return r.at[pl.ds(2 * h, 2)] if q is None else r.at[pl.ds(2 * h + q, 1)]


def view_rows(r, h, q):
    start, size = ((0, 112), (112, 96))[h]
    if q is None:
        return r.at[pl.ds(start, size)]
    first = (64, 48)[h]
    return r.at[pl.ds(start, first)] if q == 0 else r.at[pl.ds(start + first, size - first)]


def k_qkv(
    tok, wq, wout, gain, bias, qbias, toks_o, qkv_o, wof_o,
    wl, qb, wo4, toks, qkv, slots, wslots, wf, wof, hb, lsem, osem, xs, xr, ws, wr, *gs
):
    x, y, z, c = position()
    t = lax.axis_index("tok")
    depth = wq.shape[1]
    heads = wq.shape[2] // HD
    meet(x_peers() + [x_dev(x, 2)] + tok_peers())
    ring = RingGather(
        lambda i: tok.at[pl.ds(128 * i, 128)],
        lambda s, i: toks.at[s, pl.ds(128 * i, 128)],
        lambda k: xs.at[k],
        lambda k: xr.at[k],
    )
    ring.start()
    zero = jnp.zeros((depth, HPAD - HD), BF)
    for k in range(3):
        for h in range(heads):
            at = (k * heads + h) * HPAD
            wl[:, at : at + HPAD] = jnp.concatenate([wq[k, :, h * HD : h * HD + HD], zero], axis=1)
            qb[:, at : at + HPAD] = jnp.concatenate(
                [qbias[k : k + 1, h * HD : h * HD + HD], jnp.zeros((1, HPAD - HD), F32)], axis=1
            )
    wo4[x] = wout[...].T
    gq = TokGather(wl, slots, view_cols, *gs[:6])
    go = TokGather(wo4, wslots, view_lead, *gs[6:])
    gq.start()
    wo_send = [rcopy(wo4.at[x], wo4.at[x], ws.at[k], wr.at[k], x_dev(x, k + 1)) for k in range(3)]
    for d in wo_send:
        d.start()
    local = [
        pltpu.make_async_copy(tok, toks.at[x], lsem.at[0]),
        pltpu.make_async_copy(wl, slots.at[t], lsem.at[1]),
    ]
    for d in local:
        d.start()
    norm_rows(tok, hb.at[x], gain, bias, 256)
    gq.first_near()
    for d in wo_send:
        d.wait_recv()
    go.start()
    local.append(pltpu.make_async_copy(wo4, wslots.at[t], lsem.at[2]))
    local[2].start()
    gq.first_far()
    gq.second_near(0)
    ring.relay()
    for i in range(1, 4):
        gq.second_near(i)
    go.first_near()
    go.first_far()
    ring.wait_near()
    local[0].wait()
    outs = []

    def put(src, dst):
        outs.append(pltpu.make_async_copy(src, dst, osem.at[len(outs)]))
        outs[-1].start()

    for o in (0, 1, 3):
        s = (x + o) % 4
        put(toks.at[s], toks_o.at[s])
        if o:
            norm_rows(toks.at[s], hb.at[s], gain, bias, 256)
    for i in range(4):
        gq.second_far(i)
    for i in range(4):
        go.second_near(i)
    local[1].wait()
    gq.wait_all()

    @pl.loop(0, 8)
    def _(g):
        parts = [slots[4 * g + j] for j in range(4)]
        wf[pl.ds(pl.multiple_of(g * 208, 16), 208), :] = jnp.concatenate(parts, axis=0)

    def project(s):
        @pl.loop(0, wf.shape[1] // 256)
        def _(j):
            cols = pl.ds(pl.multiple_of(j * 256, 256), 256)
            v = jnp.dot(hb[s], wf[:, cols], preferred_element_type=F32) + qb[:, cols]
            v = v.astype(BF)
            rows = pl.ds(pl.multiple_of(s * 256, 256), 256)
            qkv[2 * j, rows, :] = v[:, :128]
            qkv[2 * j + 1, rows, :] = v[:, 128:]

    @pl.loop(0, 3)
    def _(i):
        project((x + i + i // 2) % 4)

    for i in range(4):
        go.second_far(i)
    local[2].wait()
    go.wait_all()

    @pl.loop(0, 8)
    def _(g):
        for b in range(4):
            parts = [wslots[4 * g + j, b] for j in range(4)]
            wof[b, pl.ds(pl.multiple_of(g * 208, 16), 208), :] = jnp.concatenate(parts, axis=0)

    put(wof, wof_o)
    ring.wait_far()
    far = (x + 2) % 4
    put(toks.at[far], toks_o.at[far])
    norm_rows(toks.at[far], hb.at[far], gain, bias, 256)
    project(far)
    put(qkv, qkv_o)
    for d in wo_send:
        d.wait_send()
    ring.finish()
    gq.finish()
    go.finish()
    for d in outs:
        d.wait()


class RingReduce:
    def __init__(self, sbuf, far_in, main_in, ss, rs, half):
        x = lax.axis_index("blk")
        self.hi, self.lo, self.far = (x + 1) % 4, (x + 3) % 4, (x + 2) % 4
        self.sbuf, self.far_in, self.main_in = sbuf, far_in, main_in
        right, left = x_dev(x, 1), x_dev(x, 3)
        self.a, self.b = pl.ds(0, half), pl.ds(half, half)
        a, b = self.a, self.b
        self.c = [
            rcopy(sbuf.at[self.far, a], far_in.at[0], ss(0), rs(0), right),
            rcopy(sbuf.at[self.far, b], far_in.at[1], ss(1), rs(1), left),
            rcopy(sbuf.at[self.hi, b], main_in.at[0, b], ss(2), rs(2), right),
            rcopy(sbuf.at[self.lo, a], main_in.at[1, a], ss(3), rs(3), left),
            rcopy(sbuf.at[self.hi, a], main_in.at[0, a], ss(4), rs(4), right),
            rcopy(sbuf.at[self.lo, b], main_in.at[1, b], ss(5), rs(5), left),
        ]

    def start(self):
        for k in range(4):
            self.c[k].start()

    def relay(self):
        self.c[0].wait_recv()
        s = self.sbuf[self.hi, self.a].astype(F32) + self.far_in[0].astype(F32)
        self.sbuf[self.hi, self.a] = s.astype(BF)
        self.c[1].wait_recv()
        s = self.sbuf[self.lo, self.b].astype(F32) + self.far_in[1].astype(F32)
        self.sbuf[self.lo, self.b] = s.astype(BF)
        self.c[4].start()
        self.c[5].start()

    def wait(self):
        for k in range(2, 6):
            self.c[k].wait_recv()

    def finish(self):
        for d in self.c:
            d.wait_send()


def gelu(v):
    return 0.5 * v * (1.0 + lax.erf(v * (1.0 / math.sqrt(2.0))))


def k_layer(
    qkv, seg, toks_h, wof_h, ob, gain, bias, fc1, b1, fc2, b2, wp, lo, wpg,
    toks, wof, w1, w2, att, oh, segc, after, h2, hid, own, sbuf, far_in, main_in,
    lsem, as_, ar, xs, xr, *gs
):
    x, y, z, c = position()
    t = lax.axis_index("tok")
    load = [
        pltpu.make_async_copy(wof_h, wof, lsem.at[0]),
        pltpu.make_async_copy(toks_h, toks, lsem.at[1]),
        pltpu.make_async_copy(fc1, w1, lsem.at[2]),
        pltpu.make_async_copy(fc2, w2, lsem.at[3]),
        pltpu.make_async_copy(wp, wpg.at[t], lsem.at[4]),
    ]
    for d in load:
        d.start()
    segr = seg[...].astype(F32)
    segc[...] = jnp.broadcast_to(segr, (128, segr.shape[1])).T
    meet(x_peers() + tok_peers())
    gath = TokGather(wp, wpg, view_rows, *gs)
    gath.start()
    scale = 1.0 / math.sqrt(HD)
    heads = qkv.shape[0] // 3

    def attend(r):
        @pl.loop(0, 2)
        def _(sub):
            rows = pl.ds(pl.multiple_of(r * 256 + sub * 128, 128), 128)
            same = segc[rows, 0:1] == segr
            for h in range(heads):
                s = lax.dot_general(
                    qkv[h, rows, :], qkv[heads + h], (((1,), (1,)), ((), ())), preferred_element_type=F32
                )
                p = jnp.where(same, jnp.exp(s * scale), 0.0)
                total = jnp.sum(p, axis=-1, keepdims=True)
                o = jnp.dot(p.astype(BF), qkv[2 * heads + h], preferred_element_type=F32) / total
                oh[h, pl.ds(pl.multiple_of(sub * 128, 128), 128), :] = o.astype(BF)

        att[x, pl.ds(r * 256, 256), :] = jnp.concatenate([oh[h][:, :HD] for h in range(heads)], axis=1)

    def gather_ring(r):
        def part(s, i):
            return att.at[s, pl.ds(pl.multiple_of(r * 256 + 128 * i, 128), 128)]

        return RingGather(lambda i: part(x, i), part, lambda k: as_.at[r, k], lambda k: ar.at[r, k])

    def reduce_ring(r):
        return RingReduce(
            sbuf.at[r],
            far_in.at[r],
            main_in.at[r],
            lambda k: xs.at[r, k],
            lambda k: xr.at[r, k],
            128,
        )

    attend(0)
    gather_ring(0).start()
    gath.first_near()
    gath.first_far()
    attend(1)
    gather_ring(1).start()
    gather_ring(0).relay()
    attend(2)
    gather_ring(2).start()
    for i in range(4):
        gath.second_near(i)
    gather_ring(1).relay()
    attend(3)
    gather_ring(3).start()
    gather_ring(2).relay()
    for i in range(4):
        gath.second_far(i)
    tiles = [(n, min(256, 1664 - n)) for n in range(0, 1664, 256)]
    for d in load[:2]:
        d.wait()

    @pl.loop(0, 6)
    def _(r):
        @pl.when(r < 4)
        def _():
            rg = gather_ring(r)
            rg.wait_near()
            rg.wait_far()
            rows = pl.ds(pl.multiple_of(r * 256, 256), 256)
            for n, w in tiles:
                acc = toks[r, :, n : n + w].astype(F32) + ob[n : n + w]
                for b in range(4):
                    acc += lax.dot_general(
                        att[b, rows, :],
                        wof[b, n : n + w, :],
                        (((1,), (1,)), ((), ())),
                        preferred_element_type=F32,
                    )
                after[:, n : n + w] = acc

            @pl.when(r == 0)
            def _():
                gather_ring(3).relay()
                load[2].wait()

            @pl.when(r > 0)
            def _():
                reduce_ring(r - 1).relay()

            norm_rows(after, h2, gain, bias, 256)
            for j in range(4):

                @pl.when(x == j)
                def _():
                    own[r] = after[:, 416 * j : 416 * j + 416] + b2[416 * j : 416 * j + 416]

            for j in range(8):
                cols = slice(256 * j, 256 * j + 256)
                v = jnp.dot(h2[...], w1[:, cols], preferred_element_type=F32) + b1[cols]
                hid[:, cols] = gelu(v).astype(BF)

            @pl.when(r == 0)
            def _():
                load[3].wait()

            for n, w in tiles:
                after[:, n : n + w] = jnp.dot(hid[...], w2[:, n : n + w], preferred_element_type=F32)
            for j in range(4):
                piece = after[:, 416 * j : 416 * j + 416]
                sbuf[r, j] = piece.astype(BF)

                @pl.when(x == j)
                def _():
                    own[r] += piece

            reduce_ring(r).start()

        @pl.when(r == 4)
        def _():
            reduce_ring(3).relay()

        @pl.when(r > 1)
        def _():
            q = r - 2
            rg = reduce_ring(q)
            rg.wait()
            total = own[q] + main_in[q, 0].astype(F32) + main_in[q, 1].astype(F32)
            lo[pl.ds(pl.multiple_of(q * 256, 256), 256), :] = total.astype(BF)
            rg.finish()
            gather_ring(q).finish()

    load[4].wait()
    gath.wait_all()
    gath.finish()


def column(rows):
    n, m = rows.shape
    return jnp.concatenate([rows, jnp.zeros((128 - n, m), F32)], axis=0).T


def k_merge(
    lo, gain3, bias3, mi, seg, owners, wpg_h, pb, out,
    wpg, fin, gb, sbuf, own, far_in, main_in, st, placed, obuf, lsem, ss, sr, xs, xr, ts, tr
):
    x, y, z, c = position()
    t = lax.axis_index("tok")
    n_tok = out.shape[0]
    slot = out.shape[1]
    merged = mi.shape[1]
    n_loc = lo.shape[1]
    load = pltpu.make_async_copy(wpg_h, wpg, lsem.at[0])
    load.start()
    bar = pltpu.get_barrier_semaphore()

    @pl.loop(1, n_tok)
    def _(i):
        pl.semaphore_signal(bar, inc=1, device_id={"tok": (t + i) % n_tok}, device_id_type=MESH_ID)

    @pl.loop(1, 4)
    def _(i):
        pl.semaphore_signal(bar, inc=1, device_id=x_dev(x, i), device_id_type=MESH_ID)

    @pl.loop(0, 8)
    def _(i):
        rows = pl.ds(pl.multiple_of(i * 128, 128), 128)
        v = lo[rows, :].astype(F32)
        mean = jnp.mean(v, axis=-1, keepdims=True)
        d = v - mean
        m2 = jnp.sum(d * d, axis=-1, keepdims=True)
        lane = lax.broadcasted_iota(jnp.int32, (128, 128), 1)
        both = jnp.where(lane == 0, mean, jnp.where(lane == 1, m2, 0.0))
        st[x, :, rows] = both.T[:8]

    pl.semaphore_wait(bar, n_tok + 2)
    sends = [rcopy(st.at[x], st.at[x], ss.at[k], sr.at[k], x_dev(x, k + 1)) for k in range(3)]
    for d in sends:
        d.start()
    for j in range(4):

        @pl.when(x == j)
        def _():
            gb[0:1, :] = gain3[n_loc * j : n_loc * j + n_loc].reshape(1, n_loc)
            gb[1:2, :] = bias3[n_loc * j : n_loc * j + n_loc].reshape(1, n_loc)

    idx = column(mi[...].astype(F32))
    toks = lax.broadcasted_iota(jnp.int32, (merged, 1024), 1).astype(F32)
    seg_of = jnp.sum(jnp.where(idx[:, 0:1] == toks, seg[...].astype(F32), 0.0), axis=1, keepdims=True)
    names = lax.broadcasted_iota(jnp.int32, (merged, n_tok), 1).astype(F32)
    owner = jnp.sum(jnp.where(seg_of == names, owners[...].astype(F32), 0.0), axis=1, keepdims=True)
    mine = (owner == names).astype(F32)
    below = lax.broadcasted_iota(jnp.int32, (merged, merged), 1) < lax.broadcasted_iota(
        jnp.int32, (merged, merged), 0
    )
    before = jnp.dot(
        jnp.where(below, 1.0, 0.0).astype(BF), mine.astype(BF), preferred_element_type=F32
    )
    rank = jnp.sum(before * mine, axis=1, keepdims=True)
    target = jnp.broadcast_to(owner * slot + rank, (merged, 128)).T[0:1]
    spots = lax.broadcasted_iota(jnp.int32, (n_tok * slot, merged), 0).astype(F32)
    placed[...] = jnp.where(spots == target, 1.0, 0.0).astype(BF)
    for d in sends:
        d.wait_recv()
    means = [st[s, 0:1, :] for s in range(4)]
    mean = 0.25 * (means[0] + means[1] + means[2] + means[3])
    m2 = st[0, 1:2, :] + st[1, 1:2, :] + st[2, 1:2, :] + st[3, 1:2, :]
    for s in range(4):
        d = means[s] - mean
        m2 = m2 + n_loc * (d * d)
    rstd = lax.rsqrt(m2 * (1.0 / (4 * n_loc)) + EPS)
    for i in range(8):
        sl = slice(128 * i, 128 * i + 128)
        row = lax.broadcasted_iota(jnp.int32, (128, 128), 0)
        cols = jnp.where(row == 0, mean[:, sl], jnp.where(row == 1, rstd[:, sl], 0.0)).T
        v = lo[sl, :].astype(F32)
        fin[sl, :] = ((v - cols[:, 0:1]) * cols[:, 1:2] * gb[0:1, :] + gb[1:2, :]).astype(BF)
    load.wait()
    got = []
    for k in range(4):
        pick = jnp.where(idx[:, k : k + 1] == toks, 1.0, 0.0).astype(BF)
        got.append(jnp.dot(pick, fin[...], preferred_element_type=F32).astype(BF))
    for j in range(4):
        acc = jnp.dot(got[0], wpg[j], preferred_element_type=F32)
        for k in range(1, 4):
            acc += jnp.dot(got[k], wpg[k * 4 + j], preferred_element_type=F32)
        own[j] = acc
        sbuf[j] = acc.astype(BF)
    rg = RingReduce(sbuf, far_in, main_in, lambda k: xs.at[k], lambda k: xr.at[k], 128)
    rg.start()
    rg.relay()
    rg.wait()
    total = own[x] + main_in[0].astype(F32) + main_in[1].astype(F32) + pb[...]
    going = jnp.dot(placed[...], total.astype(BF), preferred_element_type=F32).astype(BF)
    obuf[...] = going.reshape(n_tok, slot, n_loc)

    def slot_copy(i):
        to = (t + i) % n_tok
        return rcopy(obuf.at[to], out.at[t], ts.at[i], tr.at[i], {"tok": to})

    @pl.loop(1, n_tok)
    def _(i):
        slot_copy(i).start()

    keep = pltpu.make_async_copy(obuf.at[t], out.at[t], lsem.at[1])
    keep.start()
    rg.finish()
    for d in sends:
        d.wait_send()
    keep.wait()

    @pl.loop(1, n_tok)
    def _(i):
        slot_copy(i).wait()


def kernel_call(body, name, cid, ins, outs, out_specs, scratch, args):
    return pl.pallas_call(
        body,
        name=name,
        out_shape=outs,
        in_specs=ins,
        out_specs=out_specs,
        scratch_shapes=scratch,
        compiler_params=pltpu.CompilerParams(
            collective_id=cid, has_side_effects=True, vmem_limit_bytes=VLIM
        ),
    )(*args)


def sds(shape, dtype):
    return jax.ShapeDtypeStruct(shape, dtype)


DMA = pltpu.SemaphoreType.DMA


def body(
    tokens,
    segment_ids,
    merge_index,
    segment_owner,
    ln1_gain,
    ln1_bias,
    w_qkv,
    qkv_bias,
    w_out,
    out_bias,
    ln2_gain,
    ln2_bias,
    w_fc1,
    fc1_bias,
    w_fc2,
    fc2_bias,
    ln3_gain,
    ln3_bias,
    w_proj,
    proj_bias,
):
    tok = tokens[0]
    width = tok.shape[1]
    part_w = w_qkv.shape[2]
    depth = w_qkv.shape[1]
    heads = part_w // HD
    cols = 3 * heads * HPAD
    hidden = w_fc1.shape[1]
    perm = []
    for bx in range(4):
        for t in range(32):
            ty, tz, tc = t // 8, (t // 2) % 4, t % 2
            perm.append((bx * 32 + t, tz * 32 + (ty * 4 + bx) * 2 + tc))
    wp = lax.ppermute(w_proj, ("blk", "tok"), perm)
    toks, qkv, wof = kernel_call(
        k_qkv,
        "qkv",
        1,
        [VM] * 6,
        [sds((4, 256, width), BF), sds((3 * heads, 1024, HPAD), BF), sds((4, width, part_w), BF)],
        [ANY] * 3,
        [
            pltpu.VMEM((depth, cols), BF),
            pltpu.VMEM((1, cols), F32),
            pltpu.VMEM((4, depth, part_w), BF),
            pltpu.VMEM((4, 256, width), BF),
            pltpu.VMEM((3 * heads, 1024, HPAD), BF),
            pltpu.VMEM((32, depth, cols), BF),
            pltpu.VMEM((32, 4, depth, part_w), BF),
            pltpu.VMEM((width, cols), BF),
            pltpu.VMEM((4, width, part_w), BF),
            pltpu.VMEM((4, 256, width), BF),
            DMA((3,)),
            DMA((6,)),
            DMA((6,)),
            DMA((6,)),
            DMA((3,)),
            DMA((3,)),
        ]
        + TOK_SEMS * 2,
        (tok, w_qkv, w_out, ln1_gain, ln1_bias, qkv_bias),
    )
    lo, wpg = kernel_call(
        k_layer,
        "layer",
        2,
        [VM, VM, ANY, ANY, VM, VM, VM, ANY, VM, ANY, VM, VM],
        [sds((1024, part_w), BF), sds((32, 208, part_w), BF)],
        [VM, ANY],
        [
            pltpu.VMEM((4, 256, width), BF),
            pltpu.VMEM((4, width, part_w), BF),
            pltpu.VMEM((width, hidden), BF),
            pltpu.VMEM((hidden, width), BF),
            pltpu.VMEM((4, 1024, part_w), BF),
            pltpu.VMEM((heads, 256, HPAD), BF),
            pltpu.VMEM((1024, 128), F32),
            pltpu.VMEM((256, width), F32),
            pltpu.VMEM((256, width), BF),
            pltpu.VMEM((256, hidden), BF),
            pltpu.VMEM((4, 256, part_w), F32),
            pltpu.VMEM((4, 4, 256, part_w), BF),
            pltpu.VMEM((4, 2, 128, part_w), BF),
            pltpu.VMEM((4, 2, 256, part_w), BF),
            DMA((5,)),
            DMA((4, 6)),
            DMA((4, 6)),
            DMA((4, 6)),
            DMA((4, 6)),
        ]
        + TOK_SEMS,
        (
            qkv, segment_ids, toks, wof, out_bias, ln2_gain, ln2_bias,
            w_fc1, fc1_bias, w_fc2, fc2_bias, wp,
        ),
    )
    merged_count = merge_index.shape[1]
    n_tok = lax.axis_size("tok")
    slot = 2 * merged_count // n_tok
    arrived = kernel_call(
        k_merge,
        "merge",
        3,
        [VM] * 6 + [ANY, VM],
        [sds((n_tok, slot, part_w), BF)],
        [VM],
        [
            pltpu.VMEM((16, part_w, part_w), BF),
            pltpu.VMEM((1024, part_w), BF),
            pltpu.VMEM((2, part_w), F32),
            pltpu.VMEM((4, 256, part_w), BF),
            pltpu.VMEM((4, 256, part_w), F32),
            pltpu.VMEM((2, 128, part_w), BF),
            pltpu.VMEM((2, 256, part_w), BF),
            pltpu.VMEM((4, 8, 1024), F32),
            pltpu.VMEM((n_tok * slot, merged_count), BF),
            pltpu.VMEM((n_tok, slot, part_w), BF),
            DMA((2,)),
            DMA((3,)),
            DMA((3,)),
            DMA((6,)),
            DMA((6,)),
            DMA((n_tok,)),
            DMA((n_tok,)),
        ],
        (
            lo,
            ln3_gain,
            ln3_bias,
            merge_index[0].T,
            segment_ids,
            segment_owner,
            wpg.reshape(16, part_w, part_w),
            proj_bias,
        ),
    )[0]
    return arrived[None]


def solution(mesh):
    placed = (
        P("tok", "blk", None),
        P("tok", None),
        P("tok", None, None),
        P("tok", None),
        P(),
        P(),
        P(None, "tok", "blk"),
        P(None, "blk"),
        P("blk", "tok"),
        P(),
        P(),
        P(),
        P(None, "blk"),
        P("blk"),
        P("blk", None),
        P(),
        P(),
        P(),
        P("tok", "blk"),
        P("blk"),
    )
    return jax.shard_map(
        body, mesh=mesh, in_specs=placed, out_specs=P("tok", None, None, "blk"), check_vma=False
    )
```

```python
import math

import jax
import jax.numpy as jnp
from jax import lax
from jax.experimental import pallas as pl
from jax.experimental.pallas import tpu as pltpu
from jax.sharding import PartitionSpec as P

HD = 104
HPAD = 128
EPS = 1e-06
BF = jnp.bfloat16
F32 = jnp.float32
MESH_ID = pl.DeviceIdType.MESH
VLIM = 65000 * 1024
VM = pl.BlockSpec(memory_space=pltpu.VMEM)
ANY = pl.BlockSpec(memory_space=pl.ANY)


def position():
    x = lax.axis_index("blk")
    t = lax.axis_index("tok")
    return x, t // 8, (t // 2) % 4, t % 2


def tok_of(y, z, c):
    return ((y % 4) * 4 + z % 4) * 2 + c


def rcopy(src, dst, ssem, rsem, dev):
    return pltpu.make_async_remote_copy(
        src_ref=src, dst_ref=dst, send_sem=ssem, recv_sem=rsem, device_id=dev, device_id_type=MESH_ID
    )


def x_dev(x, off):
    return {"blk": (x + off) % 4}


def meet(peers):
    bar = pltpu.get_barrier_semaphore()
    for dev in peers:
        pl.semaphore_signal(bar, inc=1, device_id=dev, device_id_type=MESH_ID)
    pl.semaphore_wait(bar, len(peers))


def x_peers():
    x, y, z, c = position()
    return [x_dev(x, 1), x_dev(x, 3)]


def tok_peers():
    x, y, z, c = position()
    return [
        {"tok": tok_of(y, z + 1, c)},
        {"tok": tok_of(y, z + 3, c)},
        {"tok": tok_of(y + 1, z, c)},
        {"tok": tok_of(y + 3, z, c)},
        {"tok": tok_of(y, z, 1 - c)},
    ]


class RingGather:
    def __init__(self, own, half, ss, rs):
        x = lax.axis_index("blk")
        right, left = x_dev(x, 1), x_dev(x, 3)

        def send(view, src, i, k, dev):
            return rcopy(view, half(src, i), ss(k), rs(k), dev)

        me, lo, hi = x, (x + 3) % 4, (x + 1) % 4
        self.c = [
            send(own(0), me, 0, 0, right),
            send(own(1), me, 1, 1, right),
            send(own(1), me, 1, 2, left),
            send(own(0), me, 0, 3, left),
            send(half(lo, 0), lo, 0, 4, right),
            send(half(hi, 1), hi, 1, 5, left),
        ]

    def start(self):
        for k in (0, 2, 1, 3):
            self.c[k].start()

    def relay(self):
        self.c[0].wait_recv()
        self.c[4].start()
        self.c[2].wait_recv()
        self.c[5].start()

    def wait_near(self):
        self.c[1].wait_recv()
        self.c[3].wait_recv()

    def wait_far(self):
        self.c[4].wait_recv()
        self.c[5].wait_recv()

    def finish(self):
        for c in self.c:
            c.wait_send()


class TokGather:
    OFF = (0, 3, 1, 2)

    def __init__(self, own, slots, view, fs, fr, ss, sr, cs, cr):
        x, y, z, c = position()
        self.first, self.second, self.cross = [], [], []
        sib = {"tok": tok_of(y, z, 1 - c)}
        for h in range(2):

            def tok(d1, d2, h=h):
                return tok_of(y + d2, z + d1, c) if h == 0 else tok_of(y + d1, z + d2, c)

            def slot(d1, d2, tok=tok):
                return slots.at[tok(d1, d2)]

            def half(r, h=h):
                return view(r, h, None)

            def quarter(r, q, h=h):
                return view(r, h, q)

            me = slot(0, 0)
            p1, m1 = {"tok": tok(1, 0)}, {"tok": tok(3, 0)}
            p2, m2 = {"tok": tok(0, 1)}, {"tok": tok(0, 3)}
            self.first.append(
                [
                    rcopy(half(own), half(me), fs.at[h, 0], fr.at[h, 0], p1),
                    rcopy(half(own), half(me), fs.at[h, 1], fr.at[h, 1], m1),
                    rcopy(quarter(slot(3, 0), 0), quarter(slot(3, 0), 0), fs.at[h, 2], fr.at[h, 2], p1),
                    rcopy(quarter(slot(1, 0), 1), quarter(slot(1, 0), 1), fs.at[h, 3], fr.at[h, 3], m1),
                ]
            )
            second = []
            for i, o in enumerate(self.OFF):
                src = half(own) if i == 0 else half(slot(o, 0))
                here, up, dn = half(slot(o, 0)), slot(o, 3), slot(o, 1)
                second.append(
                    [
                        rcopy(src, here, ss.at[h, i, 0], sr.at[h, i, 0], p2),
                        rcopy(src, here, ss.at[h, i, 1], sr.at[h, i, 1], m2),
                        rcopy(quarter(up, 0), quarter(up, 0), ss.at[h, i, 2], sr.at[h, i, 2], p2),
                        rcopy(quarter(dn, 1), quarter(dn, 1), ss.at[h, i, 3], sr.at[h, i, 3], m2),
                    ]
                )
            self.second.append(second)
            cross = []
            for k in range(4):
                row = []
                for i, o in enumerate(self.OFF):
                    dst = half(slot(o, self.OFF[k]))
                    src = half(own) if (i == 0 and k == 0) else dst
                    row.append(rcopy(src, dst, cs.at[h, k, i], cr.at[h, k, i], sib))
                cross.append(row)
            self.cross.append(cross)

    def start(self):
        for h in range(2):
            self.first[h][0].start()
            self.first[h][1].start()
        for h in range(2):
            self._fan(h, 0)

    def _fan(self, h, i):
        self.second[h][i][0].start()
        self.second[h][i][1].start()
        self.cross[h][0][i].start()

    def first_near(self, h):
        f = self.first[h]
        f[0].wait_recv()
        f[2].start()
        self._fan(h, 1)
        f[1].wait_recv()
        f[3].start()
        self._fan(h, 2)

    def first_far(self, h):
        self.first[h][2].wait_recv()
        self.first[h][3].wait_recv()
        self._fan(h, 3)

    def second_near(self, h, i):
        f = self.second[h][i]
        f[0].wait_recv()
        f[2].start()
        self.cross[h][1][i].start()
        f[1].wait_recv()
        f[3].start()
        self.cross[h][2][i].start()

    def second_far(self, h, i):
        f = self.second[h][i]
        f[2].wait_recv()
        f[3].wait_recv()
        self.cross[h][3][i].start()

    def wait_cross(self, h, k):
        for d in self.cross[h][k]:
            d.wait_recv()

    def _all(self):
        for h in range(2):
            for row in self.cross[h]:
                yield from row

    def finish(self):
        for h in range(2):
            for d in self.first[h]:
                d.wait_send()
            for row in self.second[h]:
                for d in row:
                    d.wait_send()
        for d in self._all():
            d.wait_send()


TOK_SEMS = [pltpu.SemaphoreType.DMA((2, 4))] * 2 + [pltpu.SemaphoreType.DMA((2, 4, 4))] * 4


def norm_rows(src, dst, gain, bias, rows, step=32):
    @pl.loop(0, rows // step)
    def _(i):
        at = pl.ds(pl.multiple_of(i * step, step), step)
        v = src[at, :].astype(F32)
        mean = jnp.mean(v, axis=-1, keepdims=True)
        center = v - mean
        spread = jnp.mean(center * center, axis=-1, keepdims=True)
        dst[at, :] = (center * lax.rsqrt(spread + EPS) * gain[...] + bias[...]).astype(dst.dtype)


def view_rows(tiles):
    first = 16 * ((tiles + 1) // 2)
    halves = ((0, first), (first, 16 * tiles - first))

    def view(r, h, q):
        start, size = halves[h]
        if q is None:
            return r.at[pl.ds(start, size)]
        lead = 16 * ((size // 16 + 1) // 2)
        return r.at[pl.ds(start, lead)] if q == 0 else r.at[pl.ds(start + lead, size - lead)]

    return view


def k_qkv(
    tok, wq, wout, gain, bias, qbias, toks_o, qkv_o, wof_o,
    pack, qb, wo4, toks, qkv, slots, wf, wof, hb, lsem, osem, xs, xr, ws, wr, *gs
):
    x, y, z, c = position()
    t = lax.axis_index("tok")
    depth = wq.shape[1]
    heads = wq.shape[2] // HD
    nq = 3 * heads
    no = wof.shape[1] // 128
    meet(x_peers() + [x_dev(x, 2)] + tok_peers())
    wo_send = [rcopy(wout, wo4.at[x], ws.at[k], wr.at[k], x_dev(x, k + 1)) for k in range(3)]
    for d in wo_send:
        d.start()
    ring = RingGather(
        lambda i: tok.at[pl.ds(128 * i, 128)],
        lambda s, i: toks.at[s, pl.ds(128 * i, 128)],
        lambda k: xs.at[k],
        lambda k: xr.at[k],
    )
    ring.start()
    local = [pltpu.make_async_copy(tok, toks.at[x], lsem.at[0])]
    local[0].start()
    zero = jnp.zeros((depth, HPAD - HD), BF)
    for k in range(3):
        for h in range(heads):
            n = k * heads + h
            piece = wq[k, :, h * HD : h * HD + HD]
            pack[n * depth : n * depth + depth, :] = jnp.concatenate([piece, zero], axis=1)
            qb[:, n * HPAD : n * HPAD + HPAD] = jnp.concatenate(
                [qbias[k : k + 1, h * HD : h * HD + HD], jnp.zeros((1, HPAD - HD), F32)], axis=1
            )
    wo4[x] = wout[...]
    for d in wo_send:
        d.wait_recv()
    wide = jnp.concatenate([wo4[b] for b in range(4)], axis=1)
    for n in range(no):
        at = (nq + n) * depth
        pack[at : at + depth, :] = wide[:, 128 * n : 128 * n + 128]
    gath = TokGather(pack, slots, view_rows(pack.shape[0] // 16), *gs)
    gath.start()
    local.append(pltpu.make_async_copy(pack, slots.at[t], lsem.at[1]))
    local[1].start()
    norm_rows(tok, hb.at[x], gain, bias, 256)
    outs = []

    def put(src, dst):
        outs.append(pltpu.make_async_copy(src, dst, osem.at[len(outs)]))
        outs[-1].start()

    def unpack(g, lo, n, dst):
        for i in range(n):
            at = (lo + i) * depth
            parts = [slots[4 * g + j, at : at + depth, :] for j in range(4)]
            rows = pl.ds(pl.multiple_of(g * 208, 16), 208)
            dst[rows, 128 * i : 128 * i + 128] = jnp.concatenate(parts, axis=0)

    def unpack_qkv(k):
        gath.wait_cross(0, k)
        yy = (y + gath.OFF[k]) % 4

        @pl.loop(0, 2)
        def _(p):
            unpack(2 * yy + p, 0, nq, wf)

    def unpack_out(p):
        @pl.loop(0, 4)
        def _(yy):
            unpack(2 * yy + p, nq, no, wof)

    def project(s):
        @pl.loop(0, wf.shape[1] // 256)
        def _(j):
            cols = pl.ds(pl.multiple_of(j * 256, 256), 256)
            v = jnp.dot(hb[s], wf[:, cols], preferred_element_type=F32) + qb[:, cols]
            v = v.astype(BF)
            rows = pl.ds(pl.multiple_of(s * 256, 256), 256)
            qkv[2 * j, rows, :] = v[:, :128]
            qkv[2 * j + 1, rows, :] = v[:, 128:]

    for h in range(2):
        gath.first_near(h)
    ring.relay()
    for h in range(2):
        gath.first_far(h)
    for i in range(3):
        for h in range(2):
            gath.second_near(h, i)
    for d in local:
        d.wait()
    unpack_qkv(0)
    for h in range(2):
        gath.second_near(h, 3)
    ring.wait_near()
    for o in (0, 1, 3):
        s = (x + o) % 4
        put(toks.at[s], toks_o.at[s])
        if o:
            norm_rows(toks.at[s], hb.at[s], gain, bias, 256)
    unpack_qkv(1)
    unpack_qkv(2)
    for i in range(4):
        for h in range(2):
            gath.second_far(h, i)
    for k in range(3):
        gath.wait_cross(1, k)
    unpack_qkv(3)

    @pl.loop(0, 3)
    def _(i):
        project((x + i + i // 2) % 4)

    unpack_out(z // 2)
    gath.wait_cross(1, 3)
    unpack_out(1 - z // 2)
    put(wof, wof_o)
    ring.wait_far()
    far = (x + 2) % 4
    put(toks.at[far], toks_o.at[far])
    norm_rows(toks.at[far], hb.at[far], gain, bias, 256)
    project(far)
    put(qkv, qkv_o)
    for d in wo_send:
        d.wait_send()
    ring.finish()
    gath.finish()
    for d in outs:
        d.wait()


class RingReduce:
    def __init__(self, sbuf, far_in, main_in, ss, rs, half):
        x = lax.axis_index("blk")
        self.hi, self.lo, self.far = (x + 1) % 4, (x + 3) % 4, (x + 2) % 4
        self.sbuf, self.far_in, self.main_in = sbuf, far_in, main_in
        right, left = x_dev(x, 1), x_dev(x, 3)
        self.a, self.b = pl.ds(0, half), pl.ds(half, half)
        a, b = self.a, self.b
        self.c = [
            rcopy(sbuf.at[self.far, a], far_in.at[0], ss(0), rs(0), right),
            rcopy(sbuf.at[self.far, b], far_in.at[1], ss(1), rs(1), left),
            rcopy(sbuf.at[self.hi, b], main_in.at[0, b], ss(2), rs(2), right),
            rcopy(sbuf.at[self.lo, a], main_in.at[1, a], ss(3), rs(3), left),
            rcopy(sbuf.at[self.hi, a], main_in.at[0, a], ss(4), rs(4), right),
            rcopy(sbuf.at[self.lo, b], main_in.at[1, b], ss(5), rs(5), left),
        ]

    def start(self):
        for k in range(4):
            self.c[k].start()

    def relay(self):
        self.c[0].wait_recv()
        s = self.sbuf[self.hi, self.a].astype(F32) + self.far_in[0].astype(F32)
        self.sbuf[self.hi, self.a] = s.astype(BF)
        self.c[1].wait_recv()
        s = self.sbuf[self.lo, self.b].astype(F32) + self.far_in[1].astype(F32)
        self.sbuf[self.lo, self.b] = s.astype(BF)
        self.c[4].start()
        self.c[5].start()

    def wait(self):
        for k in range(2, 6):
            self.c[k].wait_recv()

    def finish(self):
        for d in self.c:
            d.wait_send()


def gelu(v):
    return 0.5 * v * (1.0 + lax.erf(v * (1.0 / math.sqrt(2.0))))


def k_layer(
    qkv, seg, toks_h, wof_h, ob, gain, bias, fc1, b1, fc2, b2, wp, lo, wpg,
    toks, wof, w1, w2, att, oh, attf, segc, after, h2, hid, own, sbuf, far_in, main_in,
    lsem, as_, ar, xs, xr, *gs
):
    x, y, z, c = position()
    t = lax.axis_index("tok")
    load = [
        pltpu.make_async_copy(wof_h, wof, lsem.at[0]),
        pltpu.make_async_copy(toks_h, toks, lsem.at[1]),
        pltpu.make_async_copy(fc1, w1, lsem.at[2]),
        pltpu.make_async_copy(fc2, w2, lsem.at[3]),
        pltpu.make_async_copy(wp, wpg.at[t], lsem.at[4]),
    ]
    for d in load:
        d.start()
    segr = seg[...].astype(F32)
    segc[...] = jnp.broadcast_to(segr, (128, segr.shape[1])).T
    meet(x_peers() + tok_peers())
    gath = TokGather(wp, wpg, view_rows(wp.shape[0] // 16), *gs)
    gath.start()
    scale = 1.0 / math.sqrt(HD)
    heads = qkv.shape[0] // 3

    def attend(r):
        @pl.loop(0, 2)
        def _(sub):
            rows = pl.ds(pl.multiple_of(r * 256 + sub * 128, 128), 128)
            same = segc[rows, 0:1] == segr
            for h in range(heads):
                s = lax.dot_general(
                    qkv[h, rows, :], qkv[heads + h], (((1,), (1,)), ((), ())), preferred_element_type=F32
                )
                p = jnp.where(same, jnp.exp(s * scale), 0.0)
                total = jnp.sum(p, axis=-1, keepdims=True)
                o = jnp.dot(p.astype(BF), qkv[2 * heads + h], preferred_element_type=F32) / total
                oh[h, pl.ds(pl.multiple_of(sub * 128, 128), 128), :] = o.astype(BF)

        att[x, pl.ds(r * 256, 256), :] = jnp.concatenate([oh[h][:, :HD] for h in range(heads)], axis=1)

    def gather_ring(r):
        def part(s, i):
            return att.at[s, pl.ds(pl.multiple_of(r * 256 + 128 * i, 128), 128)]

        return RingGather(lambda i: part(x, i), part, lambda k: as_.at[r, k], lambda k: ar.at[r, k])

    def reduce_ring(r):
        return RingReduce(
            sbuf.at[r],
            far_in.at[r],
            main_in.at[r],
            lambda k: xs.at[r, k],
            lambda k: xr.at[r, k],
            128,
        )

    attend(0)
    gather_ring(0).start()
    for h in range(2):
        gath.first_near(h)
    attend(1)
    gather_ring(0).relay()
    gather_ring(1).start()
    for h in range(2):
        gath.first_far(h)
    attend(2)
    gather_ring(1).relay()
    gather_ring(2).start()
    attend(3)
    gather_ring(2).relay()
    gather_ring(3).start()
    tiles = [(n, min(256, 1664 - n)) for n in range(0, 1664, 256)]
    for d in load[:2]:
        d.wait()

    @pl.loop(0, 6)
    def _(r):
        @pl.when(r < 4)
        def _():
            rg = gather_ring(r)
            rg.wait_near()
            rg.wait_far()
            rows = pl.ds(pl.multiple_of(r * 256, 256), 256)
            attf[...] = jnp.concatenate([att[b, rows, :] for b in range(4)], axis=1)
            for n, w in tiles:
                acc = lax.dot_general(
                    attf[...], wof[n : n + w, :], (((1,), (1,)), ((), ())), preferred_element_type=F32
                )
                after[:, n : n + w] = acc + toks[r, :, n : n + w].astype(F32) + ob[n : n + w]

            @pl.when(r == 0)
            def _():
                gather_ring(3).relay()
                load[2].wait()
                for i in range(4):
                    for h in range(2):
                        gath.second_near(h, i)

            @pl.when(r > 0)
            def _():
                reduce_ring(r - 1).relay()

            @pl.when(r == 2)
            def _():
                for i in range(4):
                    for h in range(2):
                        gath.second_far(h, i)

            norm_rows(after, h2, gain, bias, 256)
            for j in range(4):

                @pl.when(x == j)
                def _():
                    own[r] = after[:, 416 * j : 416 * j + 416] + b2[416 * j : 416 * j + 416]

            for j in range(8):
                cols = slice(256 * j, 256 * j + 256)
                v = jnp.dot(h2[...], w1[:, cols], preferred_element_type=F32) + b1[cols]
                hid[:, cols] = gelu(v).astype(BF)

            @pl.when(r == 0)
            def _():
                load[3].wait()

            for n, w in tiles:
                after[:, n : n + w] = jnp.dot(hid[...], w2[:, n : n + w], preferred_element_type=F32)
            for j in range(4):
                piece = after[:, 416 * j : 416 * j + 416]
                sbuf[r, j] = piece.astype(BF)

                @pl.when(x == j)
                def _():
                    own[r] += piece

            reduce_ring(r).start()

        @pl.when(r == 4)
        def _():
            reduce_ring(3).relay()

        @pl.when(r > 1)
        def _():
            q = r - 2
            rg = reduce_ring(q)
            rg.wait()
            total = own[q] + main_in[q, 0].astype(F32) + main_in[q, 1].astype(F32)
            lo[pl.ds(pl.multiple_of(q * 256, 256), 256), :] = total.astype(BF)
            rg.finish()
            gather_ring(q).finish()

    load[4].wait()
    for h in range(2):
        for k in range(4):
            gath.wait_cross(h, k)
    gath.finish()


def column(rows):
    n, m = rows.shape
    return jnp.concatenate([rows, jnp.zeros((128 - n, m), F32)], axis=0).T


def k_merge(
    lo, gain3, bias3, mi, seg, owners, wpg_h, pb, out,
    wpg, fin, gb, sbuf, own, far_in, main_in, st, placed, obuf, lsem, ss, sr, xs, xr, ts, tr
):
    x, y, z, c = position()
    t = lax.axis_index("tok")
    n_tok = out.shape[0]
    slot = out.shape[1]
    merged = mi.shape[1]
    n_loc = lo.shape[1]
    load = pltpu.make_async_copy(wpg_h, wpg, lsem.at[0])
    load.start()
    bar = pltpu.get_barrier_semaphore()

    @pl.loop(1, n_tok)
    def _(i):
        pl.semaphore_signal(bar, inc=1, device_id={"tok": (t + i) % n_tok}, device_id_type=MESH_ID)

    @pl.loop(1, 4)
    def _(i):
        pl.semaphore_signal(bar, inc=1, device_id=x_dev(x, i), device_id_type=MESH_ID)

    @pl.loop(0, 8)
    def _(i):
        rows = pl.ds(pl.multiple_of(i * 128, 128), 128)
        v = lo[rows, :].astype(F32)
        mean = jnp.mean(v, axis=-1, keepdims=True)
        d = v - mean
        m2 = jnp.sum(d * d, axis=-1, keepdims=True)
        lane = lax.broadcasted_iota(jnp.int32, (128, 128), 1)
        both = jnp.where(lane == 0, mean, jnp.where(lane == 1, m2, 0.0))
        st[x, :, rows] = both.T[:8]

    pl.semaphore_wait(bar, n_tok + 2)
    sends = [rcopy(st.at[x], st.at[x], ss.at[k], sr.at[k], x_dev(x, k + 1)) for k in range(3)]
    for d in sends:
        d.start()
    for j in range(4):

        @pl.when(x == j)
        def _():
            gb[0:1, :] = gain3[n_loc * j : n_loc * j + n_loc].reshape(1, n_loc)
            gb[1:2, :] = bias3[n_loc * j : n_loc * j + n_loc].reshape(1, n_loc)

    idx = column(mi[...].astype(F32))
    toks = lax.broadcasted_iota(jnp.int32, (merged, 1024), 1).astype(F32)
    seg_of = jnp.sum(jnp.where(idx[:, 0:1] == toks, seg[...].astype(F32), 0.0), axis=1, keepdims=True)
    names = lax.broadcasted_iota(jnp.int32, (merged, n_tok), 1).astype(F32)
    owner = jnp.sum(jnp.where(seg_of == names, owners[...].astype(F32), 0.0), axis=1, keepdims=True)
    mine = (owner == names).astype(F32)
    below = lax.broadcasted_iota(jnp.int32, (merged, merged), 1) < lax.broadcasted_iota(
        jnp.int32, (merged, merged), 0
    )
    before = jnp.dot(
        jnp.where(below, 1.0, 0.0).astype(BF), mine.astype(BF), preferred_element_type=F32
    )
    rank = jnp.sum(before * mine, axis=1, keepdims=True)
    target = jnp.broadcast_to(owner * slot + rank, (merged, 128)).T[0:1]
    spots = lax.broadcasted_iota(jnp.int32, (n_tok * slot, merged), 0).astype(F32)
    placed[...] = jnp.where(spots == target, 1.0, 0.0).astype(BF)
    for d in sends:
        d.wait_recv()
    means = [st[s, 0:1, :] for s in range(4)]
    mean = 0.25 * (means[0] + means[1] + means[2] + means[3])
    m2 = st[0, 1:2, :] + st[1, 1:2, :] + st[2, 1:2, :] + st[3, 1:2, :]
    for s in range(4):
        d = means[s] - mean
        m2 = m2 + n_loc * (d * d)
    rstd = lax.rsqrt(m2 * (1.0 / (4 * n_loc)) + EPS)
    for i in range(8):
        sl = slice(128 * i, 128 * i + 128)
        row = lax.broadcasted_iota(jnp.int32, (128, 128), 0)
        cols = jnp.where(row == 0, mean[:, sl], jnp.where(row == 1, rstd[:, sl], 0.0)).T
        v = lo[sl, :].astype(F32)
        fin[sl, :] = ((v - cols[:, 0:1]) * cols[:, 1:2] * gb[0:1, :] + gb[1:2, :]).astype(BF)
    load.wait()
    got = []
    for k in range(4):
        pick = jnp.where(idx[:, k : k + 1] == toks, 1.0, 0.0).astype(BF)
        got.append(jnp.dot(pick, fin[...], preferred_element_type=F32).astype(BF))
    for j in range(4):
        acc = jnp.dot(got[0], wpg[j], preferred_element_type=F32)
        for k in range(1, 4):
            acc += jnp.dot(got[k], wpg[k * 4 + j], preferred_element_type=F32)
        own[j] = acc
        sbuf[j] = acc.astype(BF)
    rg = RingReduce(sbuf, far_in, main_in, lambda k: xs.at[k], lambda k: xr.at[k], 128)
    rg.start()
    rg.relay()
    rg.wait()
    total = own[x] + main_in[0].astype(F32) + main_in[1].astype(F32) + pb[...]
    going = jnp.dot(placed[...], total.astype(BF), preferred_element_type=F32).astype(BF)
    obuf[...] = going.reshape(n_tok, slot, n_loc)

    def slot_copy(i):
        to = (t + i) % n_tok
        return rcopy(obuf.at[to], out.at[t], ts.at[i], tr.at[i], {"tok": to})

    @pl.loop(1, n_tok)
    def _(i):
        slot_copy(i).start()

    keep = pltpu.make_async_copy(obuf.at[t], out.at[t], lsem.at[1])
    keep.start()
    rg.finish()
    for d in sends:
        d.wait_send()
    keep.wait()

    @pl.loop(1, n_tok)
    def _(i):
        slot_copy(i).wait()


def kernel_call(body, name, cid, ins, outs, out_specs, scratch, args):
    return pl.pallas_call(
        body,
        name=name,
        out_shape=outs,
        in_specs=ins,
        out_specs=out_specs,
        scratch_shapes=scratch,
        compiler_params=pltpu.CompilerParams(
            collective_id=cid, has_side_effects=True, vmem_limit_bytes=VLIM
        ),
    )(*args)


def sds(shape, dtype):
    return jax.ShapeDtypeStruct(shape, dtype)


DMA = pltpu.SemaphoreType.DMA


def body(
    tokens,
    segment_ids,
    merge_index,
    segment_owner,
    ln1_gain,
    ln1_bias,
    w_qkv,
    qkv_bias,
    w_out,
    out_bias,
    ln2_gain,
    ln2_bias,
    w_fc1,
    fc1_bias,
    w_fc2,
    fc2_bias,
    ln3_gain,
    ln3_bias,
    w_proj,
    proj_bias,
):
    tok = tokens[0]
    width = tok.shape[1]
    part_w = w_qkv.shape[2]
    depth = w_qkv.shape[1]
    heads = part_w // HD
    cols = 3 * heads * HPAD
    blocks = (cols + width) // 128
    packed = 16 * (-(-blocks * depth // 16))
    hidden = w_fc1.shape[1]
    perm = []
    for bx in range(4):
        for t in range(32):
            ty, tz, tc = t // 8, (t // 2) % 4, t % 2
            perm.append((bx * 32 + t, tz * 32 + (ty * 4 + bx) * 2 + tc))
    wp = lax.ppermute(w_proj, ("blk", "tok"), perm)
    toks, qkv, wof = kernel_call(
        k_qkv,
        "qkv",
        1,
        [VM] * 6,
        [sds((4, 256, width), BF), sds((3 * heads, 1024, HPAD), BF), sds((width, width), BF)],
        [ANY] * 3,
        [
            pltpu.VMEM((packed, 128), BF),
            pltpu.VMEM((1, cols), F32),
            pltpu.VMEM((4, depth, part_w), BF),
            pltpu.VMEM((4, 256, width), BF),
            pltpu.VMEM((3 * heads, 1024, HPAD), BF),
            pltpu.VMEM((32, packed, 128), BF),
            pltpu.VMEM((width, cols), BF),
            pltpu.VMEM((width, width), BF),
            pltpu.VMEM((4, 256, width), BF),
            DMA((2,)),
            DMA((6,)),
            DMA((6,)),
            DMA((6,)),
            DMA((3,)),
            DMA((3,)),
        ]
        + TOK_SEMS,
        (tok, w_qkv, w_out.T, ln1_gain, ln1_bias, qkv_bias),
    )
    lo, wpg = kernel_call(
        k_layer,
        "layer",
        2,
        [VM, VM, ANY, ANY, VM, VM, VM, ANY, VM, ANY, VM, VM],
        [sds((1024, part_w), BF), sds((32, 208, part_w), BF)],
        [VM, ANY],
        [
            pltpu.VMEM((4, 256, width), BF),
            pltpu.VMEM((width, width), BF),
            pltpu.VMEM((width, hidden), BF),
            pltpu.VMEM((hidden, width), BF),
            pltpu.VMEM((4, 1024, part_w), BF),
            pltpu.VMEM((heads, 256, HPAD), BF),
            pltpu.VMEM((256, width), BF),
            pltpu.VMEM((1024, 128), F32),
            pltpu.VMEM((256, width), F32),
            pltpu.VMEM((256, width), BF),
            pltpu.VMEM((256, hidden), BF),
            pltpu.VMEM((4, 256, part_w), F32),
            pltpu.VMEM((4, 4, 256, part_w), BF),
            pltpu.VMEM((4, 2, 128, part_w), BF),
            pltpu.VMEM((4, 2, 256, part_w), BF),
            DMA((5,)),
            DMA((4, 6)),
            DMA((4, 6)),
            DMA((4, 6)),
            DMA((4, 6)),
        ]
        + TOK_SEMS,
        (
            qkv, segment_ids, toks, wof, out_bias, ln2_gain, ln2_bias,
            w_fc1, fc1_bias, w_fc2, fc2_bias, wp,
        ),
    )
    merged_count = merge_index.shape[1]
    n_tok = lax.axis_size("tok")
    slot = 2 * merged_count // n_tok
    arrived = kernel_call(
        k_merge,
        "merge",
        3,
        [VM] * 6 + [ANY, VM],
        [sds((n_tok, slot, part_w), BF)],
        [VM],
        [
            pltpu.VMEM((16, part_w, part_w), BF),
            pltpu.VMEM((1024, part_w), BF),
            pltpu.VMEM((2, part_w), F32),
            pltpu.VMEM((4, 256, part_w), BF),
            pltpu.VMEM((4, 256, part_w), F32),
            pltpu.VMEM((2, 128, part_w), BF),
            pltpu.VMEM((2, 256, part_w), BF),
            pltpu.VMEM((4, 8, 1024), F32),
            pltpu.VMEM((n_tok * slot, merged_count), BF),
            pltpu.VMEM((n_tok, slot, part_w), BF),
            DMA((2,)),
            DMA((3,)),
            DMA((3,)),
            DMA((6,)),
            DMA((6,)),
            DMA((n_tok,)),
            DMA((n_tok,)),
        ],
        (
            lo,
            ln3_gain,
            ln3_bias,
            merge_index[0].T,
            segment_ids,
            segment_owner,
            wpg.reshape(16, part_w, part_w),
            proj_bias,
        ),
    )[0]
    return arrived[None]


def solution(mesh):
    placed = (
        P("tok", "blk", None),
        P("tok", None),
        P("tok", None, None),
        P("tok", None),
        P(),
        P(),
        P(None, "tok", "blk"),
        P(None, "blk"),
        P("blk", "tok"),
        P(),
        P(),
        P(),
        P(None, "blk"),
        P("blk"),
        P("blk", None),
        P(),
        P(),
        P(),
        P("tok", "blk"),
        P("blk"),
    )
    return jax.shard_map(
        body, mesh=mesh, in_specs=placed, out_specs=P("tok", None, None, "blk"), check_vma=False
    )
```

```python
import math

import jax
import jax.numpy as jnp
from jax import lax
from jax.experimental import pallas as pl
from jax.experimental.pallas import tpu as pltpu
from jax.sharding import PartitionSpec as P

HD = 104
HPAD = 128
EPS = 1e-06
BF = jnp.bfloat16
F32 = jnp.float32
MESH_ID = pl.DeviceIdType.MESH
VLIM = 65000 * 1024
VM = pl.BlockSpec(memory_space=pltpu.VMEM)
ANY = pl.BlockSpec(memory_space=pl.ANY)


def position():
    x = lax.axis_index("blk")
    t = lax.axis_index("tok")
    return x, t // 8, (t // 2) % 4, t % 2


def tok_of(y, z, c):
    return ((y % 4) * 4 + z % 4) * 2 + c


def rcopy(src, dst, ssem, rsem, dev):
    return pltpu.make_async_remote_copy(
        src_ref=src, dst_ref=dst, send_sem=ssem, recv_sem=rsem, device_id=dev, device_id_type=MESH_ID
    )


def x_dev(x, off):
    return {"blk": (x + off) % 4}


def meet(peers):
    bar = pltpu.get_barrier_semaphore()
    for dev in peers:
        pl.semaphore_signal(bar, inc=1, device_id=dev, device_id_type=MESH_ID)
    pl.semaphore_wait(bar, len(peers))


def x_peers():
    x, y, z, c = position()
    return [x_dev(x, 1), x_dev(x, 3)]


def tok_peers():
    x, y, z, c = position()
    return [
        {"tok": tok_of(y, z + 1, c)},
        {"tok": tok_of(y, z + 3, c)},
        {"tok": tok_of(y + 1, z, c)},
        {"tok": tok_of(y + 3, z, c)},
        {"tok": tok_of(y, z, 1 - c)},
    ]


class RingGather:
    def __init__(self, own, half, ss, rs):
        x = lax.axis_index("blk")
        right, left = x_dev(x, 1), x_dev(x, 3)

        def send(view, src, i, k, dev):
            return rcopy(view, half(src, i), ss(k), rs(k), dev)

        me, lo, hi = x, (x + 3) % 4, (x + 1) % 4
        self.c = [
            send(own(0), me, 0, 0, right),
            send(own(1), me, 1, 1, right),
            send(own(1), me, 1, 2, left),
            send(own(0), me, 0, 3, left),
            send(half(lo, 0), lo, 0, 4, right),
            send(half(hi, 1), hi, 1, 5, left),
        ]

    def start(self):
        for k in (0, 2, 1, 3):
            self.c[k].start()

    def relay(self):
        self.c[0].wait_recv()
        self.c[4].start()
        self.c[2].wait_recv()
        self.c[5].start()

    def wait_near(self):
        self.c[1].wait_recv()
        self.c[3].wait_recv()

    def wait_far(self):
        self.c[4].wait_recv()
        self.c[5].wait_recv()

    def finish(self):
        for c in self.c:
            c.wait_send()


class TokGather:
    OFF = (0, 3, 1, 2)

    def __init__(self, own, slots, view, fs, fr, ss, sr, cs, cr):
        x, y, z, c = position()
        self.first, self.second, self.cross = [], [], []
        sib = {"tok": tok_of(y, z, 1 - c)}
        for h in range(2):

            def tok(d1, d2, h=h):
                return tok_of(y + d2, z + d1, c) if h == 0 else tok_of(y + d1, z + d2, c)

            def slot(d1, d2, tok=tok):
                return slots.at[tok(d1, d2)]

            def half(r, h=h):
                return view(r, h, None)

            def quarter(r, q, h=h):
                return view(r, h, q)

            me = slot(0, 0)
            p1, m1 = {"tok": tok(1, 0)}, {"tok": tok(3, 0)}
            p2, m2 = {"tok": tok(0, 1)}, {"tok": tok(0, 3)}
            self.first.append(
                [
                    rcopy(half(own), half(me), fs.at[h, 0], fr.at[h, 0], p1),
                    rcopy(half(own), half(me), fs.at[h, 1], fr.at[h, 1], m1),
                    rcopy(quarter(slot(3, 0), 0), quarter(slot(3, 0), 0), fs.at[h, 2], fr.at[h, 2], p1),
                    rcopy(quarter(slot(1, 0), 1), quarter(slot(1, 0), 1), fs.at[h, 3], fr.at[h, 3], m1),
                ]
            )
            second = []
            for i, o in enumerate(self.OFF):
                src = half(own) if i == 0 else half(slot(o, 0))
                here, up, dn = half(slot(o, 0)), slot(o, 3), slot(o, 1)
                second.append(
                    [
                        rcopy(src, here, ss.at[h, i, 0], sr.at[h, i, 0], p2),
                        rcopy(src, here, ss.at[h, i, 1], sr.at[h, i, 1], m2),
                        rcopy(quarter(up, 0), quarter(up, 0), ss.at[h, i, 2], sr.at[h, i, 2], p2),
                        rcopy(quarter(dn, 1), quarter(dn, 1), ss.at[h, i, 3], sr.at[h, i, 3], m2),
                    ]
                )
            self.second.append(second)
            cross = []
            for k in range(4):
                row = []
                for i, o in enumerate(self.OFF):
                    dst = half(slot(o, self.OFF[k]))
                    src = half(own) if (i == 0 and k == 0) else dst
                    row.append(rcopy(src, dst, cs.at[h, k, i], cr.at[h, k, i], sib))
                cross.append(row)
            self.cross.append(cross)

    def start(self):
        for h in range(2):
            self.first[h][0].start()
            self.first[h][1].start()
        for h in range(2):
            self._fan(h, 0)

    def _fan(self, h, i):
        self.second[h][i][0].start()
        self.second[h][i][1].start()
        self.cross[h][0][i].start()

    def first_near(self, h):
        f = self.first[h]
        f[0].wait_recv()
        f[2].start()
        self._fan(h, 1)
        f[1].wait_recv()
        f[3].start()
        self._fan(h, 2)

    def first_far(self, h):
        self.first[h][2].wait_recv()
        self.first[h][3].wait_recv()
        self._fan(h, 3)

    def second_near(self, h, i):
        f = self.second[h][i]
        f[0].wait_recv()
        f[2].start()
        self.cross[h][1][i].start()
        f[1].wait_recv()
        f[3].start()
        self.cross[h][2][i].start()

    def second_far(self, h, i):
        f = self.second[h][i]
        f[2].wait_recv()
        f[3].wait_recv()
        self.cross[h][3][i].start()

    def wait_cross(self, h, k):
        for d in self.cross[h][k]:
            d.wait_recv()

    def _all(self):
        for h in range(2):
            for row in self.cross[h]:
                yield from row

    def finish(self):
        for h in range(2):
            for d in self.first[h]:
                d.wait_send()
            for row in self.second[h]:
                for d in row:
                    d.wait_send()
        for d in self._all():
            d.wait_send()


TOK_SEMS = [pltpu.SemaphoreType.DMA((2, 4))] * 2 + [pltpu.SemaphoreType.DMA((2, 4, 4))] * 4


def norm_rows(src, dst, gain, bias, rows, step=32):
    @pl.loop(0, rows // step)
    def _(i):
        at = pl.ds(pl.multiple_of(i * step, step), step)
        v = src[at, :].astype(F32)
        mean = jnp.mean(v, axis=-1, keepdims=True)
        center = v - mean
        spread = jnp.mean(center * center, axis=-1, keepdims=True)
        dst[at, :] = (center * lax.rsqrt(spread + EPS) * gain[...] + bias[...]).astype(dst.dtype)


def view_rows(tiles):
    first = 16 * ((tiles + 1) // 2)
    halves = ((0, first), (first, 16 * tiles - first))

    def view(r, h, q):
        start, size = halves[h]
        if q is None:
            return r.at[pl.ds(start, size)]
        lead = 16 * ((size // 16 + 1) // 2)
        return r.at[pl.ds(start, lead)] if q == 0 else r.at[pl.ds(start + lead, size - lead)]

    return view


def k_qkv(
    tok, wq, wout, gain, bias, qbias, toks_o, qkv_o, wof_o,
    pack, qb, wo4, toks, qkv, slots, wf, wof, hb, lsem, osem, xs, xr, ws, wr, *gs
):
    x, y, z, c = position()
    t = lax.axis_index("tok")
    depth = wq.shape[1]
    heads = wq.shape[2] // HD
    nq = 3 * heads
    no = wof.shape[1] // 128
    meet(x_peers() + [x_dev(x, 2)] + tok_peers())
    wo_send = [rcopy(wout, wo4.at[x], ws.at[k], wr.at[k], x_dev(x, k + 1)) for k in range(3)]
    for d in wo_send:
        d.start()
    ring = RingGather(
        lambda i: tok.at[pl.ds(128 * i, 128)],
        lambda s, i: toks.at[s, pl.ds(128 * i, 128)],
        lambda k: xs.at[k],
        lambda k: xr.at[k],
    )
    ring.start()
    local = [pltpu.make_async_copy(tok, toks.at[x], lsem.at[0])]
    local[0].start()
    zero = jnp.zeros((depth, HPAD - HD), BF)
    for k in range(3):
        for h in range(heads):
            n = k * heads + h
            piece = wq[k, :, h * HD : h * HD + HD]
            pack[n * depth : n * depth + depth, :] = jnp.concatenate([piece, zero], axis=1)
            qb[:, n * HPAD : n * HPAD + HPAD] = jnp.concatenate(
                [qbias[k : k + 1, h * HD : h * HD + HD], jnp.zeros((1, HPAD - HD), F32)], axis=1
            )
    wo4[x] = wout[...]
    for d in wo_send:
        d.wait_recv()
    wide = jnp.concatenate([wo4[b] for b in range(4)], axis=1)
    for n in range(no):
        at = (nq + n) * depth
        pack[at : at + depth, :] = wide[:, 128 * n : 128 * n + 128]
    gath = TokGather(pack, slots, view_rows(pack.shape[0] // 16), *gs)
    gath.start()
    local.append(pltpu.make_async_copy(pack, slots.at[t], lsem.at[1]))
    local[1].start()
    norm_rows(tok, hb.at[x], gain, bias, 256)
    outs = []

    def put(src, dst):
        outs.append(pltpu.make_async_copy(src, dst, osem.at[len(outs)]))
        outs[-1].start()

    def unpack(g, lo, n, dst):
        for i in range(n):
            at = (lo + i) * depth
            parts = [slots[4 * g + j, at : at + depth, :] for j in range(4)]
            rows = pl.ds(pl.multiple_of(g * 208, 16), 208)
            dst[rows, 128 * i : 128 * i + 128] = jnp.concatenate(parts, axis=0)

    def unpack_qkv(k):
        gath.wait_cross(0, k)
        yy = (y + gath.OFF[k]) % 4

        @pl.loop(0, 2)
        def _(p):
            unpack(2 * yy + p, 0, nq, wf)

    def unpack_out(p):
        @pl.loop(0, 4)
        def _(yy):
            unpack(2 * yy + p, nq, no, wof)

    def project(s):
        @pl.loop(0, wf.shape[1] // 256)
        def _(j):
            cols = pl.ds(pl.multiple_of(j * 256, 256), 256)
            v = jnp.dot(hb[s], wf[:, cols], preferred_element_type=F32) + qb[:, cols]
            v = v.astype(BF)
            rows = pl.ds(pl.multiple_of(s * 256, 256), 256)
            qkv[2 * j, rows, :] = v[:, :128]
            qkv[2 * j + 1, rows, :] = v[:, 128:]

    for h in range(2):
        gath.first_near(h)
    ring.relay()
    for h in range(2):
        gath.first_far(h)
    for i in range(3):
        for h in range(2):
            gath.second_near(h, i)
    for d in local:
        d.wait()
    unpack_qkv(0)
    for h in range(2):
        gath.second_near(h, 3)
    ring.wait_near()
    for o in (0, 1, 3):
        s = (x + o) % 4
        put(toks.at[s], toks_o.at[s])
        if o:
            norm_rows(toks.at[s], hb.at[s], gain, bias, 256)
    unpack_qkv(1)
    unpack_qkv(2)
    for i in range(4):
        for h in range(2):
            gath.second_far(h, i)
    for k in range(3):
        gath.wait_cross(1, k)
    unpack_qkv(3)

    @pl.loop(0, 3)
    def _(i):
        project((x + i + i // 2) % 4)

    unpack_out(z // 2)
    gath.wait_cross(1, 3)
    unpack_out(1 - z // 2)
    put(wof, wof_o)
    ring.wait_far()
    far = (x + 2) % 4
    put(toks.at[far], toks_o.at[far])
    norm_rows(toks.at[far], hb.at[far], gain, bias, 256)
    project(far)
    put(qkv, qkv_o)
    for d in wo_send:
        d.wait_send()
    ring.finish()
    gath.finish()
    for d in outs:
        d.wait()


def pack_rows(v, dst):
    rows, width = v.shape
    full = width // 128
    rest = width - 128 * full
    for i in range(full):
        dst[rows * i : rows * i + rows] = v[:, 128 * i : 128 * i + 128]
    n = 128 // rest
    part = rows // n
    tail = [v[part * q : part * q + part, 128 * full :] for q in range(n)]
    dst[rows * full : rows * full + part] = jnp.concatenate(tail, axis=1)


def unpack_rows(src, rows=256, rest=32):
    n = 128 // rest
    part = rows // n
    full = (src.shape[0] - part) // rows
    last = src[rows * full : rows * full + part]
    tail = jnp.concatenate([last[:, rest * q : rest * q + rest] for q in range(n)], axis=0)
    return jnp.concatenate([src[rows * i : rows * i + rows] for i in range(full)] + [tail], axis=1)


class RingReduce:
    def __init__(self, sbuf, far_in, main_in, ss, rs, half):
        x = lax.axis_index("blk")
        self.hi, self.lo, self.far = (x + 1) % 4, (x + 3) % 4, (x + 2) % 4
        self.sbuf, self.far_in, self.main_in = sbuf, far_in, main_in
        right, left = x_dev(x, 1), x_dev(x, 3)
        self.a, self.b = pl.ds(0, half), pl.ds(half, half)
        a, b = self.a, self.b
        self.c = [
            rcopy(sbuf.at[self.far, a], far_in.at[0], ss(0), rs(0), right),
            rcopy(sbuf.at[self.far, b], far_in.at[1], ss(1), rs(1), left),
            rcopy(sbuf.at[self.hi, b], main_in.at[0, b], ss(2), rs(2), right),
            rcopy(sbuf.at[self.lo, a], main_in.at[1, a], ss(3), rs(3), left),
            rcopy(sbuf.at[self.hi, a], main_in.at[0, a], ss(4), rs(4), right),
            rcopy(sbuf.at[self.lo, b], main_in.at[1, b], ss(5), rs(5), left),
        ]

    def start(self):
        for k in range(4):
            self.c[k].start()

    def relay(self):
        self.c[0].wait_recv()
        s = self.sbuf[self.hi, self.a].astype(F32) + self.far_in[0].astype(F32)
        self.sbuf[self.hi, self.a] = s.astype(BF)
        self.c[1].wait_recv()
        s = self.sbuf[self.lo, self.b].astype(F32) + self.far_in[1].astype(F32)
        self.sbuf[self.lo, self.b] = s.astype(BF)
        self.c[4].start()
        self.c[5].start()

    def wait(self):
        for k in range(2, 6):
            self.c[k].wait_recv()

    def finish(self):
        for d in self.c:
            d.wait_send()


def gelu(v):
    return 0.5 * v * (1.0 + lax.erf(v * (1.0 / math.sqrt(2.0))))


def k_layer(
    qkv, seg, toks_h, wof_h, ob, gain, bias, fc1, b1, fc2, b2, wp, lo, wpg,
    toks, wof, w1, w2, att, oh, attf, segc, after, h2, hid, own, mine, sbuf, far_in, main_in,
    lsem, as_, ar, xs, xr, *gs
):
    x, y, z, c = position()
    t = lax.axis_index("tok")
    load = [
        pltpu.make_async_copy(wof_h, wof, lsem.at[0]),
        pltpu.make_async_copy(toks_h, toks, lsem.at[1]),
        pltpu.make_async_copy(fc1, w1, lsem.at[2]),
        pltpu.make_async_copy(fc2, w2, lsem.at[3]),
        pltpu.make_async_copy(wp, wpg.at[t], lsem.at[4]),
    ]
    for d in load:
        d.start()
    segr = seg[...].astype(F32)
    segc[...] = jnp.broadcast_to(segr, (128, segr.shape[1])).T
    meet(x_peers() + tok_peers())
    gath = TokGather(wp, wpg, view_rows(wp.shape[0] // 16), *gs)
    gath.start()
    scale = 1.0 / math.sqrt(HD)
    half = att.shape[2] // 2
    heads = qkv.shape[0] // 3

    def attend(r):
        @pl.loop(0, 2)
        def _(sub):
            rows = pl.ds(pl.multiple_of(r * 256 + sub * 128, 128), 128)
            same = segc[rows, 0:1] == segr
            for h in range(heads):
                s = lax.dot_general(
                    qkv[h, rows, :], qkv[heads + h], (((1,), (1,)), ((), ())), preferred_element_type=F32
                )
                p = jnp.where(same, jnp.exp(s * scale), 0.0)
                total = jnp.sum(p, axis=-1, keepdims=True)
                o = jnp.dot(p.astype(BF), qkv[2 * heads + h], preferred_element_type=F32) / total
                oh[h, pl.ds(pl.multiple_of(sub * 128, 128), 128), :] = o.astype(BF)

        pack_rows(jnp.concatenate([oh[h][:, :HD] for h in range(heads)], axis=1), att.at[x, r])

    def gather_ring(r):
        def part(s, i):
            return att.at[s, r, pl.ds(half * i, half)]

        return RingGather(lambda i: part(x, i), part, lambda k: as_.at[r, k], lambda k: ar.at[r, k])

    def reduce_ring(r):
        return RingReduce(
            sbuf.at[r],
            far_in.at[r],
            main_in.at[r],
            lambda k: xs.at[r, k],
            lambda k: xr.at[r, k],
            half,
        )

    attend(0)
    gather_ring(0).start()
    for h in range(2):
        gath.first_near(h)
    attend(1)
    gather_ring(0).relay()
    gather_ring(1).start()
    for h in range(2):
        gath.first_far(h)
    attend(2)
    gather_ring(1).relay()
    gather_ring(2).start()
    attend(3)
    gather_ring(2).relay()
    gather_ring(3).start()
    tiles = [(n, min(256, 1664 - n)) for n in range(0, 1664, 256)]
    for d in load[:2]:
        d.wait()

    @pl.loop(0, 6)
    def _(r):
        @pl.when(r < 4)
        def _():
            rg = gather_ring(r)
            rg.wait_near()
            rg.wait_far()
            attf[...] = jnp.concatenate([unpack_rows(att.at[b, r]) for b in range(4)], axis=1)
            for n, w in tiles:
                acc = lax.dot_general(
                    attf[...], wof[n : n + w, :], (((1,), (1,)), ((), ())), preferred_element_type=F32
                )
                after[:, n : n + w] = acc + toks[r, :, n : n + w].astype(F32) + ob[n : n + w]

            @pl.when(r == 0)
            def _():
                gather_ring(3).relay()
                load[2].wait()
                for i in range(4):
                    for h in range(2):
                        gath.second_near(h, i)

            @pl.when(r > 0)
            def _():
                reduce_ring(r - 1).relay()

            @pl.when(r == 2)
            def _():
                for i in range(4):
                    for h in range(2):
                        gath.second_far(h, i)

            norm_rows(after, h2, gain, bias, 256)
            for j in range(4):

                @pl.when(x == j)
                def _():
                    pack_rows(after[:, 416 * j : 416 * j + 416] + b2[416 * j : 416 * j + 416], own.at[r])

            for j in range(8):
                cols = slice(256 * j, 256 * j + 256)
                v = jnp.dot(h2[...], w1[:, cols], preferred_element_type=F32) + b1[cols]
                hid[:, cols] = gelu(v).astype(BF)

            @pl.when(r == 0)
            def _():
                load[3].wait()

            for n, w in tiles:
                after[:, n : n + w] = jnp.dot(hid[...], w2[:, n : n + w], preferred_element_type=F32)
            for j in range(4):
                piece = after[:, 416 * j : 416 * j + 416]
                pack_rows(piece.astype(BF), sbuf.at[r, j])

                @pl.when(x == j)
                def _():
                    pack_rows(piece, mine)
                    own[r] += mine[...]

            reduce_ring(r).start()

        @pl.when(r == 4)
        def _():
            reduce_ring(3).relay()

        @pl.when(r > 1)
        def _():
            q = r - 2
            rg = reduce_ring(q)
            rg.wait()
            total = own[q] + main_in[q, 0].astype(F32) + main_in[q, 1].astype(F32)
            lo[q] = total.astype(BF)
            rg.finish()
            gather_ring(q).finish()

    load[4].wait()
    for h in range(2):
        for k in range(4):
            gath.wait_cross(h, k)
    gath.finish()


def column(rows):
    n, m = rows.shape
    return jnp.concatenate([rows, jnp.zeros((128 - n, m), F32)], axis=0).T


def k_merge(
    lo, gain3, bias3, mi, seg, owners, wpg_h, pb, out,
    wpg, rows_f, fin, gb, sbuf, own, far_in, main_in, st, placed, obuf, lsem, ss, sr, xs, xr, ts, tr
):
    x, y, z, c = position()
    t = lax.axis_index("tok")
    n_tok = out.shape[0]
    slot = out.shape[1]
    merged = mi.shape[1]
    n_loc = wpg.shape[2]
    load = pltpu.make_async_copy(wpg_h, wpg, lsem.at[0])
    load.start()
    bar = pltpu.get_barrier_semaphore()

    @pl.loop(1, n_tok)
    def _(i):
        pl.semaphore_signal(bar, inc=1, device_id={"tok": (t + i) % n_tok}, device_id_type=MESH_ID)

    @pl.loop(1, 4)
    def _(i):
        pl.semaphore_signal(bar, inc=1, device_id=x_dev(x, i), device_id_type=MESH_ID)

    @pl.loop(0, 4)
    def _(i):
        rows = pl.ds(pl.multiple_of(i * 256, 256), 256)
        v = unpack_rows(lo.at[i]).astype(F32)
        rows_f[rows, :] = v
        mean = jnp.mean(v, axis=-1, keepdims=True)
        d = v - mean
        m2 = jnp.sum(d * d, axis=-1, keepdims=True)
        lane = lax.broadcasted_iota(jnp.int32, (256, 128), 1)
        both = jnp.where(lane == 0, mean, jnp.where(lane == 1, m2, 0.0))
        st[x, :, rows] = both.T[:8]

    pl.semaphore_wait(bar, n_tok + 2)
    sends = [rcopy(st.at[x], st.at[x], ss.at[k], sr.at[k], x_dev(x, k + 1)) for k in range(3)]
    for d in sends:
        d.start()
    for j in range(4):

        @pl.when(x == j)
        def _():
            gb[0:1, :] = gain3[n_loc * j : n_loc * j + n_loc].reshape(1, n_loc)
            gb[1:2, :] = bias3[n_loc * j : n_loc * j + n_loc].reshape(1, n_loc)

    idx = column(mi[...].astype(F32))
    toks = lax.broadcasted_iota(jnp.int32, (merged, 1024), 1).astype(F32)
    seg_of = jnp.sum(jnp.where(idx[:, 0:1] == toks, seg[...].astype(F32), 0.0), axis=1, keepdims=True)
    names = lax.broadcasted_iota(jnp.int32, (merged, n_tok), 1).astype(F32)
    owner = jnp.sum(jnp.where(seg_of == names, owners[...].astype(F32), 0.0), axis=1, keepdims=True)
    mine = (owner == names).astype(F32)
    below = lax.broadcasted_iota(jnp.int32, (merged, merged), 1) < lax.broadcasted_iota(
        jnp.int32, (merged, merged), 0
    )
    before = jnp.dot(
        jnp.where(below, 1.0, 0.0).astype(BF), mine.astype(BF), preferred_element_type=F32
    )
    rank = jnp.sum(before * mine, axis=1, keepdims=True)
    target = jnp.broadcast_to(owner * slot + rank, (merged, 128)).T[0:1]
    spots = lax.broadcasted_iota(jnp.int32, (n_tok * slot, merged), 0).astype(F32)
    placed[...] = jnp.where(spots == target, 1.0, 0.0).astype(BF)
    for d in sends:
        d.wait_recv()
    means = [st[s, 0:1, :] for s in range(4)]
    mean = 0.25 * (means[0] + means[1] + means[2] + means[3])
    m2 = st[0, 1:2, :] + st[1, 1:2, :] + st[2, 1:2, :] + st[3, 1:2, :]
    for s in range(4):
        d = means[s] - mean
        m2 = m2 + n_loc * (d * d)
    rstd = lax.rsqrt(m2 * (1.0 / (4 * n_loc)) + EPS)
    for i in range(8):
        sl = slice(128 * i, 128 * i + 128)
        row = lax.broadcasted_iota(jnp.int32, (128, 128), 0)
        cols = jnp.where(row == 0, mean[:, sl], jnp.where(row == 1, rstd[:, sl], 0.0)).T
        v = rows_f[sl, :]
        fin[sl, :] = ((v - cols[:, 0:1]) * cols[:, 1:2] * gb[0:1, :] + gb[1:2, :]).astype(BF)
    load.wait()
    got = []
    for k in range(4):
        pick = jnp.where(idx[:, k : k + 1] == toks, 1.0, 0.0).astype(BF)
        got.append(jnp.dot(pick, fin[...], preferred_element_type=F32).astype(BF))
    for j in range(4):
        acc = jnp.dot(got[0], wpg[j], preferred_element_type=F32)
        for k in range(1, 4):
            acc += jnp.dot(got[k], wpg[k * 4 + j], preferred_element_type=F32)
        pack_rows(acc, own.at[j])
        sbuf[j] = own[j].astype(BF)
    rg = RingReduce(sbuf, far_in, main_in, lambda k: xs.at[k], lambda k: xr.at[k], sbuf.shape[1] // 2)
    rg.start()
    rg.relay()
    rg.wait()
    own[x] += main_in[0].astype(F32) + main_in[1].astype(F32)
    total = unpack_rows(own.at[x]) + pb[...]
    going = jnp.dot(placed[...], total.astype(BF), preferred_element_type=F32).astype(BF)
    obuf[...] = going.reshape(n_tok, slot, n_loc)

    def slot_copy(i):
        to = (t + i) % n_tok
        return rcopy(obuf.at[to], out.at[t], ts.at[i], tr.at[i], {"tok": to})

    @pl.loop(1, n_tok)
    def _(i):
        slot_copy(i).start()

    keep = pltpu.make_async_copy(obuf.at[t], out.at[t], lsem.at[1])
    keep.start()
    rg.finish()
    for d in sends:
        d.wait_send()
    keep.wait()

    @pl.loop(1, n_tok)
    def _(i):
        slot_copy(i).wait()


def kernel_call(body, name, cid, ins, outs, out_specs, scratch, args):
    return pl.pallas_call(
        body,
        name=name,
        out_shape=outs,
        in_specs=ins,
        out_specs=out_specs,
        scratch_shapes=scratch,
        compiler_params=pltpu.CompilerParams(
            collective_id=cid, has_side_effects=True, vmem_limit_bytes=VLIM
        ),
    )(*args)


def sds(shape, dtype):
    return jax.ShapeDtypeStruct(shape, dtype)


DMA = pltpu.SemaphoreType.DMA


def body(
    tokens,
    segment_ids,
    merge_index,
    segment_owner,
    ln1_gain,
    ln1_bias,
    w_qkv,
    qkv_bias,
    w_out,
    out_bias,
    ln2_gain,
    ln2_bias,
    w_fc1,
    fc1_bias,
    w_fc2,
    fc2_bias,
    ln3_gain,
    ln3_bias,
    w_proj,
    proj_bias,
):
    tok = tokens[0]
    width = tok.shape[1]
    part_w = w_qkv.shape[2]
    depth = w_qkv.shape[1]
    heads = part_w // HD
    cols = 3 * heads * HPAD
    blocks = (cols + width) // 128
    packed = 16 * (-(-blocks * depth // 16))
    hidden = w_fc1.shape[1]
    flat = 256 * part_w // 128
    perm = []
    for bx in range(4):
        for t in range(32):
            ty, tz, tc = t // 8, (t // 2) % 4, t % 2
            perm.append((bx * 32 + t, tz * 32 + (ty * 4 + bx) * 2 + tc))
    wp = lax.ppermute(w_proj, ("blk", "tok"), perm)
    toks, qkv, wof = kernel_call(
        k_qkv,
        "qkv",
        1,
        [VM] * 6,
        [sds((4, 256, width), BF), sds((3 * heads, 1024, HPAD), BF), sds((width, width), BF)],
        [ANY] * 3,
        [
            pltpu.VMEM((packed, 128), BF),
            pltpu.VMEM((1, cols), F32),
            pltpu.VMEM((4, depth, part_w), BF),
            pltpu.VMEM((4, 256, width), BF),
            pltpu.VMEM((3 * heads, 1024, HPAD), BF),
            pltpu.VMEM((32, packed, 128), BF),
            pltpu.VMEM((width, cols), BF),
            pltpu.VMEM((width, width), BF),
            pltpu.VMEM((4, 256, width), BF),
            DMA((2,)),
            DMA((6,)),
            DMA((6,)),
            DMA((6,)),
            DMA((3,)),
            DMA((3,)),
        ]
        + TOK_SEMS,
        (tok, w_qkv, w_out.T, ln1_gain, ln1_bias, qkv_bias),
    )
    lo, wpg = kernel_call(
        k_layer,
        "layer",
        2,
        [VM, VM, ANY, ANY, VM, VM, VM, ANY, VM, ANY, VM, VM],
        [sds((4, flat, 128), BF), sds((32, 208, part_w), BF)],
        [VM, ANY],
        [
            pltpu.VMEM((4, 256, width), BF),
            pltpu.VMEM((width, width), BF),
            pltpu.VMEM((width, hidden), BF),
            pltpu.VMEM((hidden, width), BF),
            pltpu.VMEM((4, 4, flat, 128), BF),
            pltpu.VMEM((heads, 256, HPAD), BF),
            pltpu.VMEM((256, width), BF),
            pltpu.VMEM((1024, 128), F32),
            pltpu.VMEM((256, width), F32),
            pltpu.VMEM((256, width), BF),
            pltpu.VMEM((256, hidden), BF),
            pltpu.VMEM((4, flat, 128), F32),
            pltpu.VMEM((flat, 128), F32),
            pltpu.VMEM((4, 4, flat, 128), BF),
            pltpu.VMEM((4, 2, flat // 2, 128), BF),
            pltpu.VMEM((4, 2, flat, 128), BF),
            DMA((5,)),
            DMA((4, 6)),
            DMA((4, 6)),
            DMA((4, 6)),
            DMA((4, 6)),
        ]
        + TOK_SEMS,
        (
            qkv, segment_ids, toks, wof, out_bias, ln2_gain, ln2_bias,
            w_fc1, fc1_bias, w_fc2, fc2_bias, wp,
        ),
    )
    merged_count = merge_index.shape[1]
    n_tok = lax.axis_size("tok")
    slot = 2 * merged_count // n_tok
    arrived = kernel_call(
        k_merge,
        "merge",
        3,
        [VM] * 6 + [ANY, VM],
        [sds((n_tok, slot, part_w), BF)],
        [VM],
        [
            pltpu.VMEM((16, part_w, part_w), BF),
            pltpu.VMEM((1024, part_w), F32),
            pltpu.VMEM((1024, part_w), BF),
            pltpu.VMEM((2, part_w), F32),
            pltpu.VMEM((4, flat, 128), BF),
            pltpu.VMEM((4, flat, 128), F32),
            pltpu.VMEM((2, flat // 2, 128), BF),
            pltpu.VMEM((2, flat, 128), BF),
            pltpu.VMEM((4, 8, 1024), F32),
            pltpu.VMEM((n_tok * slot, merged_count), BF),
            pltpu.VMEM((n_tok, slot, part_w), BF),
            DMA((2,)),
            DMA((3,)),
            DMA((3,)),
            DMA((6,)),
            DMA((6,)),
            DMA((n_tok,)),
            DMA((n_tok,)),
        ],
        (
            lo,
            ln3_gain,
            ln3_bias,
            merge_index[0].T,
            segment_ids,
            segment_owner,
            wpg.reshape(16, part_w, part_w),
            proj_bias,
        ),
    )[0]
    return arrived[None]


def solution(mesh):
    placed = (
        P("tok", "blk", None),
        P("tok", None),
        P("tok", None, None),
        P("tok", None),
        P(),
        P(),
        P(None, "tok", "blk"),
        P(None, "blk"),
        P("blk", "tok"),
        P(),
        P(),
        P(),
        P(None, "blk"),
        P("blk"),
        P("blk", None),
        P(),
        P(),
        P(),
        P("tok", "blk"),
        P("blk"),
    )
    return jax.shard_map(
        body, mesh=mesh, in_specs=placed, out_specs=P("tok", None, None, "blk"), check_vma=False
    )
```

```python
import math

import jax
import jax.numpy as jnp
from jax import lax
from jax.experimental import pallas as pl
from jax.experimental.pallas import tpu as pltpu
from jax.sharding import PartitionSpec as P

HD = 104
HPAD = 128
EPS = 1e-06
BF = jnp.bfloat16
F32 = jnp.float32
MESH_ID = pl.DeviceIdType.MESH
VLIM = 65000 * 1024
VM = pl.BlockSpec(memory_space=pltpu.VMEM)
ANY = pl.BlockSpec(memory_space=pl.ANY)


def position():
    x = lax.axis_index("blk")
    t = lax.axis_index("tok")
    return x, t // 8, (t // 2) % 4, t % 2


def tok_of(y, z, c):
    return ((y % 4) * 4 + z % 4) * 2 + c


def rcopy(src, dst, ssem, rsem, dev):
    return pltpu.make_async_remote_copy(
        src_ref=src, dst_ref=dst, send_sem=ssem, recv_sem=rsem, device_id=dev, device_id_type=MESH_ID
    )


def x_dev(x, off):
    return {"blk": (x + off) % 4}


def meet(peers):
    bar = pltpu.get_barrier_semaphore()
    for dev in peers:
        pl.semaphore_signal(bar, inc=1, device_id=dev, device_id_type=MESH_ID)
    pl.semaphore_wait(bar, len(peers))


def x_peers():
    x, y, z, c = position()
    return [x_dev(x, 1), x_dev(x, 3)]


def tok_peers():
    x, y, z, c = position()
    return [
        {"tok": tok_of(y, z + 1, c)},
        {"tok": tok_of(y, z + 3, c)},
        {"tok": tok_of(y + 1, z, c)},
        {"tok": tok_of(y + 3, z, c)},
        {"tok": tok_of(y, z, 1 - c)},
    ]


class RingGather:
    def __init__(self, own, half, ss, rs):
        x = lax.axis_index("blk")
        right, left = x_dev(x, 1), x_dev(x, 3)

        def send(view, src, i, k, dev):
            return rcopy(view, half(src, i), ss(k), rs(k), dev)

        me, lo, hi = x, (x + 3) % 4, (x + 1) % 4
        self.c = [
            send(own(0), me, 0, 0, right),
            send(own(1), me, 1, 1, right),
            send(own(1), me, 1, 2, left),
            send(own(0), me, 0, 3, left),
            send(half(lo, 0), lo, 0, 4, right),
            send(half(hi, 1), hi, 1, 5, left),
        ]

    def start(self):
        for k in (0, 2, 1, 3):
            self.c[k].start()

    def relay(self):
        self.c[0].wait_recv()
        self.c[4].start()
        self.c[2].wait_recv()
        self.c[5].start()

    def wait_near(self):
        self.c[1].wait_recv()
        self.c[3].wait_recv()

    def wait_far(self):
        self.c[4].wait_recv()
        self.c[5].wait_recv()

    def finish(self):
        for c in self.c:
            c.wait_send()


class TokGather:
    OFF = (0, 3, 1, 2)

    def __init__(self, own, slots, view, fs, fr, ss, sr, cs, cr):
        x, y, z, c = position()
        self.first, self.second, self.cross = [], [], []
        sib = {"tok": tok_of(y, z, 1 - c)}
        for h in range(2):

            def tok(d1, d2, h=h):
                return tok_of(y + d2, z + d1, c) if h == 0 else tok_of(y + d1, z + d2, c)

            def slot(d1, d2, tok=tok):
                return slots.at[tok(d1, d2)]

            def half(r, h=h):
                return view(r, h, None)

            def quarter(r, q, h=h):
                return view(r, h, q)

            me = slot(0, 0)
            p1, m1 = {"tok": tok(1, 0)}, {"tok": tok(3, 0)}
            p2, m2 = {"tok": tok(0, 1)}, {"tok": tok(0, 3)}
            self.first.append(
                [
                    rcopy(half(own), half(me), fs.at[h, 0], fr.at[h, 0], p1),
                    rcopy(half(own), half(me), fs.at[h, 1], fr.at[h, 1], m1),
                    rcopy(quarter(slot(3, 0), 0), quarter(slot(3, 0), 0), fs.at[h, 2], fr.at[h, 2], p1),
                    rcopy(quarter(slot(1, 0), 1), quarter(slot(1, 0), 1), fs.at[h, 3], fr.at[h, 3], m1),
                ]
            )
            second = []
            for i, o in enumerate(self.OFF):
                src = half(own) if i == 0 else half(slot(o, 0))
                here, up, dn = half(slot(o, 0)), slot(o, 3), slot(o, 1)
                second.append(
                    [
                        rcopy(src, here, ss.at[h, i, 0], sr.at[h, i, 0], p2),
                        rcopy(src, here, ss.at[h, i, 1], sr.at[h, i, 1], m2),
                        rcopy(quarter(up, 0), quarter(up, 0), ss.at[h, i, 2], sr.at[h, i, 2], p2),
                        rcopy(quarter(dn, 1), quarter(dn, 1), ss.at[h, i, 3], sr.at[h, i, 3], m2),
                    ]
                )
            self.second.append(second)
            cross = []
            for k in range(4):
                row = []
                for i, o in enumerate(self.OFF):
                    dst = half(slot(o, self.OFF[k]))
                    src = half(own) if (i == 0 and k == 0) else dst
                    row.append(rcopy(src, dst, cs.at[h, k, i], cr.at[h, k, i], sib))
                cross.append(row)
            self.cross.append(cross)

    def start(self):
        for h in range(2):
            self.first[h][0].start()
            self.first[h][1].start()
        for h in range(2):
            self._fan(h, 0)

    def _fan(self, h, i):
        self.second[h][i][0].start()
        self.second[h][i][1].start()
        self.cross[h][0][i].start()

    def first_near(self, h):
        f = self.first[h]
        f[0].wait_recv()
        f[2].start()
        self._fan(h, 1)
        f[1].wait_recv()
        f[3].start()
        self._fan(h, 2)

    def first_far(self, h):
        self.first[h][2].wait_recv()
        self.first[h][3].wait_recv()
        self._fan(h, 3)

    def second_near(self, h, i):
        f = self.second[h][i]
        f[0].wait_recv()
        f[2].start()
        self.cross[h][1][i].start()
        f[1].wait_recv()
        f[3].start()
        self.cross[h][2][i].start()

    def second_far(self, h, i):
        f = self.second[h][i]
        f[2].wait_recv()
        f[3].wait_recv()
        self.cross[h][3][i].start()

    def wait_cross(self, h, k):
        for d in self.cross[h][k]:
            d.wait_recv()

    def _all(self):
        for h in range(2):
            for row in self.cross[h]:
                yield from row

    def finish(self):
        for h in range(2):
            for d in self.first[h]:
                d.wait_send()
            for row in self.second[h]:
                for d in row:
                    d.wait_send()
        for d in self._all():
            d.wait_send()


TOK_SEMS = [pltpu.SemaphoreType.DMA((2, 4))] * 2 + [pltpu.SemaphoreType.DMA((2, 4, 4))] * 4


def norm_rows(src, dst, gain, bias, rows, step=32):
    @pl.loop(0, rows // step)
    def _(i):
        at = pl.ds(pl.multiple_of(i * step, step), step)
        v = src[at, :].astype(F32)
        mean = jnp.mean(v, axis=-1, keepdims=True)
        center = v - mean
        spread = jnp.mean(center * center, axis=-1, keepdims=True)
        dst[at, :] = (center * lax.rsqrt(spread + EPS) * gain[...] + bias[...]).astype(dst.dtype)


def pack_rows(v, dst):
    rows, width = v.shape
    full = width // 128
    rest = width - 128 * full
    for i in range(full):
        dst[rows * i : rows * i + rows] = v[:, 128 * i : 128 * i + 128]
    n = 128 // rest
    part = rows // n
    tail = [v[part * q : part * q + part, 128 * full :] for q in range(n)]
    dst[rows * full : rows * full + part] = jnp.concatenate(tail, axis=1)


def unpack_rows(src, rows=256, rest=32):
    n = 128 // rest
    part = rows // n
    full = (src.shape[0] - part) // rows
    last = src[rows * full : rows * full + part]
    tail = jnp.concatenate([last[:, rest * q : rest * q + rest] for q in range(n)], axis=0)
    return jnp.concatenate([src[rows * i : rows * i + rows] for i in range(full)] + [tail], axis=1)


class RingReduce:
    def __init__(self, sbuf, far_in, main_in, ss, rs, half):
        x = lax.axis_index("blk")
        self.hi, self.lo, self.far = (x + 1) % 4, (x + 3) % 4, (x + 2) % 4
        self.sbuf, self.far_in, self.main_in = sbuf, far_in, main_in
        right, left = x_dev(x, 1), x_dev(x, 3)
        self.a, self.b = pl.ds(0, half), pl.ds(half, half)
        a, b = self.a, self.b
        self.c = [
            rcopy(sbuf.at[self.far, a], far_in.at[0], ss(0), rs(0), right),
            rcopy(sbuf.at[self.far, b], far_in.at[1], ss(1), rs(1), left),
            rcopy(sbuf.at[self.hi, b], main_in.at[0, b], ss(2), rs(2), right),
            rcopy(sbuf.at[self.lo, a], main_in.at[1, a], ss(3), rs(3), left),
            rcopy(sbuf.at[self.hi, a], main_in.at[0, a], ss(4), rs(4), right),
            rcopy(sbuf.at[self.lo, b], main_in.at[1, b], ss(5), rs(5), left),
        ]

    def start(self):
        for k in range(4):
            self.c[k].start()

    def relay(self):
        self.c[0].wait_recv()
        s = self.sbuf[self.hi, self.a].astype(F32) + self.far_in[0].astype(F32)
        self.sbuf[self.hi, self.a] = s.astype(BF)
        self.c[1].wait_recv()
        s = self.sbuf[self.lo, self.b].astype(F32) + self.far_in[1].astype(F32)
        self.sbuf[self.lo, self.b] = s.astype(BF)
        self.c[4].start()
        self.c[5].start()

    def wait(self):
        for k in range(2, 6):
            self.c[k].wait_recv()

    def finish(self):
        for d in self.c:
            d.wait_send()


def gelu(v):
    return 0.5 * v * (1.0 + lax.erf(v * (1.0 / math.sqrt(2.0))))


def view_rows(tiles):
    first = 16 * ((tiles + 1) // 2)
    halves = ((0, first), (first, 16 * tiles - first))

    def view(r, h, q):
        start, size = halves[h]
        if q is None:
            return r.at[pl.ds(start, size)]
        lead = 16 * ((size // 16 + 1) // 2)
        return r.at[pl.ds(start, lead)] if q == 0 else r.at[pl.ds(start + lead, size - lead)]

    return view


def k_layer(
    tok, wq, wout, gain1, bias1, qbias, seg, ob, gain2, bias2, fc1, b1, fc2, b2, wp, lo, wpg,
    pack, qb, wo4, toks, qkv, slots, wf, wof, hb, w1, w2, att, oh, segc, after, hid, own, mine,
    sbuf, far_in, main_in, lsem, rs, rr, ws, wr, as_, ar, xs, xr, *gs
):
    x, y, z, c = position()
    t = lax.axis_index("tok")
    depth = wq.shape[1]
    heads = wq.shape[2] // HD
    nq = 3 * heads
    no = wof.shape[1] // 128
    h2, attf = hb.at[0], hb.at[1]
    load = [
        pltpu.make_async_copy(fc1, w1, lsem.at[2]),
        pltpu.make_async_copy(fc2, w2, lsem.at[3]),
        pltpu.make_async_copy(wp, wpg.at[t], lsem.at[4]),
    ]
    meet(x_peers() + [x_dev(x, 2)] + tok_peers())
    wo_send = [rcopy(wout, wo4.at[x], ws.at[k], wr.at[k], x_dev(x, k + 1)) for k in range(3)]
    for d in wo_send:
        d.start()
    ring = RingGather(
        lambda i: tok.at[pl.ds(128 * i, 128)],
        lambda s, i: toks.at[s, pl.ds(128 * i, 128)],
        lambda k: rs.at[k],
        lambda k: rr.at[k],
    )
    ring.start()
    local = [pltpu.make_async_copy(tok, toks.at[x], lsem.at[0])]
    local[0].start()
    zero = jnp.zeros((depth, HPAD - HD), BF)
    for k in range(3):
        for h in range(heads):
            n = k * heads + h
            piece = wq[k, :, h * HD : h * HD + HD]
            pack[n * depth : n * depth + depth, :] = jnp.concatenate([piece, zero], axis=1)
            qb[:, n * HPAD : n * HPAD + HPAD] = jnp.concatenate(
                [qbias[k : k + 1, h * HD : h * HD + HD], jnp.zeros((1, HPAD - HD), F32)], axis=1
            )
    wo4[x] = wout[...]
    for d in wo_send:
        d.wait_recv()
    wide = jnp.concatenate([wo4[b] for b in range(4)], axis=1)
    for n in range(no):
        at = (nq + n) * depth
        pack[at : at + depth, :] = wide[:, 128 * n : 128 * n + 128]
    gath = TokGather(pack, slots, view_rows(pack.shape[0] // 16), *gs[:6])
    gath.start()
    for d in load:
        d.start()
    local.append(pltpu.make_async_copy(pack, slots.at[t], lsem.at[1]))
    local[1].start()
    norm_rows(tok, hb.at[x], gain1, bias1, 256)
    segr = seg[...].astype(F32)
    segc[...] = jnp.broadcast_to(segr, (128, segr.shape[1])).T

    def unpack(g, first, n, dst):
        for i in range(n):
            at = (first + i) * depth
            parts = [slots[4 * g + j, at : at + depth, :] for j in range(4)]
            rows = pl.ds(pl.multiple_of(g * 208, 16), 208)
            dst[rows, 128 * i : 128 * i + 128] = jnp.concatenate(parts, axis=0)

    def unpack_qkv(k):
        gath.wait_cross(0, k)
        yy = (y + gath.OFF[k]) % 4

        @pl.loop(0, 2)
        def _(p):
            unpack(2 * yy + p, 0, nq, wf)

    def unpack_out(p):
        @pl.loop(0, 4)
        def _(yy):
            unpack(2 * yy + p, nq, no, wof)

    def project(s):
        @pl.loop(0, wf.shape[1] // 256)
        def _(j):
            cols = pl.ds(pl.multiple_of(j * 256, 256), 256)
            v = jnp.dot(hb[s], wf[:, cols], preferred_element_type=F32) + qb[:, cols]
            v = v.astype(BF)
            rows = pl.ds(pl.multiple_of(s * 256, 256), 256)
            qkv[2 * j, rows, :] = v[:, :128]
            qkv[2 * j + 1, rows, :] = v[:, 128:]

    for h in range(2):
        gath.first_near(h)
    ring.relay()
    for h in range(2):
        gath.first_far(h)
    for i in range(4):
        for h in range(2):
            gath.second_near(h, i)
    for d in local:
        d.wait()
    unpack_qkv(0)
    ring.wait_near()
    for o in (1, 3):
        s = (x + o) % 4
        norm_rows(toks.at[s], hb.at[s], gain1, bias1, 256)
    unpack_qkv(1)
    unpack_qkv(2)
    for i in range(4):
        gath.second_far(0, i)
    unpack_qkv(3)

    @pl.loop(0, 3)
    def _(i):
        project((x + i + i // 2) % 4)

    for i in range(4):
        gath.second_far(1, i)
    ring.wait_far()
    far = (x + 2) % 4
    norm_rows(toks.at[far], hb.at[far], gain1, bias1, 256)
    project(far)
    scale = 1.0 / math.sqrt(HD)
    half = att.shape[2] // 2

    def attend(r):
        @pl.loop(0, 2)
        def _(sub):
            rows = pl.ds(pl.multiple_of(r * 256 + sub * 128, 128), 128)
            same = segc[rows, 0:1] == segr
            for h in range(heads):
                s = lax.dot_general(
                    qkv[h, rows, :], qkv[heads + h], (((1,), (1,)), ((), ())), preferred_element_type=F32
                )
                p = jnp.where(same, jnp.exp(s * scale), 0.0)
                total = jnp.sum(p, axis=-1, keepdims=True)
                o = jnp.dot(p.astype(BF), qkv[2 * heads + h], preferred_element_type=F32) / total
                oh[h, pl.ds(pl.multiple_of(sub * 128, 128), 128), :] = o.astype(BF)

        pack_rows(jnp.concatenate([oh[h][:, :HD] for h in range(heads)], axis=1), att.at[x, r])

    def gather_ring(r):
        def part(s, i):
            return att.at[s, r, pl.ds(half * i, half)]

        return RingGather(lambda i: part(x, i), part, lambda k: as_.at[r, k], lambda k: ar.at[r, k])

    def reduce_ring(r):
        return RingReduce(
            sbuf.at[r],
            far_in.at[r],
            main_in.at[r],
            lambda k: xs.at[r, k],
            lambda k: xr.at[r, k],
            half,
        )

    attend(0)
    gather_ring(0).start()
    attend(1)
    gather_ring(0).relay()
    gather_ring(1).start()
    attend(2)
    gather_ring(1).relay()
    gather_ring(2).start()
    attend(3)
    gather_ring(2).relay()
    gather_ring(3).start()
    for k in range(4):
        gath.wait_cross(1, k)
    for p in range(2):
        unpack_out(p)
    merg = TokGather(wp, wpg, view_rows(wp.shape[0] // 16), *gs[6:])
    merg.start()
    tiles = [(n, min(256, 1664 - n)) for n in range(0, 1664, 256)]
    @pl.loop(0, 6)
    def _(r):
        @pl.when(r < 4)
        def _():
            rg = gather_ring(r)
            rg.wait_near()
            rg.wait_far()
            attf[...] = jnp.concatenate([unpack_rows(att.at[b, r]) for b in range(4)], axis=1)
            for n, w in tiles:
                acc = lax.dot_general(
                    attf[...], wof[n : n + w, :], (((1,), (1,)), ((), ())), preferred_element_type=F32
                )
                after[:, n : n + w] = acc + toks[r, :, n : n + w].astype(F32) + ob[n : n + w]

            @pl.when(r == 0)
            def _():
                gather_ring(3).relay()
                load[0].wait()

            @pl.when(r > 0)
            def _():
                reduce_ring(r - 1).relay()

            @pl.when(r == 1)
            def _():
                for h in range(2):
                    merg.first_near(h)
                for h in range(2):
                    merg.first_far(h)

            @pl.when(r == 2)
            def _():
                for i in range(4):
                    for h in range(2):
                        merg.second_near(h, i)

            @pl.when(r == 3)
            def _():
                for i in range(4):
                    for h in range(2):
                        merg.second_far(h, i)

            norm_rows(after, h2, gain2, bias2, 256)
            for j in range(4):

                @pl.when(x == j)
                def _():
                    pack_rows(after[:, 416 * j : 416 * j + 416] + b2[416 * j : 416 * j + 416], own.at[r])

            for j in range(8):
                cols = slice(256 * j, 256 * j + 256)
                v = jnp.dot(h2[...], w1[:, cols], preferred_element_type=F32) + b1[cols]
                hid[:, cols] = gelu(v).astype(BF)

            @pl.when(r == 0)
            def _():
                load[1].wait()

            for n, w in tiles:
                after[:, n : n + w] = jnp.dot(hid[...], w2[:, n : n + w], preferred_element_type=F32)
            for j in range(4):
                piece = after[:, 416 * j : 416 * j + 416]
                pack_rows(piece.astype(BF), sbuf.at[r, j])

                @pl.when(x == j)
                def _():
                    pack_rows(piece, mine)
                    own[r] += mine[...]

            reduce_ring(r).start()

        @pl.when(r == 4)
        def _():
            reduce_ring(3).relay()

        @pl.when(r > 1)
        def _():
            q = r - 2
            rg = reduce_ring(q)
            rg.wait()
            total = own[q] + main_in[q, 0].astype(F32) + main_in[q, 1].astype(F32)
            lo[q] = total.astype(BF)
            rg.finish()
            gather_ring(q).finish()

    load[2].wait()
    for h in range(2):
        for k in range(4):
            merg.wait_cross(h, k)
    for d in wo_send:
        d.wait_send()
    ring.finish()
    gath.finish()
    merg.finish()


def column(rows):
    n, m = rows.shape
    return jnp.concatenate([rows, jnp.zeros((128 - n, m), F32)], axis=0).T


def k_merge(
    lo, gain3, bias3, mi, seg, owners, wpg_h, pb, out,
    wpg, rows_f, fin, gb, sbuf, own, far_in, main_in, st, placed, obuf, lsem, ss, sr, xs, xr, ts, tr
):
    x, y, z, c = position()
    t = lax.axis_index("tok")
    n_tok = out.shape[0]
    slot = out.shape[1]
    merged = mi.shape[1]
    n_loc = wpg.shape[2]
    load = pltpu.make_async_copy(wpg_h, wpg, lsem.at[0])
    load.start()
    bar = pltpu.get_barrier_semaphore()

    @pl.loop(1, n_tok)
    def _(i):
        pl.semaphore_signal(bar, inc=1, device_id={"tok": (t + i) % n_tok}, device_id_type=MESH_ID)

    @pl.loop(1, 4)
    def _(i):
        pl.semaphore_signal(bar, inc=1, device_id=x_dev(x, i), device_id_type=MESH_ID)

    @pl.loop(0, 4)
    def _(i):
        rows = pl.ds(pl.multiple_of(i * 256, 256), 256)
        v = unpack_rows(lo.at[i]).astype(F32)
        rows_f[rows, :] = v
        mean = jnp.mean(v, axis=-1, keepdims=True)
        d = v - mean
        m2 = jnp.sum(d * d, axis=-1, keepdims=True)
        lane = lax.broadcasted_iota(jnp.int32, (256, 128), 1)
        both = jnp.where(lane == 0, mean, jnp.where(lane == 1, m2, 0.0))
        st[x, :, rows] = both.T[:8]

    pl.semaphore_wait(bar, n_tok + 2)
    sends = [rcopy(st.at[x], st.at[x], ss.at[k], sr.at[k], x_dev(x, k + 1)) for k in range(3)]
    for d in sends:
        d.start()
    for j in range(4):

        @pl.when(x == j)
        def _():
            gb[0:1, :] = gain3[n_loc * j : n_loc * j + n_loc].reshape(1, n_loc)
            gb[1:2, :] = bias3[n_loc * j : n_loc * j + n_loc].reshape(1, n_loc)

    idx = column(mi[...].astype(F32))
    toks = lax.broadcasted_iota(jnp.int32, (merged, 1024), 1).astype(F32)
    seg_of = jnp.sum(jnp.where(idx[:, 0:1] == toks, seg[...].astype(F32), 0.0), axis=1, keepdims=True)
    names = lax.broadcasted_iota(jnp.int32, (merged, n_tok), 1).astype(F32)
    owner = jnp.sum(jnp.where(seg_of == names, owners[...].astype(F32), 0.0), axis=1, keepdims=True)
    mine = (owner == names).astype(F32)
    below = lax.broadcasted_iota(jnp.int32, (merged, merged), 1) < lax.broadcasted_iota(
        jnp.int32, (merged, merged), 0
    )
    before = jnp.dot(
        jnp.where(below, 1.0, 0.0).astype(BF), mine.astype(BF), preferred_element_type=F32
    )
    rank = jnp.sum(before * mine, axis=1, keepdims=True)
    target = jnp.broadcast_to(owner * slot + rank, (merged, 128)).T[0:1]
    spots = lax.broadcasted_iota(jnp.int32, (n_tok * slot, merged), 0).astype(F32)
    placed[...] = jnp.where(spots == target, 1.0, 0.0).astype(BF)
    for d in sends:
        d.wait_recv()
    means = [st[s, 0:1, :] for s in range(4)]
    mean = 0.25 * (means[0] + means[1] + means[2] + means[3])
    m2 = st[0, 1:2, :] + st[1, 1:2, :] + st[2, 1:2, :] + st[3, 1:2, :]
    for s in range(4):
        d = means[s] - mean
        m2 = m2 + n_loc * (d * d)
    rstd = lax.rsqrt(m2 * (1.0 / (4 * n_loc)) + EPS)
    for i in range(8):
        sl = slice(128 * i, 128 * i + 128)
        row = lax.broadcasted_iota(jnp.int32, (128, 128), 0)
        cols = jnp.where(row == 0, mean[:, sl], jnp.where(row == 1, rstd[:, sl], 0.0)).T
        v = rows_f[sl, :]
        fin[sl, :] = ((v - cols[:, 0:1]) * cols[:, 1:2] * gb[0:1, :] + gb[1:2, :]).astype(BF)
    load.wait()
    got = []
    for k in range(4):
        pick = jnp.where(idx[:, k : k + 1] == toks, 1.0, 0.0).astype(BF)
        got.append(jnp.dot(pick, fin[...], preferred_element_type=F32).astype(BF))
    for j in range(4):
        acc = jnp.dot(got[0], wpg[j], preferred_element_type=F32)
        for k in range(1, 4):
            acc += jnp.dot(got[k], wpg[k * 4 + j], preferred_element_type=F32)
        pack_rows(acc, own.at[j])
        sbuf[j] = own[j].astype(BF)
    rg = RingReduce(sbuf, far_in, main_in, lambda k: xs.at[k], lambda k: xr.at[k], sbuf.shape[1] // 2)
    rg.start()
    rg.relay()
    rg.wait()
    own[x] += main_in[0].astype(F32) + main_in[1].astype(F32)
    total = unpack_rows(own.at[x]) + pb[...]
    going = jnp.dot(placed[...], total.astype(BF), preferred_element_type=F32).astype(BF)
    obuf[...] = going.reshape(n_tok, slot, n_loc)

    def slot_copy(i):
        to = (t + i) % n_tok
        return rcopy(obuf.at[to], out.at[t], ts.at[i], tr.at[i], {"tok": to})

    @pl.loop(1, n_tok)
    def _(i):
        slot_copy(i).start()

    keep = pltpu.make_async_copy(obuf.at[t], out.at[t], lsem.at[1])
    keep.start()
    rg.finish()
    for d in sends:
        d.wait_send()
    keep.wait()

    @pl.loop(1, n_tok)
    def _(i):
        slot_copy(i).wait()


def kernel_call(body, name, cid, ins, outs, out_specs, scratch, args):
    return pl.pallas_call(
        body,
        name=name,
        out_shape=outs,
        in_specs=ins,
        out_specs=out_specs,
        scratch_shapes=scratch,
        compiler_params=pltpu.CompilerParams(
            collective_id=cid, has_side_effects=True, vmem_limit_bytes=VLIM
        ),
    )(*args)


def sds(shape, dtype):
    return jax.ShapeDtypeStruct(shape, dtype)


DMA = pltpu.SemaphoreType.DMA


def body(
    tokens,
    segment_ids,
    merge_index,
    segment_owner,
    ln1_gain,
    ln1_bias,
    w_qkv,
    qkv_bias,
    w_out,
    out_bias,
    ln2_gain,
    ln2_bias,
    w_fc1,
    fc1_bias,
    w_fc2,
    fc2_bias,
    ln3_gain,
    ln3_bias,
    w_proj,
    proj_bias,
):
    tok = tokens[0]
    width = tok.shape[1]
    part_w = w_qkv.shape[2]
    depth = w_qkv.shape[1]
    heads = part_w // HD
    cols = 3 * heads * HPAD
    blocks = (cols + width) // 128
    packed = 16 * (-(-blocks * depth // 16))
    hidden = w_fc1.shape[1]
    flat = 256 * part_w // 128
    perm = []
    for bx in range(4):
        for t in range(32):
            ty, tz, tc = t // 8, (t // 2) % 4, t % 2
            perm.append((bx * 32 + t, tz * 32 + (ty * 4 + bx) * 2 + tc))
    wp = lax.ppermute(w_proj, ("blk", "tok"), perm)
    lo, wpg = kernel_call(
        k_layer,
        "layer",
        1,
        [VM] * 10 + [ANY, VM, ANY, VM, VM],
        [sds((4, flat, 128), BF), sds((32, 208, part_w), BF)],
        [VM, ANY],
        [
            pltpu.VMEM((packed, 128), BF),
            pltpu.VMEM((1, cols), F32),
            pltpu.VMEM((4, depth, part_w), BF),
            pltpu.VMEM((4, 256, width), BF),
            pltpu.VMEM((3 * heads, 1024, HPAD), BF),
            pltpu.VMEM((32, packed, 128), BF),
            pltpu.VMEM((width, cols), BF),
            pltpu.VMEM((width, width), BF),
            pltpu.VMEM((4, 256, width), BF),
            pltpu.VMEM((width, hidden), BF),
            pltpu.VMEM((hidden, width), BF),
            pltpu.VMEM((4, 4, flat, 128), BF),
            pltpu.VMEM((heads, 256, HPAD), BF),
            pltpu.VMEM((1024, 128), F32),
            pltpu.VMEM((256, width), F32),
            pltpu.VMEM((256, hidden), BF),
            pltpu.VMEM((4, flat, 128), F32),
            pltpu.VMEM((flat, 128), F32),
            pltpu.VMEM((4, 4, flat, 128), BF),
            pltpu.VMEM((4, 2, flat // 2, 128), BF),
            pltpu.VMEM((4, 2, flat, 128), BF),
            DMA((5,)),
            DMA((6,)),
            DMA((6,)),
            DMA((3,)),
            DMA((3,)),
            DMA((4, 6)),
            DMA((4, 6)),
            DMA((4, 6)),
            DMA((4, 6)),
        ]
        + TOK_SEMS * 2,
        (
            tok, w_qkv, w_out.T, ln1_gain, ln1_bias, qkv_bias, segment_ids, out_bias, ln2_gain,
            ln2_bias, w_fc1, fc1_bias, w_fc2, fc2_bias, wp,
        ),
    )
    merged_count = merge_index.shape[1]
    n_tok = lax.axis_size("tok")
    slot = 2 * merged_count // n_tok
    arrived = kernel_call(
        k_merge,
        "merge",
        3,
        [VM] * 6 + [ANY, VM],
        [sds((n_tok, slot, part_w), BF)],
        [VM],
        [
            pltpu.VMEM((16, part_w, part_w), BF),
            pltpu.VMEM((1024, part_w), F32),
            pltpu.VMEM((1024, part_w), BF),
            pltpu.VMEM((2, part_w), F32),
            pltpu.VMEM((4, flat, 128), BF),
            pltpu.VMEM((4, flat, 128), F32),
            pltpu.VMEM((2, flat // 2, 128), BF),
            pltpu.VMEM((2, flat, 128), BF),
            pltpu.VMEM((4, 8, 1024), F32),
            pltpu.VMEM((n_tok * slot, merged_count), BF),
            pltpu.VMEM((n_tok, slot, part_w), BF),
            DMA((2,)),
            DMA((3,)),
            DMA((3,)),
            DMA((6,)),
            DMA((6,)),
            DMA((n_tok,)),
            DMA((n_tok,)),
        ],
        (
            lo,
            ln3_gain,
            ln3_bias,
            merge_index[0].T,
            segment_ids,
            segment_owner,
            wpg.reshape(16, part_w, part_w),
            proj_bias,
        ),
    )[0]
    return arrived[None]


def solution(mesh):
    placed = (
        P("tok", "blk", None),
        P("tok", None),
        P("tok", None, None),
        P("tok", None),
        P(),
        P(),
        P(None, "tok", "blk"),
        P(None, "blk"),
        P("blk", "tok"),
        P(),
        P(),
        P(),
        P(None, "blk"),
        P("blk"),
        P("blk", None),
        P(),
        P(),
        P(),
        P("tok", "blk"),
        P("blk"),
    )
    return jax.shard_map(
        body, mesh=mesh, in_specs=placed, out_specs=P("tok", None, None, "blk"), check_vma=False
    )
```

```python
import math

import jax
import jax.numpy as jnp
from jax import lax
from jax.experimental import pallas as pl
from jax.experimental.pallas import tpu as pltpu
from jax.sharding import PartitionSpec as P

HD = 104
HPAD = 128
EPS = 1e-06
BF = jnp.bfloat16
F32 = jnp.float32
MESH_ID = pl.DeviceIdType.MESH
VLIM = 65000 * 1024
VM = pl.BlockSpec(memory_space=pltpu.VMEM)
ANY = pl.BlockSpec(memory_space=pl.ANY)


def position():
    x = lax.axis_index("blk")
    t = lax.axis_index("tok")
    return x, t // 8, (t // 2) % 4, t % 2


def tok_of(y, z, c):
    return ((y % 4) * 4 + z % 4) * 2 + c


def rcopy(src, dst, ssem, rsem, dev):
    return pltpu.make_async_remote_copy(
        src_ref=src, dst_ref=dst, send_sem=ssem, recv_sem=rsem, device_id=dev, device_id_type=MESH_ID
    )


def x_dev(x, off):
    return {"blk": (x + off) % 4}


def meet(peers):
    bar = pltpu.get_barrier_semaphore()
    for dev in peers:
        pl.semaphore_signal(bar, inc=1, device_id=dev, device_id_type=MESH_ID)
    pl.semaphore_wait(bar, len(peers))


def x_peers():
    x, y, z, c = position()
    return [x_dev(x, 1), x_dev(x, 3)]


def tok_peers():
    x, y, z, c = position()
    return [
        {"tok": tok_of(y, z + 1, c)},
        {"tok": tok_of(y, z + 3, c)},
        {"tok": tok_of(y + 1, z, c)},
        {"tok": tok_of(y + 3, z, c)},
        {"tok": tok_of(y, z, 1 - c)},
    ]


class RingGather:
    def __init__(self, own, half, ss, rs):
        x = lax.axis_index("blk")
        right, left = x_dev(x, 1), x_dev(x, 3)

        def send(view, src, i, k, dev):
            return rcopy(view, half(src, i), ss(k), rs(k), dev)

        me, lo, hi = x, (x + 3) % 4, (x + 1) % 4
        self.c = [
            send(own(0), me, 0, 0, right),
            send(own(1), me, 1, 1, right),
            send(own(1), me, 1, 2, left),
            send(own(0), me, 0, 3, left),
            send(half(lo, 0), lo, 0, 4, right),
            send(half(hi, 1), hi, 1, 5, left),
        ]

    def start(self):
        for k in (0, 2, 1, 3):
            self.c[k].start()

    def relay(self):
        self.c[0].wait_recv()
        self.c[4].start()
        self.c[2].wait_recv()
        self.c[5].start()

    def wait_near(self):
        self.c[1].wait_recv()
        self.c[3].wait_recv()

    def wait_far(self):
        self.c[4].wait_recv()
        self.c[5].wait_recv()

    def finish(self):
        for c in self.c:
            c.wait_send()


class TokGather:
    OFF = (0, 3, 1, 2)

    def __init__(self, own, slots, view, fs, fr, ss, sr, cs, cr):
        x, y, z, c = position()
        self.first, self.second, self.cross = [], [], []
        sib = {"tok": tok_of(y, z, 1 - c)}
        for h in range(2):

            def tok(d1, d2, h=h):
                return tok_of(y + d2, z + d1, c) if h == 0 else tok_of(y + d1, z + d2, c)

            def slot(d1, d2, tok=tok):
                return slots.at[tok(d1, d2)]

            def half(r, h=h):
                return view(r, h, None)

            def quarter(r, q, h=h):
                return view(r, h, q)

            me = slot(0, 0)
            p1, m1 = {"tok": tok(1, 0)}, {"tok": tok(3, 0)}
            p2, m2 = {"tok": tok(0, 1)}, {"tok": tok(0, 3)}
            self.first.append(
                [
                    rcopy(half(own), half(me), fs.at[h, 0], fr.at[h, 0], p1),
                    rcopy(half(own), half(me), fs.at[h, 1], fr.at[h, 1], m1),
                    rcopy(quarter(slot(3, 0), 0), quarter(slot(3, 0), 0), fs.at[h, 2], fr.at[h, 2], p1),
                    rcopy(quarter(slot(1, 0), 1), quarter(slot(1, 0), 1), fs.at[h, 3], fr.at[h, 3], m1),
                ]
            )
            second = []
            for i, o in enumerate(self.OFF):
                src = half(own) if i == 0 else half(slot(o, 0))
                here, up, dn = half(slot(o, 0)), slot(o, 3), slot(o, 1)
                second.append(
                    [
                        rcopy(src, here, ss.at[h, i, 0], sr.at[h, i, 0], p2),
                        rcopy(src, here, ss.at[h, i, 1], sr.at[h, i, 1], m2),
                        rcopy(quarter(up, 0), quarter(up, 0), ss.at[h, i, 2], sr.at[h, i, 2], p2),
                        rcopy(quarter(dn, 1), quarter(dn, 1), ss.at[h, i, 3], sr.at[h, i, 3], m2),
                    ]
                )
            self.second.append(second)
            cross = []
            for k in range(4):
                row = []
                for i, o in enumerate(self.OFF):
                    dst = half(slot(o, self.OFF[k]))
                    src = half(own) if (i == 0 and k == 0) else dst
                    row.append(rcopy(src, dst, cs.at[h, k, i], cr.at[h, k, i], sib))
                cross.append(row)
            self.cross.append(cross)

    def start(self):
        for h in range(2):
            self.first[h][0].start()
            self.first[h][1].start()
        for h in range(2):
            self._fan(h, 0)

    def _fan(self, h, i):
        self.second[h][i][0].start()
        self.second[h][i][1].start()
        self.cross[h][0][i].start()

    def first_near(self, h):
        f = self.first[h]
        f[0].wait_recv()
        f[2].start()
        self._fan(h, 1)
        f[1].wait_recv()
        f[3].start()
        self._fan(h, 2)

    def first_far(self, h):
        self.first[h][2].wait_recv()
        self.first[h][3].wait_recv()
        self._fan(h, 3)

    def second_near(self, h, i):
        f = self.second[h][i]
        f[0].wait_recv()
        f[2].start()
        self.cross[h][1][i].start()
        f[1].wait_recv()
        f[3].start()
        self.cross[h][2][i].start()

    def second_far(self, h, i):
        f = self.second[h][i]
        f[2].wait_recv()
        f[3].wait_recv()
        self.cross[h][3][i].start()

    def wait_cross(self, h, k):
        for d in self.cross[h][k]:
            d.wait_recv()

    def _all(self):
        for h in range(2):
            for row in self.cross[h]:
                yield from row

    def finish(self):
        for h in range(2):
            for d in self.first[h]:
                d.wait_send()
            for row in self.second[h]:
                for d in row:
                    d.wait_send()
        for d in self._all():
            d.wait_send()


TOK_SEMS = [pltpu.SemaphoreType.DMA((2, 4))] * 2 + [pltpu.SemaphoreType.DMA((2, 4, 4))] * 4


def norm_rows(src, dst, gain, bias, rows, step=32):
    @pl.loop(0, rows // step)
    def _(i):
        at = pl.ds(pl.multiple_of(i * step, step), step)
        v = src[at, :].astype(F32)
        mean = jnp.mean(v, axis=-1, keepdims=True)
        center = v - mean
        spread = jnp.mean(center * center, axis=-1, keepdims=True)
        dst[at, :] = (center * lax.rsqrt(spread + EPS) * gain[...] + bias[...]).astype(dst.dtype)


def pack_rows(v, dst):
    rows, width = v.shape
    full = width // 128
    rest = width - 128 * full
    for i in range(full):
        dst[rows * i : rows * i + rows] = v[:, 128 * i : 128 * i + 128]
    n = 128 // rest
    part = rows // n
    tail = [v[part * q : part * q + part, 128 * full :] for q in range(n)]
    dst[rows * full : rows * full + part] = jnp.concatenate(tail, axis=1)


def unpack_rows(src, rows=256, rest=32):
    n = 128 // rest
    part = rows // n
    full = (src.shape[0] - part) // rows
    last = src[rows * full : rows * full + part]
    tail = jnp.concatenate([last[:, rest * q : rest * q + rest] for q in range(n)], axis=0)
    return jnp.concatenate([src[rows * i : rows * i + rows] for i in range(full)] + [tail], axis=1)


class RingReduce:
    def __init__(self, sbuf, far_in, main_in, ss, rs, half):
        x = lax.axis_index("blk")
        self.hi, self.lo, self.far = (x + 1) % 4, (x + 3) % 4, (x + 2) % 4
        self.sbuf, self.far_in, self.main_in = sbuf, far_in, main_in
        right, left = x_dev(x, 1), x_dev(x, 3)
        self.a, self.b = pl.ds(0, half), pl.ds(half, half)
        a, b = self.a, self.b
        self.c = [
            rcopy(sbuf.at[self.far, a], far_in.at[0], ss(0), rs(0), right),
            rcopy(sbuf.at[self.far, b], far_in.at[1], ss(1), rs(1), left),
            rcopy(sbuf.at[self.hi, b], main_in.at[0, b], ss(2), rs(2), right),
            rcopy(sbuf.at[self.lo, a], main_in.at[1, a], ss(3), rs(3), left),
            rcopy(sbuf.at[self.hi, a], main_in.at[0, a], ss(4), rs(4), right),
            rcopy(sbuf.at[self.lo, b], main_in.at[1, b], ss(5), rs(5), left),
        ]

    def start(self):
        for k in range(4):
            self.c[k].start()

    def relay(self):
        self.c[0].wait_recv()
        s = self.sbuf[self.hi, self.a].astype(F32) + self.far_in[0].astype(F32)
        self.sbuf[self.hi, self.a] = s.astype(BF)
        self.c[1].wait_recv()
        s = self.sbuf[self.lo, self.b].astype(F32) + self.far_in[1].astype(F32)
        self.sbuf[self.lo, self.b] = s.astype(BF)
        self.c[4].start()
        self.c[5].start()

    def wait(self):
        for k in range(2, 6):
            self.c[k].wait_recv()

    def finish(self):
        for d in self.c:
            d.wait_send()


def gelu(v):
    return 0.5 * v * (1.0 + lax.erf(v * (1.0 / math.sqrt(2.0))))


def view_rows(tiles):
    first = 16 * ((tiles + 1) // 2)
    halves = ((0, first), (first, 16 * tiles - first))

    def view(r, h, q):
        start, size = halves[h]
        if q is None:
            return r.at[pl.ds(start, size)]
        lead = 16 * ((size // 16 + 1) // 2)
        return r.at[pl.ds(start, lead)] if q == 0 else r.at[pl.ds(start + lead, size - lead)]

    return view


def k_layer(
    tok, wq, wout, gain1, bias1, qbias, seg, ob, gain2, bias2, fc1, b1, fc2, b2, wp, lo, wpg,
    pack, packo, vec, qb, wo4, toks, qkv, slots, oslots, wf, wof, hb, w1, w2, att, oh, segc, after, hid, own, mine,
    sbuf, far_in, main_in, lsem, rs, rr, ws, wr, as_, ar, xs, xr, *gs
):
    x, y, z, c = position()
    t = lax.axis_index("tok")
    depth = wq.shape[1]
    heads = wq.shape[2] // HD
    nq = 3 * heads
    no = wof.shape[1] // 128
    h2, attf = hb.at[0], hb.at[1]
    width = tok.shape[1]
    load = [
        pltpu.make_async_copy(fc1, w1, lsem.at[2]),
        pltpu.make_async_copy(fc2, w2, lsem.at[3]),
        pltpu.make_async_copy(wp, wpg.at[t], lsem.at[4]),
    ]
    meet(x_peers() + [x_dev(x, 2)] + tok_peers())
    wo_send = [rcopy(wout, wo4.at[x], ws.at[k], wr.at[k], x_dev(x, k + 1)) for k in range(3)]
    for d in wo_send:
        d.start()
    ring = RingGather(
        lambda i: tok.at[pl.ds(128 * i, 128)],
        lambda s, i: toks.at[s, pl.ds(128 * i, 128)],
        lambda k: rs.at[k],
        lambda k: rr.at[k],
    )
    ring.start()
    for i, v in enumerate((gain1, bias1, gain2, bias2, ob, b2, b1)):
        vec[i : i + 1, : v.shape[0]] = v[...].reshape(1, v.shape[0])
    gain1, bias1, gain2, bias2, ob, b2 = [vec.at[i : i + 1, :width] for i in range(6)]
    b1 = vec.at[6:7]
    local = [pltpu.make_async_copy(tok, toks.at[x], lsem.at[0])]
    local[0].start()
    zero = jnp.zeros((depth, HPAD - HD), BF)
    for k in range(3):
        for h in range(heads):
            n = k * heads + h
            piece = wq[k, :, h * HD : h * HD + HD]
            pack[n * depth : n * depth + depth, :] = jnp.concatenate([piece, zero], axis=1)
            qb[:, n * HPAD : n * HPAD + HPAD] = jnp.concatenate(
                [qbias[k : k + 1, h * HD : h * HD + HD], jnp.zeros((1, HPAD - HD), F32)], axis=1
            )
    gath = TokGather(pack, slots, view_rows(pack.shape[0] // 16), *gs[:6])
    gath.start()
    wo4[x] = wout[...]
    for d in wo_send:
        d.wait_recv()
    wide = jnp.concatenate([wo4[b] for b in range(4)], axis=1)
    for n in range(no):
        packo[n * depth : n * depth + depth, :] = wide[:, 128 * n : 128 * n + 128]
    gout = TokGather(packo, oslots, view_rows(packo.shape[0] // 16), *gs[6:12])
    local.append(pltpu.make_async_copy(pack, slots.at[t], lsem.at[1]))
    local[1].start()
    for d in load:
        d.start()
    norm_rows(tok, hb.at[x], gain1, bias1, 256)
    segr = seg[...].astype(F32)
    segc[...] = jnp.broadcast_to(segr, (128, segr.shape[1])).T

    def unpack(g, src, n, dst):
        for i in range(n):
            at = i * depth
            parts = [src[4 * g + j, at : at + depth, :] for j in range(4)]
            rows = pl.ds(pl.multiple_of(g * 208, 16), 208)
            dst[rows, 128 * i : 128 * i + 128] = jnp.concatenate(parts, axis=0)

    def unpack_all(gat, src, n, dst):
        for h in range(2):
            for k in range(4):
                gat.wait_cross(h, k)

        @pl.loop(0, 8)
        def _(g):
            unpack(g, src, n, dst)

    def project(s):
        @pl.loop(0, wf.shape[1] // 256)
        def _(j):
            cols = pl.ds(pl.multiple_of(j * 256, 256), 256)
            v = jnp.dot(hb[s], wf[:, cols], preferred_element_type=F32) + qb[:, cols]
            v = v.astype(BF)
            rows = pl.ds(pl.multiple_of(s * 256, 256), 256)
            qkv[2 * j, rows, :] = v[:, :128]
            qkv[2 * j + 1, rows, :] = v[:, 128:]

    for h in range(2):
        gath.first_near(h)
    for h in range(2):
        gath.first_far(h)
    for i in range(2):
        for h in range(2):
            gath.second_near(h, i)
    ring.relay()
    for i in range(2, 4):
        for h in range(2):
            gath.second_near(h, i)
    gout.start()
    local.append(pltpu.make_async_copy(packo, oslots.at[t], lsem.at[5]))
    local[2].start()
    for i in range(4):
        for h in range(2):
            gath.second_far(h, i)
    for d in local:
        d.wait()
    ring.wait_near()
    for o in (1, 3):
        s = (x + o) % 4
        norm_rows(toks.at[s], hb.at[s], gain1, bias1, 256)
    for h in range(2):
        gout.first_near(h)
    unpack_all(gath, slots, nq, wf)
    for h in range(2):
        gout.first_far(h)

    @pl.loop(0, 3)
    def _(i):
        project((x + i + i // 2) % 4)

    for i in range(4):
        for h in range(2):
            gout.second_near(h, i)
    ring.wait_far()
    far = (x + 2) % 4
    norm_rows(toks.at[far], hb.at[far], gain1, bias1, 256)
    project(far)
    scale = 1.0 / math.sqrt(HD)
    half = att.shape[2] // 2

    def attend(r):
        @pl.loop(0, 2)
        def _(sub):
            rows = pl.ds(pl.multiple_of(r * 256 + sub * 128, 128), 128)
            same = segc[rows, 0:1] == segr
            for h in range(heads):
                s = lax.dot_general(
                    qkv[h, rows, :], qkv[heads + h], (((1,), (1,)), ((), ())), preferred_element_type=F32
                )
                p = jnp.where(same, jnp.exp(s * scale), 0.0)
                total = jnp.sum(p, axis=-1, keepdims=True)
                o = jnp.dot(p.astype(BF), qkv[2 * heads + h], preferred_element_type=F32) / total
                oh[h, pl.ds(pl.multiple_of(sub * 128, 128), 128), :] = o.astype(BF)

        pack_rows(jnp.concatenate([oh[h][:, :HD] for h in range(heads)], axis=1), att.at[x, r])

    def gather_ring(r):
        def part(s, i):
            return att.at[s, r, pl.ds(half * i, half)]

        return RingGather(lambda i: part(x, i), part, lambda k: as_.at[r, k], lambda k: ar.at[r, k])

    def reduce_ring(r):
        return RingReduce(
            sbuf.at[r],
            far_in.at[r],
            main_in.at[r],
            lambda k: xs.at[r, k],
            lambda k: xr.at[r, k],
            half,
        )

    attend(0)
    gather_ring(0).start()
    for i in range(4):
        for h in range(2):
            gout.second_far(h, i)
    attend(1)
    gather_ring(0).relay()
    gather_ring(1).start()
    attend(2)
    gather_ring(1).relay()
    gather_ring(2).start()
    attend(3)
    gather_ring(2).relay()
    gather_ring(3).start()
    unpack_all(gout, oslots, no, wof)
    merg = TokGather(wp, wpg, view_rows(wp.shape[0] // 16), *gs[12:])
    merg.start()
    tiles = [(n, min(256, 1664 - n)) for n in range(0, 1664, 256)]
    @pl.loop(0, 6)
    def _(r):
        @pl.when(r < 4)
        def _():
            rg = gather_ring(r)
            rg.wait_near()
            rg.wait_far()
            attf[...] = jnp.concatenate([unpack_rows(att.at[b, r]) for b in range(4)], axis=1)
            for n, w in tiles:
                acc = lax.dot_general(
                    attf[...], wof[n : n + w, :], (((1,), (1,)), ((), ())), preferred_element_type=F32
                )
                after[:, n : n + w] = acc + toks[r, :, n : n + w].astype(F32) + ob[:, n : n + w]

            @pl.when(r == 0)
            def _():
                gather_ring(3).relay()
                load[0].wait()

            @pl.when(r > 0)
            def _():
                reduce_ring(r - 1).relay()

            @pl.when(r == 1)
            def _():
                for h in range(2):
                    merg.first_near(h)
                for h in range(2):
                    merg.first_far(h)

            @pl.when(r == 2)
            def _():
                for i in range(4):
                    for h in range(2):
                        merg.second_near(h, i)

            @pl.when(r == 3)
            def _():
                for i in range(4):
                    for h in range(2):
                        merg.second_far(h, i)

            norm_rows(after, h2, gain2, bias2, 256)
            for j in range(4):

                @pl.when(x == j)
                def _():
                    pack_rows(after[:, 416 * j : 416 * j + 416] + b2[:, 416 * j : 416 * j + 416], own.at[r])

            for j in range(8):
                cols = slice(256 * j, 256 * j + 256)
                v = jnp.dot(h2[...], w1[:, cols], preferred_element_type=F32) + b1[:, cols]
                hid[:, cols] = gelu(v).astype(BF)

            @pl.when(r == 0)
            def _():
                load[1].wait()

            for n, w in tiles:
                after[:, n : n + w] = jnp.dot(hid[...], w2[:, n : n + w], preferred_element_type=F32)
            for j in range(4):
                piece = after[:, 416 * j : 416 * j + 416]
                pack_rows(piece.astype(BF), sbuf.at[r, j])

                @pl.when(x == j)
                def _():
                    pack_rows(piece, mine)
                    own[r] += mine[...]

            reduce_ring(r).start()

        @pl.when(r == 4)
        def _():
            reduce_ring(3).relay()

        @pl.when(r > 1)
        def _():
            q = r - 2
            rg = reduce_ring(q)
            rg.wait()
            total = own[q] + main_in[q, 0].astype(F32) + main_in[q, 1].astype(F32)
            lo[q] = total.astype(BF)
            rg.finish()
            gather_ring(q).finish()

    load[2].wait()
    for h in range(2):
        for k in range(4):
            merg.wait_cross(h, k)
    for d in wo_send:
        d.wait_send()
    ring.finish()
    gath.finish()
    gout.finish()
    merg.finish()


def column(rows):
    n, m = rows.shape
    return jnp.concatenate([rows, jnp.zeros((128 - n, m), F32)], axis=0).T


def k_merge(
    lo, gain3, bias3, mi, seg, owners, wpg_h, pb, out,
    wpg, rows_f, fin, gb, sbuf, own, far_in, main_in, st, placed, obuf, lsem, ss, sr, xs, xr, ts, tr
):
    x, y, z, c = position()
    t = lax.axis_index("tok")
    n_tok = out.shape[0]
    slot = out.shape[1]
    merged = mi.shape[1]
    n_loc = wpg.shape[2]
    load = pltpu.make_async_copy(wpg_h, wpg, lsem.at[0])
    load.start()
    bar = pltpu.get_barrier_semaphore()

    @pl.loop(1, n_tok)
    def _(i):
        pl.semaphore_signal(bar, inc=1, device_id={"tok": (t + i) % n_tok}, device_id_type=MESH_ID)

    @pl.loop(1, 4)
    def _(i):
        pl.semaphore_signal(bar, inc=1, device_id=x_dev(x, i), device_id_type=MESH_ID)

    @pl.loop(0, 4)
    def _(i):
        rows = pl.ds(pl.multiple_of(i * 256, 256), 256)
        v = unpack_rows(lo.at[i]).astype(F32)
        rows_f[rows, :] = v
        mean = jnp.mean(v, axis=-1, keepdims=True)
        d = v - mean
        m2 = jnp.sum(d * d, axis=-1, keepdims=True)
        lane = lax.broadcasted_iota(jnp.int32, (256, 128), 1)
        both = jnp.where(lane == 0, mean, jnp.where(lane == 1, m2, 0.0))
        st[x, :, rows] = both.T[:8]

    pl.semaphore_wait(bar, n_tok + 2)
    sends = [rcopy(st.at[x], st.at[x], ss.at[k], sr.at[k], x_dev(x, k + 1)) for k in range(3)]
    for d in sends:
        d.start()
    for j in range(4):

        @pl.when(x == j)
        def _():
            gb[0:1, :] = gain3[n_loc * j : n_loc * j + n_loc].reshape(1, n_loc)
            gb[1:2, :] = bias3[n_loc * j : n_loc * j + n_loc].reshape(1, n_loc)

    idx = column(mi[...].astype(F32))
    toks = lax.broadcasted_iota(jnp.int32, (merged, 1024), 1).astype(F32)
    seg_of = jnp.sum(jnp.where(idx[:, 0:1] == toks, seg[...].astype(F32), 0.0), axis=1, keepdims=True)
    names = lax.broadcasted_iota(jnp.int32, (merged, n_tok), 1).astype(F32)
    owner = jnp.sum(jnp.where(seg_of == names, owners[...].astype(F32), 0.0), axis=1, keepdims=True)
    mine = (owner == names).astype(F32)
    below = lax.broadcasted_iota(jnp.int32, (merged, merged), 1) < lax.broadcasted_iota(
        jnp.int32, (merged, merged), 0
    )
    before = jnp.dot(
        jnp.where(below, 1.0, 0.0).astype(BF), mine.astype(BF), preferred_element_type=F32
    )
    rank = jnp.sum(before * mine, axis=1, keepdims=True)
    target = jnp.broadcast_to(owner * slot + rank, (merged, 128)).T[0:1]
    spots = lax.broadcasted_iota(jnp.int32, (n_tok * slot, merged), 0).astype(F32)
    placed[...] = jnp.where(spots == target, 1.0, 0.0).astype(BF)
    for d in sends:
        d.wait_recv()
    means = [st[s, 0:1, :] for s in range(4)]
    mean = 0.25 * (means[0] + means[1] + means[2] + means[3])
    m2 = st[0, 1:2, :] + st[1, 1:2, :] + st[2, 1:2, :] + st[3, 1:2, :]
    for s in range(4):
        d = means[s] - mean
        m2 = m2 + n_loc * (d * d)
    rstd = lax.rsqrt(m2 * (1.0 / (4 * n_loc)) + EPS)
    for i in range(8):
        sl = slice(128 * i, 128 * i + 128)
        row = lax.broadcasted_iota(jnp.int32, (128, 128), 0)
        cols = jnp.where(row == 0, mean[:, sl], jnp.where(row == 1, rstd[:, sl], 0.0)).T
        v = rows_f[sl, :]
        fin[sl, :] = ((v - cols[:, 0:1]) * cols[:, 1:2] * gb[0:1, :] + gb[1:2, :]).astype(BF)
    load.wait()
    got = []
    for k in range(4):
        pick = jnp.where(idx[:, k : k + 1] == toks, 1.0, 0.0).astype(BF)
        got.append(jnp.dot(pick, fin[...], preferred_element_type=F32).astype(BF))
    for j in range(4):
        acc = jnp.dot(got[0], wpg[j], preferred_element_type=F32)
        for k in range(1, 4):
            acc += jnp.dot(got[k], wpg[k * 4 + j], preferred_element_type=F32)
        pack_rows(acc, own.at[j])
        sbuf[j] = own[j].astype(BF)
    rg = RingReduce(sbuf, far_in, main_in, lambda k: xs.at[k], lambda k: xr.at[k], sbuf.shape[1] // 2)
    rg.start()
    rg.relay()
    rg.wait()
    own[x] += main_in[0].astype(F32) + main_in[1].astype(F32)
    total = unpack_rows(own.at[x]) + pb[...]
    going = jnp.dot(placed[...], total.astype(BF), preferred_element_type=F32).astype(BF)
    obuf[...] = going.reshape(n_tok, slot, n_loc)

    def slot_copy(i):
        to = (t + i) % n_tok
        return rcopy(obuf.at[to], out.at[t], ts.at[i], tr.at[i], {"tok": to})

    @pl.loop(1, n_tok)
    def _(i):
        slot_copy(i).start()

    keep = pltpu.make_async_copy(obuf.at[t], out.at[t], lsem.at[1])
    keep.start()
    rg.finish()
    for d in sends:
        d.wait_send()
    keep.wait()

    @pl.loop(1, n_tok)
    def _(i):
        slot_copy(i).wait()


def kernel_call(body, name, cid, ins, outs, out_specs, scratch, args):
    return pl.pallas_call(
        body,
        name=name,
        out_shape=outs,
        in_specs=ins,
        out_specs=out_specs,
        scratch_shapes=scratch,
        compiler_params=pltpu.CompilerParams(
            collective_id=cid, has_side_effects=True, vmem_limit_bytes=VLIM
        ),
    )(*args)


def sds(shape, dtype):
    return jax.ShapeDtypeStruct(shape, dtype)


DMA = pltpu.SemaphoreType.DMA


def body(
    tokens,
    segment_ids,
    merge_index,
    segment_owner,
    ln1_gain,
    ln1_bias,
    w_qkv,
    qkv_bias,
    w_out,
    out_bias,
    ln2_gain,
    ln2_bias,
    w_fc1,
    fc1_bias,
    w_fc2,
    fc2_bias,
    ln3_gain,
    ln3_bias,
    w_proj,
    proj_bias,
):
    tok = tokens[0]
    width = tok.shape[1]
    part_w = w_qkv.shape[2]
    depth = w_qkv.shape[1]
    heads = part_w // HD
    cols = 3 * heads * HPAD

    def tall(n):
        return 16 * (-(-(n // 128) * depth // 16))

    hidden = w_fc1.shape[1]
    flat = 256 * part_w // 128
    perm = []
    for bx in range(4):
        for t in range(32):
            ty, tz, tc = t // 8, (t // 2) % 4, t % 2
            perm.append((bx * 32 + t, tz * 32 + (ty * 4 + bx) * 2 + tc))
    wp = lax.ppermute(w_proj, ("blk", "tok"), perm)
    lo, wpg = kernel_call(
        k_layer,
        "layer",
        1,
        [VM] * 10 + [ANY, VM, ANY, VM, VM],
        [sds((4, flat, 128), BF), sds((32, 208, part_w), BF)],
        [VM, ANY],
        [
            pltpu.VMEM((tall(cols), 128), BF),
            pltpu.VMEM((tall(width), 128), BF),
            pltpu.VMEM((8, hidden), F32),
            pltpu.VMEM((1, cols), F32),
            pltpu.VMEM((4, depth, part_w), BF),
            pltpu.VMEM((4, 256, width), BF),
            pltpu.VMEM((3 * heads, 1024, HPAD), BF),
            pltpu.VMEM((32, tall(cols), 128), BF),
            pltpu.VMEM((32, tall(width), 128), BF),
            pltpu.VMEM((width, cols), BF),
            pltpu.VMEM((width, width), BF),
            pltpu.VMEM((4, 256, width), BF),
            pltpu.VMEM((width, hidden), BF),
            pltpu.VMEM((hidden, width), BF),
            pltpu.VMEM((4, 4, flat, 128), BF),
            pltpu.VMEM((heads, 256, HPAD), BF),
            pltpu.VMEM((1024, 128), F32),
            pltpu.VMEM((256, width), F32),
            pltpu.VMEM((256, hidden), BF),
            pltpu.VMEM((4, flat, 128), F32),
            pltpu.VMEM((flat, 128), F32),
            pltpu.VMEM((4, 4, flat, 128), BF),
            pltpu.VMEM((4, 2, flat // 2, 128), BF),
            pltpu.VMEM((4, 2, flat, 128), BF),
            DMA((6,)),
            DMA((6,)),
            DMA((6,)),
            DMA((3,)),
            DMA((3,)),
            DMA((4, 6)),
            DMA((4, 6)),
            DMA((4, 6)),
            DMA((4, 6)),
        ]
        + TOK_SEMS * 3,
        (
            tok, w_qkv, w_out.T, ln1_gain, ln1_bias, qkv_bias, segment_ids, out_bias, ln2_gain,
            ln2_bias, w_fc1, fc1_bias, w_fc2, fc2_bias, wp,
        ),
    )
    merged_count = merge_index.shape[1]
    n_tok = lax.axis_size("tok")
    slot = 2 * merged_count // n_tok
    arrived = kernel_call(
        k_merge,
        "merge",
        3,
        [VM] * 6 + [ANY, VM],
        [sds((n_tok, slot, part_w), BF)],
        [VM],
        [
            pltpu.VMEM((16, part_w, part_w), BF),
            pltpu.VMEM((1024, part_w), F32),
            pltpu.VMEM((1024, part_w), BF),
            pltpu.VMEM((2, part_w), F32),
            pltpu.VMEM((4, flat, 128), BF),
            pltpu.VMEM((4, flat, 128), F32),
            pltpu.VMEM((2, flat // 2, 128), BF),
            pltpu.VMEM((2, flat, 128), BF),
            pltpu.VMEM((4, 8, 1024), F32),
            pltpu.VMEM((n_tok * slot, merged_count), BF),
            pltpu.VMEM((n_tok, slot, part_w), BF),
            DMA((2,)),
            DMA((3,)),
            DMA((3,)),
            DMA((6,)),
            DMA((6,)),
            DMA((n_tok,)),
            DMA((n_tok,)),
        ],
        (
            lo,
            ln3_gain,
            ln3_bias,
            merge_index[0].T,
            segment_ids,
            segment_owner,
            wpg.reshape(16, part_w, part_w),
            proj_bias,
        ),
    )[0]
    return arrived[None]


def solution(mesh):
    placed = (
        P("tok", "blk", None),
        P("tok", None),
        P("tok", None, None),
        P("tok", None),
        P(),
        P(),
        P(None, "tok", "blk"),
        P(None, "blk"),
        P("blk", "tok"),
        P(),
        P(),
        P(),
        P(None, "blk"),
        P("blk"),
        P("blk", None),
        P(),
        P(),
        P(),
        P("tok", "blk"),
        P("blk"),
    )
    return jax.shard_map(
        body, mesh=mesh, in_specs=placed, out_specs=P("tok", None, None, "blk"), check_vma=False
    )
```

```python
import math

import jax
import jax.numpy as jnp
from jax import lax
from jax.experimental import pallas as pl
from jax.experimental.pallas import tpu as pltpu
from jax.sharding import PartitionSpec as P

HD = 104
HPAD = 128
EPS = 1e-06
BF = jnp.bfloat16
F32 = jnp.float32
MESH_ID = pl.DeviceIdType.MESH
VLIM = 65000 * 1024
VM = pl.BlockSpec(memory_space=pltpu.VMEM)
ANY = pl.BlockSpec(memory_space=pl.ANY)


def position():
    x = lax.axis_index("blk")
    t = lax.axis_index("tok")
    return x, t // 8, (t // 2) % 4, t % 2


def tok_of(y, z, c):
    return ((y % 4) * 4 + z % 4) * 2 + c


def rcopy(src, dst, ssem, rsem, dev):
    return pltpu.make_async_remote_copy(
        src_ref=src, dst_ref=dst, send_sem=ssem, recv_sem=rsem, device_id=dev, device_id_type=MESH_ID
    )


def x_dev(x, off):
    return {"blk": (x + off) % 4}


def meet(peers):
    bar = pltpu.get_barrier_semaphore()
    for dev in peers:
        pl.semaphore_signal(bar, inc=1, device_id=dev, device_id_type=MESH_ID)
    pl.semaphore_wait(bar, len(peers))


def x_peers():
    x, y, z, c = position()
    return [x_dev(x, 1), x_dev(x, 3)]


def tok_peers():
    x, y, z, c = position()
    return [
        {"tok": tok_of(y, z + 1, c)},
        {"tok": tok_of(y, z + 3, c)},
        {"tok": tok_of(y + 1, z, c)},
        {"tok": tok_of(y + 3, z, c)},
        {"tok": tok_of(y, z, 1 - c)},
    ]


class RingGather:
    def __init__(self, own, half, ss, rs):
        x = lax.axis_index("blk")
        right, left = x_dev(x, 1), x_dev(x, 3)

        def send(view, src, i, k, dev):
            return rcopy(view, half(src, i), ss(k), rs(k), dev)

        me, lo, hi = x, (x + 3) % 4, (x + 1) % 4
        self.c = [
            send(own(0), me, 0, 0, right),
            send(own(1), me, 1, 1, right),
            send(own(1), me, 1, 2, left),
            send(own(0), me, 0, 3, left),
            send(half(lo, 0), lo, 0, 4, right),
            send(half(hi, 1), hi, 1, 5, left),
        ]

    def start(self):
        for k in (0, 2, 1, 3):
            self.c[k].start()

    def relay(self):
        self.c[0].wait_recv()
        self.c[4].start()
        self.c[2].wait_recv()
        self.c[5].start()

    def wait_near(self):
        self.c[1].wait_recv()
        self.c[3].wait_recv()

    def wait_far(self):
        self.c[4].wait_recv()
        self.c[5].wait_recv()

    def finish(self):
        for c in self.c:
            c.wait_send()


class TokGather:
    OFF = (0, 3, 1, 2)

    def __init__(self, own, slots, view, fs, fr, ss, sr, cs, cr):
        x, y, z, c = position()
        self.first, self.second, self.cross = [], [], []
        sib = {"tok": tok_of(y, z, 1 - c)}
        for h in range(2):

            def tok(d1, d2, h=h):
                return tok_of(y + d2, z + d1, c) if h == 0 else tok_of(y + d1, z + d2, c)

            def slot(d1, d2, tok=tok):
                return slots.at[tok(d1, d2)]

            def half(r, h=h):
                return view(r, h, None)

            def quarter(r, q, h=h):
                return view(r, h, q)

            me = slot(0, 0)
            p1, m1 = {"tok": tok(1, 0)}, {"tok": tok(3, 0)}
            p2, m2 = {"tok": tok(0, 1)}, {"tok": tok(0, 3)}
            self.first.append(
                [
                    rcopy(half(own), half(me), fs.at[h, 0], fr.at[h, 0], p1),
                    rcopy(half(own), half(me), fs.at[h, 1], fr.at[h, 1], m1),
                    rcopy(quarter(slot(3, 0), 0), quarter(slot(3, 0), 0), fs.at[h, 2], fr.at[h, 2], p1),
                    rcopy(quarter(slot(1, 0), 1), quarter(slot(1, 0), 1), fs.at[h, 3], fr.at[h, 3], m1),
                ]
            )
            second = []
            for i, o in enumerate(self.OFF):
                src = half(own) if i == 0 else half(slot(o, 0))
                here, up, dn = half(slot(o, 0)), slot(o, 3), slot(o, 1)
                second.append(
                    [
                        rcopy(src, here, ss.at[h, i, 0], sr.at[h, i, 0], p2),
                        rcopy(src, here, ss.at[h, i, 1], sr.at[h, i, 1], m2),
                        rcopy(quarter(up, 0), quarter(up, 0), ss.at[h, i, 2], sr.at[h, i, 2], p2),
                        rcopy(quarter(dn, 1), quarter(dn, 1), ss.at[h, i, 3], sr.at[h, i, 3], m2),
                    ]
                )
            self.second.append(second)
            cross = []
            for k in range(4):
                row = []
                for i, o in enumerate(self.OFF):
                    dst = half(slot(o, self.OFF[k]))
                    src = half(own) if (i == 0 and k == 0) else dst
                    row.append(rcopy(src, dst, cs.at[h, k, i], cr.at[h, k, i], sib))
                cross.append(row)
            self.cross.append(cross)

    def start(self):
        for h in range(2):
            self.first[h][0].start()
            self.first[h][1].start()
        for h in range(2):
            self._fan(h, 0)

    def _fan(self, h, i):
        self.second[h][i][0].start()
        self.second[h][i][1].start()
        self.cross[h][0][i].start()

    def first_near(self, h):
        f = self.first[h]
        f[0].wait_recv()
        f[2].start()
        self._fan(h, 1)
        f[1].wait_recv()
        f[3].start()
        self._fan(h, 2)

    def first_far(self, h):
        self.first[h][2].wait_recv()
        self.first[h][3].wait_recv()
        self._fan(h, 3)

    def second_near(self, h, i):
        f = self.second[h][i]
        f[0].wait_recv()
        f[2].start()
        self.cross[h][1][i].start()
        f[1].wait_recv()
        f[3].start()
        self.cross[h][2][i].start()

    def second_far(self, h, i):
        f = self.second[h][i]
        f[2].wait_recv()
        f[3].wait_recv()
        self.cross[h][3][i].start()

    def wait_cross(self, h, k):
        for d in self.cross[h][k]:
            d.wait_recv()

    def _all(self):
        for h in range(2):
            for row in self.cross[h]:
                yield from row

    def finish(self):
        for h in range(2):
            for d in self.first[h]:
                d.wait_send()
            for row in self.second[h]:
                for d in row:
                    d.wait_send()
        for d in self._all():
            d.wait_send()


TOK_SEMS = [pltpu.SemaphoreType.DMA((2, 4))] * 2 + [pltpu.SemaphoreType.DMA((2, 4, 4))] * 4


def norm_rows(src, dst, gain, bias, rows, first=0, step=32):
    @pl.loop(0, rows // step)
    def _(i):
        at = pl.ds(pl.multiple_of(first + i * step, step), step)
        v = src[at, :].astype(F32)
        mean = jnp.mean(v, axis=-1, keepdims=True)
        center = v - mean
        spread = jnp.mean(center * center, axis=-1, keepdims=True)
        dst[at, :] = (center * lax.rsqrt(spread + EPS) * gain[...] + bias[...]).astype(dst.dtype)


def pack_rows(v, dst):
    rows, width = v.shape
    full = width // 128
    rest = width - 128 * full
    for i in range(full):
        dst[rows * i : rows * i + rows] = v[:, 128 * i : 128 * i + 128]
    n = 128 // rest
    part = rows // n
    tail = [v[part * q : part * q + part, 128 * full :] for q in range(n)]
    dst[rows * full : rows * full + part] = jnp.concatenate(tail, axis=1)


def unpack_rows(src, rows=256, rest=32):
    n = 128 // rest
    part = rows // n
    full = (src.shape[0] - part) // rows
    last = src[rows * full : rows * full + part]
    tail = jnp.concatenate([last[:, rest * q : rest * q + rest] for q in range(n)], axis=0)
    return jnp.concatenate([src[rows * i : rows * i + rows] for i in range(full)] + [tail], axis=1)


class RingReduce:
    def __init__(self, sbuf, far_in, main_in, ss, rs, half):
        x = lax.axis_index("blk")
        self.hi, self.lo, self.far = (x + 1) % 4, (x + 3) % 4, (x + 2) % 4
        self.sbuf, self.far_in, self.main_in = sbuf, far_in, main_in
        right, left = x_dev(x, 1), x_dev(x, 3)
        self.a, self.b = pl.ds(0, half), pl.ds(half, half)
        a, b = self.a, self.b
        self.c = [
            rcopy(sbuf.at[self.far, a], far_in.at[0], ss(0), rs(0), right),
            rcopy(sbuf.at[self.far, b], far_in.at[1], ss(1), rs(1), left),
            rcopy(sbuf.at[self.hi, b], main_in.at[0, b], ss(2), rs(2), right),
            rcopy(sbuf.at[self.lo, a], main_in.at[1, a], ss(3), rs(3), left),
            rcopy(sbuf.at[self.hi, a], main_in.at[0, a], ss(4), rs(4), right),
            rcopy(sbuf.at[self.lo, b], main_in.at[1, b], ss(5), rs(5), left),
        ]

    def start(self):
        for k in range(4):
            self.c[k].start()

    def relay(self):
        self.c[0].wait_recv()
        s = self.sbuf[self.hi, self.a].astype(F32) + self.far_in[0].astype(F32)
        self.sbuf[self.hi, self.a] = s.astype(BF)
        self.c[1].wait_recv()
        s = self.sbuf[self.lo, self.b].astype(F32) + self.far_in[1].astype(F32)
        self.sbuf[self.lo, self.b] = s.astype(BF)
        self.c[4].start()
        self.c[5].start()

    def wait(self):
        for k in range(2, 6):
            self.c[k].wait_recv()

    def finish(self):
        for d in self.c:
            d.wait_send()


def gelu(v):
    return 0.5 * v * (1.0 + lax.erf(v * (1.0 / math.sqrt(2.0))))


def view_rows(tiles):
    first = 16 * ((tiles + 1) // 2)
    halves = ((0, first), (first, 16 * tiles - first))

    def view(r, h, q):
        start, size = halves[h]
        if q is None:
            return r.at[pl.ds(start, size)]
        lead = 16 * ((size // 16 + 1) // 2)
        return r.at[pl.ds(start, lead)] if q == 0 else r.at[pl.ds(start + lead, size - lead)]

    return view


def k_layer(
    tok, wq, wout, gain1, bias1, qbias, seg, ob, gain2, bias2, fc1, b1, fc2, b2, wp, lo, wpg,
    pack, packo, vec, qb, wo4, toks, qkv, slots, oslots, wf, wof, hb, w1, w2, att, oh, segc, after, hid, own, mine,
    sbuf, far_in, main_in, lsem, rs, rr, ws, wr, as_, ar, xs, xr, *gs
):
    x, y, z, c = position()
    t = lax.axis_index("tok")
    depth = wq.shape[1]
    heads = wq.shape[2] // HD
    nq = 3 * heads
    no = wof.shape[1] // 128
    h2, attf = hb.at[0], hb.at[1]
    width = tok.shape[1]
    load = [
        pltpu.make_async_copy(fc1, w1, lsem.at[2]),
        pltpu.make_async_copy(fc2, w2, lsem.at[3]),
        pltpu.make_async_copy(wp, wpg.at[t], lsem.at[4]),
    ]
    meet(x_peers() + [x_dev(x, 2)] + tok_peers())
    wo_send = [rcopy(wout, wo4.at[x], ws.at[k], wr.at[k], x_dev(x, k + 1)) for k in range(3)]
    for d in wo_send:
        d.start()
    ring = RingGather(
        lambda i: tok.at[pl.ds(128 * i, 128)],
        lambda s, i: toks.at[s, pl.ds(128 * i, 128)],
        lambda k: rs.at[k],
        lambda k: rr.at[k],
    )
    ring.start()
    for i, v in enumerate((gain1, bias1, gain2, bias2, ob, b2, b1)):
        vec[i : i + 1, : v.shape[0]] = v[...].reshape(1, v.shape[0])
    gain1, bias1, gain2, bias2, ob, b2 = [vec.at[i : i + 1, :width] for i in range(6)]
    b1 = vec.at[6:7]
    local = [pltpu.make_async_copy(tok, toks.at[x], lsem.at[0])]
    local[0].start()
    zero = jnp.zeros((depth, HPAD - HD), BF)
    for k in range(3):
        for h in range(heads):
            n = k * heads + h
            piece = wq[k, :, h * HD : h * HD + HD]
            pack[n * depth : n * depth + depth, :] = jnp.concatenate([piece, zero], axis=1)
            qb[:, n * HPAD : n * HPAD + HPAD] = jnp.concatenate(
                [qbias[k : k + 1, h * HD : h * HD + HD], jnp.zeros((1, HPAD - HD), F32)], axis=1
            )
    gath = TokGather(pack, slots, view_rows(pack.shape[0] // 16), *gs[:6])
    gath.start()
    wo4[x] = wout[...]
    for d in wo_send:
        d.wait_recv()
    wide = jnp.concatenate([wo4[b] for b in range(4)], axis=1)
    for n in range(no):
        packo[n * depth : n * depth + depth, :] = wide[:, 128 * n : 128 * n + 128]
    gout = TokGather(packo, oslots, view_rows(packo.shape[0] // 16), *gs[6:12])
    local.append(pltpu.make_async_copy(pack, slots.at[t], lsem.at[1]))
    local[1].start()
    for d in load:
        d.start()
    norm_rows(tok, hb.at[x], gain1, bias1, 256)
    segr = seg[...].astype(F32)
    segc[...] = jnp.broadcast_to(segr, (128, segr.shape[1])).T

    def unpack(g, src, n, dst):
        for i in range(n):
            at = i * depth
            parts = [src[4 * g + j, at : at + depth, :] for j in range(4)]
            rows = pl.ds(pl.multiple_of(g * 208, 16), 208)
            dst[rows, 128 * i : 128 * i + 128] = jnp.concatenate(parts, axis=0)

    def unpack_all(gat, src, n, dst):
        for h in range(2):
            for k in range(4):
                gat.wait_cross(h, k)

        @pl.loop(0, 8)
        def _(g):
            unpack(g, src, n, dst)

    def project(s):
        @pl.loop(0, wf.shape[1] // 256)
        def _(j):
            cols = pl.ds(pl.multiple_of(j * 256, 256), 256)
            v = jnp.dot(hb[s], wf[:, cols], preferred_element_type=F32) + qb[:, cols]
            v = v.astype(BF)
            rows = pl.ds(pl.multiple_of(s * 256, 256), 256)
            qkv[2 * j, rows, :] = v[:, :128]
            qkv[2 * j + 1, rows, :] = v[:, 128:]

    for h in range(2):
        gath.first_near(h)
    for h in range(2):
        gath.first_far(h)
    for i in range(2):
        for h in range(2):
            gath.second_near(h, i)
    ring.relay()
    for i in range(2, 4):
        for h in range(2):
            gath.second_near(h, i)
    gout.start()
    local.append(pltpu.make_async_copy(packo, oslots.at[t], lsem.at[5]))
    local[2].start()
    lo_x, hi_x = (x + 3) % 4, (x + 1) % 4
    norm_rows(toks.at[lo_x], hb.at[lo_x], gain1, bias1, 128)
    norm_rows(toks.at[hi_x], hb.at[hi_x], gain1, bias1, 128, first=128)
    for d in local:
        d.wait()
    ring.wait_near()
    norm_rows(toks.at[lo_x], hb.at[lo_x], gain1, bias1, 128, first=128)
    norm_rows(toks.at[hi_x], hb.at[hi_x], gain1, bias1, 128)
    for i in range(4):
        for h in range(2):
            gath.second_far(h, i)
    for h in range(2):
        gout.first_near(h)
    unpack_all(gath, slots, nq, wf)
    for h in range(2):
        gout.first_far(h)

    @pl.loop(0, 3)
    def _(i):
        project((x + i + i // 2) % 4)

    for i in range(4):
        for h in range(2):
            gout.second_near(h, i)
    merg = TokGather(wp, wpg, view_rows(wp.shape[0] // 16), *gs[12:])
    merg.start()
    ring.wait_far()
    far = (x + 2) % 4
    norm_rows(toks.at[far], hb.at[far], gain1, bias1, 256)
    project(far)
    scale = 1.0 / math.sqrt(HD)
    half = att.shape[2] // 2

    def attend(r):
        @pl.loop(0, 2)
        def _(sub):
            rows = pl.ds(pl.multiple_of(r * 256 + sub * 128, 128), 128)
            same = segc[rows, 0:1] == segr
            for h in range(heads):
                s = lax.dot_general(
                    qkv[h, rows, :], qkv[heads + h], (((1,), (1,)), ((), ())), preferred_element_type=F32
                )
                p = jnp.where(same, jnp.exp(s * scale), 0.0)
                total = jnp.sum(p, axis=-1, keepdims=True)
                o = jnp.dot(p.astype(BF), qkv[2 * heads + h], preferred_element_type=F32) / total
                oh[h, pl.ds(pl.multiple_of(sub * 128, 128), 128), :] = o.astype(BF)

        pack_rows(jnp.concatenate([oh[h][:, :HD] for h in range(heads)], axis=1), att.at[x, r])

    def gather_ring(r):
        def part(s, i):
            return att.at[s, r, pl.ds(half * i, half)]

        return RingGather(lambda i: part(x, i), part, lambda k: as_.at[r, k], lambda k: ar.at[r, k])

    def reduce_ring(r):
        return RingReduce(
            sbuf.at[r],
            far_in.at[r],
            main_in.at[r],
            lambda k: xs.at[r, k],
            lambda k: xr.at[r, k],
            half,
        )

    attend(0)
    gather_ring(0).start()
    for i in range(4):
        for h in range(2):
            gout.second_far(h, i)
    attend(1)
    gather_ring(0).relay()
    gather_ring(1).start()
    for h in range(2):
        merg.first_near(h)
    attend(2)
    gather_ring(1).relay()
    gather_ring(2).start()
    for h in range(2):
        merg.first_far(h)
    attend(3)
    gather_ring(2).relay()
    gather_ring(3).start()
    unpack_all(gout, oslots, no, wof)
    tiles = [(n, min(256, 1664 - n)) for n in range(0, 1664, 256)]
    @pl.loop(0, 6)
    def _(r):
        @pl.when(r < 4)
        def _():
            rg = gather_ring(r)
            rg.wait_near()
            rg.wait_far()
            attf[...] = jnp.concatenate([unpack_rows(att.at[b, r]) for b in range(4)], axis=1)
            for n, w in tiles:
                acc = lax.dot_general(
                    attf[...], wof[n : n + w, :], (((1,), (1,)), ((), ())), preferred_element_type=F32
                )
                after[:, n : n + w] = acc + toks[r, :, n : n + w].astype(F32) + ob[:, n : n + w]

            @pl.when(r == 0)
            def _():
                gather_ring(3).relay()
                load[0].wait()

            @pl.when(r > 0)
            def _():
                reduce_ring(r - 1).relay()

            @pl.when(r == 1)
            def _():
                for i in range(4):
                    for h in range(2):
                        merg.second_near(h, i)

            @pl.when(r == 3)
            def _():
                for i in range(4):
                    for h in range(2):
                        merg.second_far(h, i)

            norm_rows(after, h2, gain2, bias2, 256)
            for j in range(4):

                @pl.when(x == j)
                def _():
                    pack_rows(after[:, 416 * j : 416 * j + 416] + b2[:, 416 * j : 416 * j + 416], own.at[r])

            for j in range(8):
                cols = slice(256 * j, 256 * j + 256)
                v = jnp.dot(h2[...], w1[:, cols], preferred_element_type=F32) + b1[:, cols]
                hid[:, cols] = gelu(v).astype(BF)

            @pl.when(r == 0)
            def _():
                load[1].wait()

            for n, w in tiles:
                after[:, n : n + w] = jnp.dot(hid[...], w2[:, n : n + w], preferred_element_type=F32)
            for j in range(4):
                piece = after[:, 416 * j : 416 * j + 416]
                pack_rows(piece.astype(BF), sbuf.at[r, j])

                @pl.when(x == j)
                def _():
                    pack_rows(piece, mine)
                    own[r] += mine[...]

            reduce_ring(r).start()

        @pl.when(r == 4)
        def _():
            reduce_ring(3).relay()

        @pl.when(r > 1)
        def _():
            q = r - 2
            rg = reduce_ring(q)
            rg.wait()
            total = own[q] + main_in[q, 0].astype(F32) + main_in[q, 1].astype(F32)
            lo[q] = total.astype(BF)
            rg.finish()
            gather_ring(q).finish()

    load[2].wait()
    for h in range(2):
        for k in range(4):
            merg.wait_cross(h, k)
    for d in wo_send:
        d.wait_send()
    ring.finish()
    gath.finish()
    gout.finish()
    merg.finish()


def column(rows):
    n, m = rows.shape
    return jnp.concatenate([rows, jnp.zeros((128 - n, m), F32)], axis=0).T


def k_merge(
    lo, gain3, bias3, mi, seg, owners, wpg_h, pb, out,
    wpg, rows_f, fin, gb, sbuf, own, far_in, main_in, st, placed, obuf, lsem, ss, sr, xs, xr, ts, tr
):
    x, y, z, c = position()
    t = lax.axis_index("tok")
    n_tok = out.shape[0]
    slot = out.shape[1]
    merged = mi.shape[1]
    n_loc = wpg.shape[2]
    load = pltpu.make_async_copy(wpg_h, wpg, lsem.at[0])
    load.start()
    bar = pltpu.get_barrier_semaphore()

    @pl.loop(1, n_tok)
    def _(i):
        pl.semaphore_signal(bar, inc=1, device_id={"tok": (t + i) % n_tok}, device_id_type=MESH_ID)

    @pl.loop(1, 4)
    def _(i):
        pl.semaphore_signal(bar, inc=1, device_id=x_dev(x, i), device_id_type=MESH_ID)

    @pl.loop(0, 4)
    def _(i):
        rows = pl.ds(pl.multiple_of(i * 256, 256), 256)
        v = unpack_rows(lo.at[i]).astype(F32)
        rows_f[rows, :] = v
        mean = jnp.mean(v, axis=-1, keepdims=True)
        d = v - mean
        m2 = jnp.sum(d * d, axis=-1, keepdims=True)
        lane = lax.broadcasted_iota(jnp.int32, (256, 128), 1)
        both = jnp.where(lane == 0, mean, jnp.where(lane == 1, m2, 0.0))
        st[x, :, rows] = both.T[:8]

    pl.semaphore_wait(bar, n_tok + 2)
    sends = [rcopy(st.at[x], st.at[x], ss.at[k], sr.at[k], x_dev(x, k + 1)) for k in range(3)]
    for d in sends:
        d.start()
    for j in range(4):

        @pl.when(x == j)
        def _():
            gb[0:1, :] = gain3[n_loc * j : n_loc * j + n_loc].reshape(1, n_loc)
            gb[1:2, :] = bias3[n_loc * j : n_loc * j + n_loc].reshape(1, n_loc)

    idx = column(mi[...].astype(F32))
    toks = lax.broadcasted_iota(jnp.int32, (merged, 1024), 1).astype(F32)
    seg_of = jnp.sum(jnp.where(idx[:, 0:1] == toks, seg[...].astype(F32), 0.0), axis=1, keepdims=True)
    names = lax.broadcasted_iota(jnp.int32, (merged, n_tok), 1).astype(F32)
    owner = jnp.sum(jnp.where(seg_of == names, owners[...].astype(F32), 0.0), axis=1, keepdims=True)
    mine = (owner == names).astype(F32)
    below = lax.broadcasted_iota(jnp.int32, (merged, merged), 1) < lax.broadcasted_iota(
        jnp.int32, (merged, merged), 0
    )
    before = jnp.dot(
        jnp.where(below, 1.0, 0.0).astype(BF), mine.astype(BF), preferred_element_type=F32
    )
    rank = jnp.sum(before * mine, axis=1, keepdims=True)
    target = jnp.broadcast_to(owner * slot + rank, (merged, 128)).T[0:1]
    spots = lax.broadcasted_iota(jnp.int32, (n_tok * slot, merged), 0).astype(F32)
    placed[...] = jnp.where(spots == target, 1.0, 0.0).astype(BF)
    for d in sends:
        d.wait_recv()
    means = [st[s, 0:1, :] for s in range(4)]
    mean = 0.25 * (means[0] + means[1] + means[2] + means[3])
    m2 = st[0, 1:2, :] + st[1, 1:2, :] + st[2, 1:2, :] + st[3, 1:2, :]
    for s in range(4):
        d = means[s] - mean
        m2 = m2 + n_loc * (d * d)
    rstd = lax.rsqrt(m2 * (1.0 / (4 * n_loc)) + EPS)
    for i in range(8):
        sl = slice(128 * i, 128 * i + 128)
        row = lax.broadcasted_iota(jnp.int32, (128, 128), 0)
        cols = jnp.where(row == 0, mean[:, sl], jnp.where(row == 1, rstd[:, sl], 0.0)).T
        v = rows_f[sl, :]
        fin[sl, :] = ((v - cols[:, 0:1]) * cols[:, 1:2] * gb[0:1, :] + gb[1:2, :]).astype(BF)
    load.wait()
    got = []
    for k in range(4):
        pick = jnp.where(idx[:, k : k + 1] == toks, 1.0, 0.0).astype(BF)
        got.append(jnp.dot(pick, fin[...], preferred_element_type=F32).astype(BF))
    for j in range(4):
        acc = jnp.dot(got[0], wpg[j], preferred_element_type=F32)
        for k in range(1, 4):
            acc += jnp.dot(got[k], wpg[k * 4 + j], preferred_element_type=F32)
        pack_rows(acc, own.at[j])
        sbuf[j] = own[j].astype(BF)
    rg = RingReduce(sbuf, far_in, main_in, lambda k: xs.at[k], lambda k: xr.at[k], sbuf.shape[1] // 2)
    rg.start()
    rg.relay()
    rg.wait()
    own[x] += main_in[0].astype(F32) + main_in[1].astype(F32)
    total = unpack_rows(own.at[x]) + pb[...]
    going = jnp.dot(placed[...], total.astype(BF), preferred_element_type=F32).astype(BF)
    obuf[...] = going.reshape(n_tok, slot, n_loc)

    def slot_copy(i):
        to = (t + i) % n_tok
        return rcopy(obuf.at[to], out.at[t], ts.at[i], tr.at[i], {"tok": to})

    @pl.loop(1, n_tok)
    def _(i):
        slot_copy(i).start()

    keep = pltpu.make_async_copy(obuf.at[t], out.at[t], lsem.at[1])
    keep.start()
    rg.finish()
    for d in sends:
        d.wait_send()
    keep.wait()

    @pl.loop(1, n_tok)
    def _(i):
        slot_copy(i).wait()


def kernel_call(body, name, cid, ins, outs, out_specs, scratch, args):
    return pl.pallas_call(
        body,
        name=name,
        out_shape=outs,
        in_specs=ins,
        out_specs=out_specs,
        scratch_shapes=scratch,
        compiler_params=pltpu.CompilerParams(
            collective_id=cid, has_side_effects=True, vmem_limit_bytes=VLIM
        ),
    )(*args)


def sds(shape, dtype):
    return jax.ShapeDtypeStruct(shape, dtype)


DMA = pltpu.SemaphoreType.DMA


def body(
    tokens,
    segment_ids,
    merge_index,
    segment_owner,
    ln1_gain,
    ln1_bias,
    w_qkv,
    qkv_bias,
    w_out,
    out_bias,
    ln2_gain,
    ln2_bias,
    w_fc1,
    fc1_bias,
    w_fc2,
    fc2_bias,
    ln3_gain,
    ln3_bias,
    w_proj,
    proj_bias,
):
    tok = tokens[0]
    width = tok.shape[1]
    part_w = w_qkv.shape[2]
    depth = w_qkv.shape[1]
    heads = part_w // HD
    cols = 3 * heads * HPAD

    def tall(n):
        return 16 * (-(-(n // 128) * depth // 16))

    hidden = w_fc1.shape[1]
    flat = 256 * part_w // 128
    perm = []
    for bx in range(4):
        for t in range(32):
            ty, tz, tc = t // 8, (t // 2) % 4, t % 2
            perm.append((bx * 32 + t, tz * 32 + (ty * 4 + bx) * 2 + tc))
    wp = lax.ppermute(w_proj, ("blk", "tok"), perm)
    lo, wpg = kernel_call(
        k_layer,
        "layer",
        1,
        [VM] * 10 + [ANY, VM, ANY, VM, VM],
        [sds((4, flat, 128), BF), sds((32, 208, part_w), BF)],
        [VM, ANY],
        [
            pltpu.VMEM((tall(cols), 128), BF),
            pltpu.VMEM((tall(width), 128), BF),
            pltpu.VMEM((8, hidden), F32),
            pltpu.VMEM((1, cols), F32),
            pltpu.VMEM((4, depth, part_w), BF),
            pltpu.VMEM((4, 256, width), BF),
            pltpu.VMEM((3 * heads, 1024, HPAD), BF),
            pltpu.VMEM((32, tall(cols), 128), BF),
            pltpu.VMEM((32, tall(width), 128), BF),
            pltpu.VMEM((width, cols), BF),
            pltpu.VMEM((width, width), BF),
            pltpu.VMEM((4, 256, width), BF),
            pltpu.VMEM((width, hidden), BF),
            pltpu.VMEM((hidden, width), BF),
            pltpu.VMEM((4, 4, flat, 128), BF),
            pltpu.VMEM((heads, 256, HPAD), BF),
            pltpu.VMEM((1024, 128), F32),
            pltpu.VMEM((256, width), F32),
            pltpu.VMEM((256, hidden), BF),
            pltpu.VMEM((4, flat, 128), F32),
            pltpu.VMEM((flat, 128), F32),
            pltpu.VMEM((4, 4, flat, 128), BF),
            pltpu.VMEM((4, 2, flat // 2, 128), BF),
            pltpu.VMEM((4, 2, flat, 128), BF),
            DMA((6,)),
            DMA((6,)),
            DMA((6,)),
            DMA((3,)),
            DMA((3,)),
            DMA((4, 6)),
            DMA((4, 6)),
            DMA((4, 6)),
            DMA((4, 6)),
        ]
        + TOK_SEMS * 3,
        (
            tok, w_qkv, w_out.T, ln1_gain, ln1_bias, qkv_bias, segment_ids, out_bias, ln2_gain,
            ln2_bias, w_fc1, fc1_bias, w_fc2, fc2_bias, wp,
        ),
    )
    merged_count = merge_index.shape[1]
    n_tok = lax.axis_size("tok")
    slot = 2 * merged_count // n_tok
    arrived = kernel_call(
        k_merge,
        "merge",
        3,
        [VM] * 6 + [ANY, VM],
        [sds((n_tok, slot, part_w), BF)],
        [VM],
        [
            pltpu.VMEM((16, part_w, part_w), BF),
            pltpu.VMEM((1024, part_w), F32),
            pltpu.VMEM((1024, part_w), BF),
            pltpu.VMEM((2, part_w), F32),
            pltpu.VMEM((4, flat, 128), BF),
            pltpu.VMEM((4, flat, 128), F32),
            pltpu.VMEM((2, flat // 2, 128), BF),
            pltpu.VMEM((2, flat, 128), BF),
            pltpu.VMEM((4, 8, 1024), F32),
            pltpu.VMEM((n_tok * slot, merged_count), BF),
            pltpu.VMEM((n_tok, slot, part_w), BF),
            DMA((2,)),
            DMA((3,)),
            DMA((3,)),
            DMA((6,)),
            DMA((6,)),
            DMA((n_tok,)),
            DMA((n_tok,)),
        ],
        (
            lo,
            ln3_gain,
            ln3_bias,
            merge_index[0].T,
            segment_ids,
            segment_owner,
            wpg.reshape(16, part_w, part_w),
            proj_bias,
        ),
    )[0]
    return arrived[None]


def solution(mesh):
    placed = (
        P("tok", "blk", None),
        P("tok", None),
        P("tok", None, None),
        P("tok", None),
        P(),
        P(),
        P(None, "tok", "blk"),
        P(None, "blk"),
        P("blk", "tok"),
        P(),
        P(),
        P(),
        P(None, "blk"),
        P("blk"),
        P("blk", None),
        P(),
        P(),
        P(),
        P("tok", "blk"),
        P("blk"),
    )
    return jax.shard_map(
        body, mesh=mesh, in_specs=placed, out_specs=P("tok", None, None, "blk"), check_vma=False
    )
```

```python
import math

import jax
import jax.numpy as jnp
from jax import lax
from jax.experimental import pallas as pl
from jax.experimental.pallas import tpu as pltpu
from jax.sharding import PartitionSpec as P

HD = 104
HPAD = 128
EPS = 1e-06
BF = jnp.bfloat16
F32 = jnp.float32
MESH_ID = pl.DeviceIdType.MESH
VLIM = 64600 * 1024
VM = pl.BlockSpec(memory_space=pltpu.VMEM)
ANY = pl.BlockSpec(memory_space=pl.ANY)


def position():
    x = lax.axis_index("blk")
    t = lax.axis_index("tok")
    return x, t // 8, (t // 2) % 4, t % 2


def tok_of(y, z, c):
    return ((y % 4) * 4 + z % 4) * 2 + c


def rcopy(src, dst, ssem, rsem, dev):
    return pltpu.make_async_remote_copy(
        src_ref=src, dst_ref=dst, send_sem=ssem, recv_sem=rsem, device_id=dev, device_id_type=MESH_ID
    )


def x_dev(x, off):
    return {"blk": (x + off) % 4}


def meet(peers):
    bar = pltpu.get_barrier_semaphore()
    for dev in peers:
        pl.semaphore_signal(bar, inc=1, device_id=dev, device_id_type=MESH_ID)
    pl.semaphore_wait(bar, len(peers))


def x_peers():
    x, y, z, c = position()
    return [x_dev(x, 1), x_dev(x, 3)]


def tok_peers():
    x, y, z, c = position()
    return [
        {"tok": tok_of(y, z + 1, c)},
        {"tok": tok_of(y, z + 3, c)},
        {"tok": tok_of(y + 1, z, c)},
        {"tok": tok_of(y + 3, z, c)},
        {"tok": tok_of(y, z, 1 - c)},
    ]


class RingGather:
    def __init__(self, own, half, ss, rs):
        x = lax.axis_index("blk")
        right, left = x_dev(x, 1), x_dev(x, 3)

        def send(view, src, i, k, dev):
            return rcopy(view, half(src, i), ss(k), rs(k), dev)

        me, lo, hi = x, (x + 3) % 4, (x + 1) % 4
        self.c = [
            send(own(0), me, 0, 0, right),
            send(own(1), me, 1, 1, right),
            send(own(1), me, 1, 2, left),
            send(own(0), me, 0, 3, left),
            send(half(lo, 0), lo, 0, 4, right),
            send(half(hi, 1), hi, 1, 5, left),
        ]

    def start(self):
        for k in (0, 2, 1, 3):
            self.c[k].start()

    def relay(self):
        self.c[0].wait_recv()
        self.c[4].start()
        self.c[2].wait_recv()
        self.c[5].start()

    def wait_near(self):
        self.c[1].wait_recv()
        self.c[3].wait_recv()

    def wait_far(self):
        self.c[4].wait_recv()
        self.c[5].wait_recv()

    def finish(self):
        for c in self.c:
            c.wait_send()


class TokGather:
    OFF = (0, 3, 1, 2)

    def __init__(self, own, slots, view, fs, fr, ss, sr, cs, cr):
        x, y, z, c = position()
        self.first, self.second, self.cross = [], [], []
        sib = {"tok": tok_of(y, z, 1 - c)}
        for h in range(2):

            def tok(d1, d2, h=h):
                return tok_of(y + d2, z + d1, c) if h == 0 else tok_of(y + d1, z + d2, c)

            def slot(d1, d2, tok=tok):
                return slots.at[tok(d1, d2)]

            def half(r, h=h):
                return view(r, h, None)

            def quarter(r, q, h=h):
                return view(r, h, q)

            me = slot(0, 0)
            p1, m1 = {"tok": tok(1, 0)}, {"tok": tok(3, 0)}
            p2, m2 = {"tok": tok(0, 1)}, {"tok": tok(0, 3)}
            self.first.append(
                [
                    rcopy(half(own), half(me), fs.at[h, 0], fr.at[h, 0], p1),
                    rcopy(half(own), half(me), fs.at[h, 1], fr.at[h, 1], m1),
                    rcopy(quarter(slot(3, 0), 0), quarter(slot(3, 0), 0), fs.at[h, 2], fr.at[h, 2], p1),
                    rcopy(quarter(slot(1, 0), 1), quarter(slot(1, 0), 1), fs.at[h, 3], fr.at[h, 3], m1),
                ]
            )
            second = []
            for i, o in enumerate(self.OFF):
                src = half(own) if i == 0 else half(slot(o, 0))
                here, up, dn = half(slot(o, 0)), slot(o, 3), slot(o, 1)
                second.append(
                    [
                        rcopy(src, here, ss.at[h, i, 0], sr.at[h, i, 0], p2),
                        rcopy(src, here, ss.at[h, i, 1], sr.at[h, i, 1], m2),
                        rcopy(quarter(up, 0), quarter(up, 0), ss.at[h, i, 2], sr.at[h, i, 2], p2),
                        rcopy(quarter(dn, 1), quarter(dn, 1), ss.at[h, i, 3], sr.at[h, i, 3], m2),
                    ]
                )
            self.second.append(second)
            cross = []
            for k in range(4):
                row = []
                for i, o in enumerate(self.OFF):
                    dst = half(slot(o, self.OFF[k]))
                    src = half(own) if (i == 0 and k == 0) else dst
                    row.append(rcopy(src, dst, cs.at[h, k, i], cr.at[h, k, i], sib))
                cross.append(row)
            self.cross.append(cross)

    def start(self):
        for h in range(2):
            self.first[h][0].start()
            self.first[h][1].start()
        for h in range(2):
            self._fan(h, 0)

    def _fan(self, h, i):
        self.second[h][i][0].start()
        self.second[h][i][1].start()
        self.cross[h][0][i].start()

    def first_near(self, h):
        f = self.first[h]
        f[0].wait_recv()
        f[2].start()
        self._fan(h, 1)
        f[1].wait_recv()
        f[3].start()
        self._fan(h, 2)

    def first_far(self, h):
        self.first[h][2].wait_recv()
        self.first[h][3].wait_recv()
        self._fan(h, 3)

    def second_near(self, h, i):
        f = self.second[h][i]
        f[0].wait_recv()
        f[2].start()
        self.cross[h][1][i].start()
        f[1].wait_recv()
        f[3].start()
        self.cross[h][2][i].start()

    def second_far(self, h, i):
        f = self.second[h][i]
        f[2].wait_recv()
        f[3].wait_recv()
        self.cross[h][3][i].start()

    def wait_cross(self, h, k):
        for d in self.cross[h][k]:
            d.wait_recv()

    def _all(self):
        for h in range(2):
            for row in self.cross[h]:
                yield from row

    def finish(self):
        for h in range(2):
            for d in self.first[h]:
                d.wait_send()
            for row in self.second[h]:
                for d in row:
                    d.wait_send()
        for d in self._all():
            d.wait_send()


TOK_SEMS = [pltpu.SemaphoreType.DMA((2, 4))] * 2 + [pltpu.SemaphoreType.DMA((2, 4, 4))] * 4


def norm_rows(src, dst, gain, bias, rows, first=0, step=64):
    @pl.loop(0, rows // step)
    def _(i):
        at = pl.ds(pl.multiple_of(first + i * step, step), step)
        v = src[at, :].astype(F32)
        mean = jnp.mean(v, axis=-1, keepdims=True)
        center = v - mean
        spread = jnp.mean(center * center, axis=-1, keepdims=True)
        dst[at, :] = (center * lax.rsqrt(spread + EPS) * gain[...] + bias[...]).astype(dst.dtype)


def pack_rows(v, dst):
    rows, width = v.shape
    full = width // 128
    rest = width - 128 * full
    for i in range(full):
        dst[rows * i : rows * i + rows] = v[:, 128 * i : 128 * i + 128]
    n = 128 // rest
    part = rows // n
    tail = [v[part * q : part * q + part, 128 * full :] for q in range(n)]
    dst[rows * full : rows * full + part] = jnp.concatenate(tail, axis=1)


def unpack_rows(src, rows=256, rest=32):
    n = 128 // rest
    part = rows // n
    full = (src.shape[0] - part) // rows
    last = src[rows * full : rows * full + part]
    tail = jnp.concatenate([last[:, rest * q : rest * q + rest] for q in range(n)], axis=0)
    return jnp.concatenate([src[rows * i : rows * i + rows] for i in range(full)] + [tail], axis=1)


class RingReduce:
    def __init__(self, sbuf, far_in, main_in, ss, rs, half):
        x = lax.axis_index("blk")
        self.hi, self.lo, self.far = (x + 1) % 4, (x + 3) % 4, (x + 2) % 4
        self.sbuf, self.far_in, self.main_in = sbuf, far_in, main_in
        right, left = x_dev(x, 1), x_dev(x, 3)
        self.a, self.b = pl.ds(0, half), pl.ds(half, half)
        a, b = self.a, self.b
        self.c = [
            rcopy(sbuf.at[self.far, a], far_in.at[0], ss(0), rs(0), right),
            rcopy(sbuf.at[self.far, b], far_in.at[1], ss(1), rs(1), left),
            rcopy(sbuf.at[self.hi, b], main_in.at[0, b], ss(2), rs(2), right),
            rcopy(sbuf.at[self.lo, a], main_in.at[1, a], ss(3), rs(3), left),
            rcopy(sbuf.at[self.hi, a], main_in.at[0, a], ss(4), rs(4), right),
            rcopy(sbuf.at[self.lo, b], main_in.at[1, b], ss(5), rs(5), left),
        ]

    def start(self):
        for k in range(4):
            self.c[k].start()

    def relay(self):
        self.c[0].wait_recv()
        s = self.sbuf[self.hi, self.a].astype(F32) + self.far_in[0].astype(F32)
        self.sbuf[self.hi, self.a] = s.astype(BF)
        self.c[1].wait_recv()
        s = self.sbuf[self.lo, self.b].astype(F32) + self.far_in[1].astype(F32)
        self.sbuf[self.lo, self.b] = s.astype(BF)
        self.c[4].start()
        self.c[5].start()

    def wait(self):
        for k in range(2, 6):
            self.c[k].wait_recv()

    def finish(self):
        for d in self.c:
            d.wait_send()


def gelu(v):
    return 0.5 * v * (1.0 + lax.erf(v * (1.0 / math.sqrt(2.0))))


def view_rows(tiles):
    first = 16 * ((tiles + 1) // 2)
    halves = ((0, first), (first, 16 * tiles - first))

    def view(r, h, q):
        start, size = halves[h]
        if q is None:
            return r.at[pl.ds(start, size)]
        lead = 16 * ((size // 16 + 1) // 2)
        return r.at[pl.ds(start, lead)] if q == 0 else r.at[pl.ds(start + lead, size - lead)]

    return view


def k_layer(
    tok, wq, wout, gain1, bias1, qbias, seg, ob, gain2, bias2, fc1, b1, fc2, b2, wp, lo, wpg,
    pack, packo, vec, qb, wo4, toks, qkv, slots, oslots, wps, wof, hb, w1, w2, att, oh, segc, after, hid, own,
    sbuf, far_in, main_in, lsem, rs, rr, ws, wr, as_, ar, xs, xr, *gs
):
    x, y, z, c = position()
    t = lax.axis_index("tok")
    depth = wq.shape[1]
    heads = wq.shape[2] // HD
    nq = 3 * heads
    no = wof.shape[1] // 128
    h2, attf = hb.at[0], hb.at[1]
    mine = segc.at[pl.ds(0, own.shape[1])]
    wf = wof.at[:, pl.ds(0, nq * HPAD)]
    width = tok.shape[1]
    load = [
        pltpu.make_async_copy(fc1, w1, lsem.at[2]),
        pltpu.make_async_copy(fc2, w2, lsem.at[3]),
        pltpu.make_async_copy(wp, wps.at[t], lsem.at[4]),
    ]
    meet(x_peers() + [x_dev(x, 2)] + tok_peers())
    wo_send = [rcopy(wout, wo4.at[x], ws.at[k], wr.at[k], x_dev(x, k + 1)) for k in range(3)]
    for d in wo_send:
        d.start()
    ring = RingGather(
        lambda i: tok.at[pl.ds(128 * i, 128)],
        lambda s, i: toks.at[s, pl.ds(128 * i, 128)],
        lambda k: rs.at[k],
        lambda k: rr.at[k],
    )
    ring.start()
    for i, v in enumerate((gain1, bias1, gain2, bias2, ob, b2, b1)):
        vec[i : i + 1, : v.shape[0]] = v[...].reshape(1, v.shape[0])
    gain1, bias1, gain2, bias2, ob, b2 = [vec.at[i : i + 1, :width] for i in range(6)]
    b1 = vec.at[6:7]
    local = [pltpu.make_async_copy(tok, toks.at[x], lsem.at[0])]
    local[0].start()
    zero = jnp.zeros((depth, HPAD - HD), BF)
    for k in range(3):
        for h in range(heads):
            n = k * heads + h
            piece = wq[k, :, h * HD : h * HD + HD]
            pack[n * depth : n * depth + depth, :] = jnp.concatenate([piece, zero], axis=1)
            qb[:, n * HPAD : n * HPAD + HPAD] = jnp.concatenate(
                [qbias[k : k + 1, h * HD : h * HD + HD], jnp.zeros((1, HPAD - HD), F32)], axis=1
            )
    gath = TokGather(pack, slots, view_rows(pack.shape[0] // 16), *gs[:6])
    gath.start()
    wo4[x] = wout[...]
    for d in wo_send:
        d.wait_recv()
    wide = jnp.concatenate([wo4[b] for b in range(4)], axis=1)
    for n in range(no):
        packo[n * depth : n * depth + depth, :] = wide[:, 128 * n : 128 * n + 128]
    gout = TokGather(packo, oslots, view_rows(packo.shape[0] // 16), *gs[6:12])
    local.append(pltpu.make_async_copy(pack, slots.at[t], lsem.at[1]))
    local[1].start()
    for d in load:
        d.start()
    norm_rows(tok, hb.at[x], gain1, bias1, 256)
    segr = seg[...].astype(F32)
    segc[...] = jnp.broadcast_to(segr, (128, segr.shape[1])).T

    def unpack(g, src, n, dst):
        for i in range(n):
            at = i * depth
            parts = [src[4 * g + j, at : at + depth, :] for j in range(4)]
            rows = pl.ds(pl.multiple_of(g * 208, 16), 208)
            dst[rows, 128 * i : 128 * i + 128] = jnp.concatenate(parts, axis=0)

    def unpack_all(gat, src, n, dst):
        for h in range(2):
            for k in range(4):
                gat.wait_cross(h, k)

        @pl.loop(0, 8)
        def _(g):
            unpack(g, src, n, dst)

    def project(s):
        @pl.loop(0, wf.shape[1] // 256)
        def _(j):
            cols = pl.ds(pl.multiple_of(j * 256, 256), 256)
            v = jnp.dot(hb[s], wf[:, cols], preferred_element_type=F32) + qb[:, cols]
            v = v.astype(BF)
            rows = pl.ds(pl.multiple_of(s * 256, 256), 256)
            qkv[2 * j, rows, :] = v[:, :128]
            qkv[2 * j + 1, rows, :] = v[:, 128:]

    for h in range(2):
        gath.first_near(h)
    for h in range(2):
        gath.first_far(h)
    for i in range(2):
        for h in range(2):
            gath.second_near(h, i)
    ring.relay()
    for i in range(2, 4):
        for h in range(2):
            gath.second_near(h, i)
    gout.start()
    local.append(pltpu.make_async_copy(packo, oslots.at[t], lsem.at[5]))
    local[2].start()
    lo_x, hi_x = (x + 3) % 4, (x + 1) % 4
    norm_rows(toks.at[lo_x], hb.at[lo_x], gain1, bias1, 128)
    norm_rows(toks.at[hi_x], hb.at[hi_x], gain1, bias1, 128, first=128)
    for d in local:
        d.wait()
    ring.wait_near()
    norm_rows(toks.at[lo_x], hb.at[lo_x], gain1, bias1, 128, first=128)
    norm_rows(toks.at[hi_x], hb.at[hi_x], gain1, bias1, 128)
    for i in range(4):
        for h in range(2):
            gath.second_far(h, i)
    for h in range(2):
        gout.first_near(h)
    unpack_all(gath, slots, nq, wf)
    for h in range(2):
        gout.first_far(h)

    @pl.loop(0, 3)
    def _(i):
        project((x + i + i // 2) % 4)

    for i in range(4):
        for h in range(2):
            gout.second_near(h, i)
    merg = TokGather(wp, wps, view_rows(wp.shape[0] // 16), *gs[12:])
    merg.start()
    ring.wait_far()
    far = (x + 2) % 4
    norm_rows(toks.at[far], hb.at[far], gain1, bias1, 256)
    project(far)
    scale = 1.0 / math.sqrt(HD)
    half = att.shape[2] // 2

    def attend(r):
        @pl.loop(0, 2)
        def _(sub):
            rows = pl.ds(pl.multiple_of(r * 256 + sub * 128, 128), 128)
            same = segc[rows, 0:1] == segr
            for h in range(heads):
                s = lax.dot_general(
                    qkv[h, rows, :], qkv[heads + h], (((1,), (1,)), ((), ())), preferred_element_type=F32
                )
                p = jnp.where(same, jnp.exp(s * scale), 0.0)
                total = jnp.sum(p, axis=-1, keepdims=True)
                o = jnp.dot(p.astype(BF), qkv[2 * heads + h], preferred_element_type=F32) / total
                oh[h, pl.ds(pl.multiple_of(sub * 128, 128), 128), :] = o.astype(BF)

        pack_rows(jnp.concatenate([oh[h][:, :HD] for h in range(heads)], axis=1), att.at[x, r])

    def gather_ring(r):
        def part(s, i):
            return att.at[s, r, pl.ds(half * i, half)]

        return RingGather(lambda i: part(x, i), part, lambda k: as_.at[r, k], lambda k: ar.at[r, k])

    def reduce_ring(r):
        return RingReduce(
            sbuf.at[r],
            far_in.at[r],
            main_in.at[r],
            lambda k: xs.at[r, k],
            lambda k: xr.at[r, k],
            half,
        )

    attend(0)
    gather_ring(0).start()
    for i in range(4):
        for h in range(2):
            gout.second_far(h, i)
    attend(1)
    gather_ring(0).relay()
    gather_ring(1).start()
    for h in range(2):
        merg.first_near(h)
    attend(2)
    gather_ring(1).relay()
    gather_ring(2).start()
    for h in range(2):
        merg.first_far(h)
    attend(3)
    gather_ring(2).relay()
    gather_ring(3).start()
    unpack_all(gout, oslots, no, wof)
    save = pltpu.make_async_copy(wps, wpg, lsem.at[0])
    tiles = [(n, min(256, 1664 - n)) for n in range(0, 1664, 256)]
    @pl.loop(0, 6)
    def _(r):
        @pl.when(r < 4)
        def _():
            rg = gather_ring(r)
            rg.wait_near()
            rg.wait_far()
            attf[...] = jnp.concatenate([unpack_rows(att.at[b, r]) for b in range(4)], axis=1)
            for n, w in tiles:
                acc = lax.dot_general(
                    attf[...], wof[n : n + w, :], (((1,), (1,)), ((), ())), preferred_element_type=F32
                )
                after[:, n : n + w] = acc + toks[r, :, n : n + w].astype(F32) + ob[:, n : n + w]

            @pl.when(r == 0)
            def _():
                gather_ring(3).relay()
                load[0].wait()

            @pl.when(r > 0)
            def _():
                reduce_ring(r - 1).relay()

            @pl.when(r == 1)
            def _():
                for i in range(4):
                    for h in range(2):
                        merg.second_near(h, i)

            @pl.when(r == 3)
            def _():
                for i in range(4):
                    for h in range(2):
                        merg.second_far(h, i)

            norm_rows(after, h2, gain2, bias2, 256)
            for j in range(4):

                @pl.when(x == j)
                def _():
                    pack_rows(after[:, 416 * j : 416 * j + 416] + b2[:, 416 * j : 416 * j + 416], own.at[r])

            for j in range(8):
                cols = slice(256 * j, 256 * j + 256)
                v = jnp.dot(h2[...], w1[:, cols], preferred_element_type=F32) + b1[:, cols]
                hid[:, cols] = gelu(v).astype(BF)

            @pl.when(r == 0)
            def _():
                load[1].wait()

            for n, w in tiles:
                after[:, n : n + w] = jnp.dot(hid[...], w2[:, n : n + w], preferred_element_type=F32)
            for j in range(4):
                piece = after[:, 416 * j : 416 * j + 416]
                pack_rows(piece.astype(BF), sbuf.at[r, j])

                @pl.when(x == j)
                def _():
                    pack_rows(piece, mine)
                    own[r] += mine[...]

            reduce_ring(r).start()

        @pl.when(r == 4)
        def _():
            reduce_ring(3).relay()
            load[2].wait()
            for h in range(2):
                for k in range(4):
                    merg.wait_cross(h, k)
            save.start()

        @pl.when(r > 1)
        def _():
            q = r - 2
            rg = reduce_ring(q)
            rg.wait()
            total = own[q] + main_in[q, 0].astype(F32) + main_in[q, 1].astype(F32)
            lo[q] = total.astype(BF)
            rg.finish()
            gather_ring(q).finish()

    save.wait()
    for d in wo_send:
        d.wait_send()
    ring.finish()
    gath.finish()
    gout.finish()
    merg.finish()


def column(rows):
    n, m = rows.shape
    return jnp.concatenate([rows, jnp.zeros((128 - n, m), F32)], axis=0).T


def k_merge(
    lo, gain3, bias3, mi, seg, owners, wpg_h, pb, out,
    wpg, rows_f, fin, gb, sbuf, own, far_in, main_in, st, placed, obuf, lsem, ss, sr, xs, xr, ts, tr
):
    x, y, z, c = position()
    t = lax.axis_index("tok")
    n_tok = out.shape[0]
    slot = out.shape[1]
    merged = mi.shape[1]
    n_loc = wpg.shape[2]
    load = pltpu.make_async_copy(wpg_h, wpg, lsem.at[0])
    load.start()
    bar = pltpu.get_barrier_semaphore()

    @pl.loop(1, n_tok)
    def _(i):
        pl.semaphore_signal(bar, inc=1, device_id={"tok": (t + i) % n_tok}, device_id_type=MESH_ID)

    @pl.loop(1, 4)
    def _(i):
        pl.semaphore_signal(bar, inc=1, device_id=x_dev(x, i), device_id_type=MESH_ID)

    @pl.loop(0, 4)
    def _(i):
        rows = pl.ds(pl.multiple_of(i * 256, 256), 256)
        v = unpack_rows(lo.at[i]).astype(F32)
        rows_f[rows, :] = v
        mean = jnp.mean(v, axis=-1, keepdims=True)
        d = v - mean
        m2 = jnp.sum(d * d, axis=-1, keepdims=True)
        lane = lax.broadcasted_iota(jnp.int32, (256, 128), 1)
        both = jnp.where(lane == 0, mean, jnp.where(lane == 1, m2, 0.0))
        st[x, :, rows] = both.T[:8]

    pl.semaphore_wait(bar, n_tok + 2)
    sends = [rcopy(st.at[x], st.at[x], ss.at[k], sr.at[k], x_dev(x, k + 1)) for k in range(3)]
    for d in sends:
        d.start()
    for j in range(4):

        @pl.when(x == j)
        def _():
            gb[0:1, :] = gain3[n_loc * j : n_loc * j + n_loc].reshape(1, n_loc)
            gb[1:2, :] = bias3[n_loc * j : n_loc * j + n_loc].reshape(1, n_loc)

    idx = column(mi[...].astype(F32))
    toks = lax.broadcasted_iota(jnp.int32, (merged, 1024), 1).astype(F32)
    seg_of = jnp.sum(jnp.where(idx[:, 0:1] == toks, seg[...].astype(F32), 0.0), axis=1, keepdims=True)
    names = lax.broadcasted_iota(jnp.int32, (merged, n_tok), 1).astype(F32)
    owner = jnp.sum(jnp.where(seg_of == names, owners[...].astype(F32), 0.0), axis=1, keepdims=True)
    mine = (owner == names).astype(F32)
    below = lax.broadcasted_iota(jnp.int32, (merged, merged), 1) < lax.broadcasted_iota(
        jnp.int32, (merged, merged), 0
    )
    before = jnp.dot(
        jnp.where(below, 1.0, 0.0).astype(BF), mine.astype(BF), preferred_element_type=F32
    )
    rank = jnp.sum(before * mine, axis=1, keepdims=True)
    target = jnp.broadcast_to(owner * slot + rank, (merged, 128)).T[0:1]
    spots = lax.broadcasted_iota(jnp.int32, (n_tok * slot, merged), 0).astype(F32)
    placed[...] = jnp.where(spots == target, 1.0, 0.0).astype(BF)
    for d in sends:
        d.wait_recv()
    means = [st[s, 0:1, :] for s in range(4)]
    mean = 0.25 * (means[0] + means[1] + means[2] + means[3])
    m2 = st[0, 1:2, :] + st[1, 1:2, :] + st[2, 1:2, :] + st[3, 1:2, :]
    for s in range(4):
        d = means[s] - mean
        m2 = m2 + n_loc * (d * d)
    rstd = lax.rsqrt(m2 * (1.0 / (4 * n_loc)) + EPS)
    for i in range(8):
        sl = slice(128 * i, 128 * i + 128)
        row = lax.broadcasted_iota(jnp.int32, (128, 128), 0)
        cols = jnp.where(row == 0, mean[:, sl], jnp.where(row == 1, rstd[:, sl], 0.0)).T
        v = rows_f[sl, :]
        fin[sl, :] = ((v - cols[:, 0:1]) * cols[:, 1:2] * gb[0:1, :] + gb[1:2, :]).astype(BF)
    load.wait()
    got = []
    for k in range(4):
        pick = jnp.where(idx[:, k : k + 1] == toks, 1.0, 0.0).astype(BF)
        got.append(jnp.dot(pick, fin[...], preferred_element_type=F32).astype(BF))
    for j in range(4):
        acc = jnp.dot(got[0], wpg[j], preferred_element_type=F32)
        for k in range(1, 4):
            acc += jnp.dot(got[k], wpg[k * 4 + j], preferred_element_type=F32)
        pack_rows(acc, own.at[j])
        sbuf[j] = own[j].astype(BF)
    rg = RingReduce(sbuf, far_in, main_in, lambda k: xs.at[k], lambda k: xr.at[k], sbuf.shape[1] // 2)
    rg.start()
    rg.relay()
    rg.wait()
    own[x] += main_in[0].astype(F32) + main_in[1].astype(F32)
    total = unpack_rows(own.at[x]) + pb[...]
    going = jnp.dot(placed[...], total.astype(BF), preferred_element_type=F32).astype(BF)
    obuf[...] = going.reshape(n_tok, slot, n_loc)

    def slot_copy(i):
        to = (t + i) % n_tok
        return rcopy(obuf.at[to], out.at[t], ts.at[i], tr.at[i], {"tok": to})

    @pl.loop(1, n_tok)
    def _(i):
        slot_copy(i).start()

    keep = pltpu.make_async_copy(obuf.at[t], out.at[t], lsem.at[1])
    keep.start()
    rg.finish()
    for d in sends:
        d.wait_send()
    keep.wait()

    @pl.loop(1, n_tok)
    def _(i):
        slot_copy(i).wait()


def kernel_call(body, name, cid, ins, outs, out_specs, scratch, args):
    return pl.pallas_call(
        body,
        name=name,
        out_shape=outs,
        in_specs=ins,
        out_specs=out_specs,
        scratch_shapes=scratch,
        compiler_params=pltpu.CompilerParams(
            collective_id=cid, has_side_effects=True, vmem_limit_bytes=VLIM
        ),
    )(*args)


def sds(shape, dtype):
    return jax.ShapeDtypeStruct(shape, dtype)


DMA = pltpu.SemaphoreType.DMA


def body(
    tokens,
    segment_ids,
    merge_index,
    segment_owner,
    ln1_gain,
    ln1_bias,
    w_qkv,
    qkv_bias,
    w_out,
    out_bias,
    ln2_gain,
    ln2_bias,
    w_fc1,
    fc1_bias,
    w_fc2,
    fc2_bias,
    ln3_gain,
    ln3_bias,
    w_proj,
    proj_bias,
):
    tok = tokens[0]
    width = tok.shape[1]
    part_w = w_qkv.shape[2]
    depth = w_qkv.shape[1]
    heads = part_w // HD
    cols = 3 * heads * HPAD

    def tall(n):
        return 16 * (-(-(n // 128) * depth // 16))

    hidden = w_fc1.shape[1]
    flat = 256 * part_w // 128
    perm = []
    for bx in range(4):
        for t in range(32):
            ty, tz, tc = t // 8, (t // 2) % 4, t % 2
            perm.append((bx * 32 + t, tz * 32 + (ty * 4 + bx) * 2 + tc))
    wp = lax.ppermute(w_proj, ("blk", "tok"), perm)
    lo, wpg = kernel_call(
        k_layer,
        "layer",
        1,
        [VM] * 10 + [ANY, VM, ANY, VM, VM],
        [sds((4, flat, 128), BF), sds((32, 208, part_w), BF)],
        [VM, ANY],
        [
            pltpu.VMEM((tall(cols), 128), BF),
            pltpu.VMEM((tall(width), 128), BF),
            pltpu.VMEM((8, hidden), F32),
            pltpu.VMEM((1, cols), F32),
            pltpu.VMEM((4, depth, part_w), BF),
            pltpu.VMEM((4, 256, width), BF),
            pltpu.VMEM((3 * heads, 1024, HPAD), BF),
            pltpu.VMEM((32, tall(cols), 128), BF),
            pltpu.VMEM((32, tall(width), 128), BF),
            pltpu.VMEM((32, 208, part_w), BF),
            pltpu.VMEM((width, width), BF),
            pltpu.VMEM((4, 256, width), BF),
            pltpu.VMEM((width, hidden), BF),
            pltpu.VMEM((hidden, width), BF),
            pltpu.VMEM((4, 4, flat, 128), BF),
            pltpu.VMEM((heads, 256, HPAD), BF),
            pltpu.VMEM((1024, 128), F32),
            pltpu.VMEM((256, width), F32),
            pltpu.VMEM((256, hidden), BF),
            pltpu.VMEM((4, flat, 128), F32),
            pltpu.VMEM((4, 4, flat, 128), BF),
            pltpu.VMEM((4, 2, flat // 2, 128), BF),
            pltpu.VMEM((4, 2, flat, 128), BF),
            DMA((6,)),
            DMA((6,)),
            DMA((6,)),
            DMA((3,)),
            DMA((3,)),
            DMA((4, 6)),
            DMA((4, 6)),
            DMA((4, 6)),
            DMA((4, 6)),
        ]
        + TOK_SEMS * 3,
        (
            tok, w_qkv, w_out.T, ln1_gain, ln1_bias, qkv_bias, segment_ids, out_bias, ln2_gain,
            ln2_bias, w_fc1, fc1_bias, w_fc2, fc2_bias, wp,
        ),
    )
    merged_count = merge_index.shape[1]
    n_tok = lax.axis_size("tok")
    slot = 2 * merged_count // n_tok
    arrived = kernel_call(
        k_merge,
        "merge",
        3,
        [VM] * 6 + [ANY, VM],
        [sds((n_tok, slot, part_w), BF)],
        [VM],
        [
            pltpu.VMEM((16, part_w, part_w), BF),
            pltpu.VMEM((1024, part_w), F32),
            pltpu.VMEM((1024, part_w), BF),
            pltpu.VMEM((2, part_w), F32),
            pltpu.VMEM((4, flat, 128), BF),
            pltpu.VMEM((4, flat, 128), F32),
            pltpu.VMEM((2, flat // 2, 128), BF),
            pltpu.VMEM((2, flat, 128), BF),
            pltpu.VMEM((4, 8, 1024), F32),
            pltpu.VMEM((n_tok * slot, merged_count), BF),
            pltpu.VMEM((n_tok, slot, part_w), BF),
            DMA((2,)),
            DMA((3,)),
            DMA((3,)),
            DMA((6,)),
            DMA((6,)),
            DMA((n_tok,)),
            DMA((n_tok,)),
        ],
        (
            lo,
            ln3_gain,
            ln3_bias,
            merge_index[0].T,
            segment_ids,
            segment_owner,
            wpg.reshape(16, part_w, part_w),
            proj_bias,
        ),
    )[0]
    return arrived[None]


def solution(mesh):
    placed = (
        P("tok", "blk", None),
        P("tok", None),
        P("tok", None, None),
        P("tok", None),
        P(),
        P(),
        P(None, "tok", "blk"),
        P(None, "blk"),
        P("blk", "tok"),
        P(),
        P(),
        P(),
        P(None, "blk"),
        P("blk"),
        P("blk", None),
        P(),
        P(),
        P(),
        P("tok", "blk"),
        P("blk"),
    )
    return jax.shard_map(
        body, mesh=mesh, in_specs=placed, out_specs=P("tok", None, None, "blk"), check_vma=False
    )
```

```python
import math

import jax
import jax.numpy as jnp
from jax import lax
from jax.experimental import pallas as pl
from jax.experimental.pallas import tpu as pltpu
from jax.sharding import PartitionSpec as P

HD = 104
HPAD = 128
EPS = 1e-06
BF = jnp.bfloat16
F32 = jnp.float32
MESH_ID = pl.DeviceIdType.MESH
VLIM = 64600 * 1024
VM = pl.BlockSpec(memory_space=pltpu.VMEM)
ANY = pl.BlockSpec(memory_space=pl.ANY)


def position():
    x = lax.axis_index("blk")
    t = lax.axis_index("tok")
    return x, t // 8, (t // 2) % 4, t % 2


def tok_of(y, z, c):
    return ((y % 4) * 4 + z % 4) * 2 + c


def rcopy(src, dst, ssem, rsem, dev):
    return pltpu.make_async_remote_copy(
        src_ref=src, dst_ref=dst, send_sem=ssem, recv_sem=rsem, device_id=dev, device_id_type=MESH_ID
    )


def x_dev(x, off):
    return {"blk": (x + off) % 4}


def meet(peers):
    bar = pltpu.get_barrier_semaphore()
    for dev in peers:
        pl.semaphore_signal(bar, inc=1, device_id=dev, device_id_type=MESH_ID)
    pl.semaphore_wait(bar, len(peers))


def x_peers():
    x, y, z, c = position()
    return [x_dev(x, 1), x_dev(x, 3)]


def tok_peers():
    x, y, z, c = position()
    return [
        {"tok": tok_of(y, z + 1, c)},
        {"tok": tok_of(y, z + 3, c)},
        {"tok": tok_of(y + 1, z, c)},
        {"tok": tok_of(y + 3, z, c)},
        {"tok": tok_of(y, z, 1 - c)},
    ]


class RingGather:
    def __init__(self, own, half, ss, rs):
        x = lax.axis_index("blk")
        right, left = x_dev(x, 1), x_dev(x, 3)

        def send(view, src, i, k, dev):
            return rcopy(view, half(src, i), ss(k), rs(k), dev)

        me, lo, hi = x, (x + 3) % 4, (x + 1) % 4
        self.c = [
            send(own(0), me, 0, 0, right),
            send(own(1), me, 1, 1, right),
            send(own(1), me, 1, 2, left),
            send(own(0), me, 0, 3, left),
            send(half(lo, 0), lo, 0, 4, right),
            send(half(hi, 1), hi, 1, 5, left),
        ]

    def start(self):
        for k in (0, 2, 1, 3):
            self.c[k].start()

    def relay(self):
        self.c[0].wait_recv()
        self.c[4].start()
        self.c[2].wait_recv()
        self.c[5].start()

    def wait_near(self):
        self.c[1].wait_recv()
        self.c[3].wait_recv()

    def wait_far(self):
        self.c[4].wait_recv()
        self.c[5].wait_recv()

    def finish(self):
        for c in self.c:
            c.wait_send()


class TokGather:
    OFF = (0, 3, 1, 2)

    def __init__(self, own, slots, view, fs, fr, ss, sr, cs, cr):
        x, y, z, c = position()
        self.first, self.second, self.cross = [], [], []
        sib = {"tok": tok_of(y, z, 1 - c)}
        for h in range(2):

            def tok(d1, d2, h=h):
                return tok_of(y + d2, z + d1, c) if h == 0 else tok_of(y + d1, z + d2, c)

            def slot(d1, d2, tok=tok):
                return slots.at[tok(d1, d2)]

            def half(r, h=h):
                return view(r, h, None)

            def quarter(r, q, h=h):
                return view(r, h, q)

            me = slot(0, 0)
            p1, m1 = {"tok": tok(1, 0)}, {"tok": tok(3, 0)}
            p2, m2 = {"tok": tok(0, 1)}, {"tok": tok(0, 3)}
            self.first.append(
                [
                    rcopy(half(own), half(me), fs.at[h, 0], fr.at[h, 0], p1),
                    rcopy(half(own), half(me), fs.at[h, 1], fr.at[h, 1], m1),
                    rcopy(quarter(slot(3, 0), 0), quarter(slot(3, 0), 0), fs.at[h, 2], fr.at[h, 2], p1),
                    rcopy(quarter(slot(1, 0), 1), quarter(slot(1, 0), 1), fs.at[h, 3], fr.at[h, 3], m1),
                ]
            )
            second = []
            for i, o in enumerate(self.OFF):
                src = half(own) if i == 0 else half(slot(o, 0))
                here, up, dn = half(slot(o, 0)), slot(o, 3), slot(o, 1)
                second.append(
                    [
                        rcopy(src, here, ss.at[h, i, 0], sr.at[h, i, 0], p2),
                        rcopy(src, here, ss.at[h, i, 1], sr.at[h, i, 1], m2),
                        rcopy(quarter(up, 0), quarter(up, 0), ss.at[h, i, 2], sr.at[h, i, 2], p2),
                        rcopy(quarter(dn, 1), quarter(dn, 1), ss.at[h, i, 3], sr.at[h, i, 3], m2),
                    ]
                )
            self.second.append(second)
            cross = []
            for k in range(4):
                row = []
                for i, o in enumerate(self.OFF):
                    dst = half(slot(o, self.OFF[k]))
                    src = half(own) if (i == 0 and k == 0) else dst
                    row.append(rcopy(src, dst, cs.at[h, k, i], cr.at[h, k, i], sib))
                cross.append(row)
            self.cross.append(cross)

    def start(self):
        for h in range(2):
            self.first[h][0].start()
            self.first[h][1].start()
        for h in range(2):
            self._fan(h, 0)

    def _fan(self, h, i):
        self.second[h][i][0].start()
        self.second[h][i][1].start()
        self.cross[h][0][i].start()

    def first_near(self, h):
        f = self.first[h]
        f[0].wait_recv()
        f[2].start()
        self._fan(h, 1)
        f[1].wait_recv()
        f[3].start()
        self._fan(h, 2)

    def first_far(self, h):
        self.first[h][2].wait_recv()
        self.first[h][3].wait_recv()
        self._fan(h, 3)

    def second_near(self, h, i):
        f = self.second[h][i]
        f[0].wait_recv()
        f[2].start()
        self.cross[h][1][i].start()
        f[1].wait_recv()
        f[3].start()
        self.cross[h][2][i].start()

    def second_far(self, h, i):
        f = self.second[h][i]
        f[2].wait_recv()
        f[3].wait_recv()
        self.cross[h][3][i].start()

    def wait_cross(self, h, k):
        for d in self.cross[h][k]:
            d.wait_recv()

    def _all(self):
        for h in range(2):
            for row in self.cross[h]:
                yield from row

    def finish(self):
        for h in range(2):
            for d in self.first[h]:
                d.wait_send()
            for row in self.second[h]:
                for d in row:
                    d.wait_send()
        for d in self._all():
            d.wait_send()


TOK_SEMS = [pltpu.SemaphoreType.DMA((2, 4))] * 2 + [pltpu.SemaphoreType.DMA((2, 4, 4))] * 4


def norm_rows(src, dst, gain, bias, rows, first=0, step=64):
    @pl.loop(0, rows // step)
    def _(i):
        at = pl.ds(pl.multiple_of(first + i * step, step), step)
        v = src[at, :].astype(F32)
        mean = jnp.mean(v, axis=-1, keepdims=True)
        center = v - mean
        spread = jnp.mean(center * center, axis=-1, keepdims=True)
        dst[at, :] = (center * lax.rsqrt(spread + EPS) * gain[...] + bias[...]).astype(dst.dtype)


def pack_rows(v, dst):
    rows, width = v.shape
    full = width // 128
    rest = width - 128 * full
    for i in range(full):
        dst[rows * i : rows * i + rows] = v[:, 128 * i : 128 * i + 128]
    n = 128 // rest
    part = rows // n
    tail = [v[part * q : part * q + part, 128 * full :] for q in range(n)]
    dst[rows * full : rows * full + part] = jnp.concatenate(tail, axis=1)


def unpack_rows(src, rows=256, rest=32):
    n = 128 // rest
    part = rows // n
    full = (src.shape[0] - part) // rows
    last = src[rows * full : rows * full + part]
    tail = jnp.concatenate([last[:, rest * q : rest * q + rest] for q in range(n)], axis=0)
    return jnp.concatenate([src[rows * i : rows * i + rows] for i in range(full)] + [tail], axis=1)


class RingReduce:
    def __init__(self, sbuf, far_in, main_in, ss, rs, half):
        x = lax.axis_index("blk")
        self.hi, self.lo, self.far = (x + 1) % 4, (x + 3) % 4, (x + 2) % 4
        self.sbuf, self.far_in, self.main_in = sbuf, far_in, main_in
        right, left = x_dev(x, 1), x_dev(x, 3)
        self.a, self.b = pl.ds(0, half), pl.ds(half, half)
        a, b = self.a, self.b
        self.c = [
            rcopy(sbuf.at[self.far, a], far_in.at[0], ss(0), rs(0), right),
            rcopy(sbuf.at[self.far, b], far_in.at[1], ss(1), rs(1), left),
            rcopy(sbuf.at[self.hi, b], main_in.at[0, b], ss(2), rs(2), right),
            rcopy(sbuf.at[self.lo, a], main_in.at[1, a], ss(3), rs(3), left),
            rcopy(sbuf.at[self.hi, a], main_in.at[0, a], ss(4), rs(4), right),
            rcopy(sbuf.at[self.lo, b], main_in.at[1, b], ss(5), rs(5), left),
        ]

    def start(self):
        for k in range(4):
            self.c[k].start()

    def relay(self):
        self.c[0].wait_recv()
        s = self.sbuf[self.hi, self.a].astype(F32) + self.far_in[0].astype(F32)
        self.sbuf[self.hi, self.a] = s.astype(BF)
        self.c[1].wait_recv()
        s = self.sbuf[self.lo, self.b].astype(F32) + self.far_in[1].astype(F32)
        self.sbuf[self.lo, self.b] = s.astype(BF)
        self.c[4].start()
        self.c[5].start()

    def wait(self):
        for k in range(2, 6):
            self.c[k].wait_recv()

    def finish(self):
        for d in self.c:
            d.wait_send()


def gelu(v):
    return 0.5 * v * (1.0 + lax.erf(v * (1.0 / math.sqrt(2.0))))


def view_rows(tiles):
    first = 16 * ((tiles + 1) // 2)
    halves = ((0, first), (first, 16 * tiles - first))

    def view(r, h, q):
        start, size = halves[h]
        if q is None:
            return r.at[pl.ds(start, size)]
        lead = 16 * ((size // 16 + 1) // 2)
        return r.at[pl.ds(start, lead)] if q == 0 else r.at[pl.ds(start + lead, size - lead)]

    return view


def k_layer(
    tok, wq, wout, gain1, bias1, qbias, seg, ob, gain2, bias2, fc1, b1, fc2, b2, wp, lo, wpg,
    pack, packo, vec, qb, wo4, toks, qkv, slots, oslots, wps, wof, hb, w1, w2, att, oh, segc, after, hid, own,
    sbuf, far_in, main_in, lsem, rs, rr, ws, wr, as_, ar, xs, xr, *gs
):
    x, y, z, c = position()
    t = lax.axis_index("tok")
    depth = wq.shape[1]
    heads = wq.shape[2] // HD
    nq = 3 * heads
    no = wof.shape[1] // 128
    h2, attf = hb.at[0], hb.at[1]
    mine = segc.at[pl.ds(0, own.shape[1])]
    wf = wof.at[:, pl.ds(0, nq * HPAD)]
    width = tok.shape[1]
    load = [
        pltpu.make_async_copy(fc1, w1, lsem.at[2]),
        pltpu.make_async_copy(fc2, w2, lsem.at[3]),
        pltpu.make_async_copy(wp, wps.at[t], lsem.at[4]),
    ]
    meet(x_peers() + [x_dev(x, 2)] + tok_peers())
    wo_send = [rcopy(wout, wo4.at[x], ws.at[k], wr.at[k], x_dev(x, k + 1)) for k in range(3)]
    for d in wo_send:
        d.start()
    ring = RingGather(
        lambda i: tok.at[pl.ds(128 * i, 128)],
        lambda s, i: toks.at[s, pl.ds(128 * i, 128)],
        lambda k: rs.at[k],
        lambda k: rr.at[k],
    )
    ring.start()
    for i, v in enumerate((gain1, bias1, gain2, bias2, ob, b2, b1)):
        vec[i : i + 1, : v.shape[0]] = v[...].reshape(1, v.shape[0])
    gain1, bias1, gain2, bias2, ob, b2 = [vec.at[i : i + 1, :width] for i in range(6)]
    b1 = vec.at[6:7]
    local = [pltpu.make_async_copy(tok, toks.at[x], lsem.at[0])]
    local[0].start()
    zero = jnp.zeros((depth, HPAD - HD), BF)
    for k in range(3):
        for h in range(heads):
            n = k * heads + h
            piece = wq[k, :, h * HD : h * HD + HD]
            pack[n * depth : n * depth + depth, :] = jnp.concatenate([piece, zero], axis=1)
            qb[:, n * HPAD : n * HPAD + HPAD] = jnp.concatenate(
                [qbias[k : k + 1, h * HD : h * HD + HD], jnp.zeros((1, HPAD - HD), F32)], axis=1
            )
    gath = TokGather(pack, slots, view_rows(pack.shape[0] // 16), *gs[:6])
    gath.start()
    wo4[x] = wout[...]
    for d in wo_send:
        d.wait_recv()
    wide = jnp.concatenate([wo4[b] for b in range(4)], axis=1)
    for n in range(no):
        packo[n * depth : n * depth + depth, :] = wide[:, 128 * n : 128 * n + 128]
    gout = TokGather(packo, oslots, view_rows(packo.shape[0] // 16), *gs[6:12])
    local.append(pltpu.make_async_copy(pack, slots.at[t], lsem.at[1]))
    local[1].start()
    for d in load:
        d.start()
    norm_rows(tok, hb.at[x], gain1, bias1, 256)
    segr = seg[...].astype(F32)
    segc[...] = jnp.broadcast_to(segr, (128, segr.shape[1])).T

    def unpack(g, src, n, dst):
        for i in range(n):
            at = i * depth
            parts = [src[4 * g + j, at : at + depth, :] for j in range(4)]
            rows = pl.ds(pl.multiple_of(g * 208, 16), 208)
            dst[rows, 128 * i : 128 * i + 128] = jnp.concatenate(parts, axis=0)

    def unpack_all(gat, src, n, dst):
        for h in range(2):
            for k in range(4):
                gat.wait_cross(h, k)

        @pl.loop(0, 8)
        def _(g):
            unpack(g, src, n, dst)

    def project(sources):
        @pl.loop(0, wf.shape[1] // 256)
        def _(j):
            cols = pl.ds(pl.multiple_of(j * 256, 256), 256)
            for s in sources:
                v = jnp.dot(hb[s], wf[:, cols], preferred_element_type=F32) + qb[:, cols]
                v = v.astype(BF)
                rows = pl.ds(pl.multiple_of(s * 256, 256), 256)
                qkv[2 * j, rows, :] = v[:, :128]
                qkv[2 * j + 1, rows, :] = v[:, 128:]

    for h in range(2):
        gath.first_near(h)
    for h in range(2):
        gath.first_far(h)
    for i in range(2):
        for h in range(2):
            gath.second_near(h, i)
    ring.relay()
    for i in range(2, 4):
        for h in range(2):
            gath.second_near(h, i)
    gout.start()
    local.append(pltpu.make_async_copy(packo, oslots.at[t], lsem.at[5]))
    local[2].start()
    lo_x, hi_x = (x + 3) % 4, (x + 1) % 4
    norm_rows(toks.at[lo_x], hb.at[lo_x], gain1, bias1, 128)
    norm_rows(toks.at[hi_x], hb.at[hi_x], gain1, bias1, 128, first=128)
    for d in local:
        d.wait()
    ring.wait_near()
    norm_rows(toks.at[lo_x], hb.at[lo_x], gain1, bias1, 128, first=128)
    norm_rows(toks.at[hi_x], hb.at[hi_x], gain1, bias1, 128)
    for i in range(4):
        for h in range(2):
            gath.second_far(h, i)
    for h in range(2):
        gout.first_near(h)
    unpack_all(gath, slots, nq, wf)
    for h in range(2):
        gout.first_far(h)

    project([x, hi_x, lo_x])

    for i in range(4):
        for h in range(2):
            gout.second_near(h, i)
    merg = TokGather(wp, wps, view_rows(wp.shape[0] // 16), *gs[12:])
    merg.start()
    ring.wait_far()
    far = (x + 2) % 4
    norm_rows(toks.at[far], hb.at[far], gain1, bias1, 256)
    project([far])
    scale = 1.0 / math.sqrt(HD)
    half = att.shape[2] // 2

    def attend(r):
        @pl.loop(0, 2)
        def _(sub):
            rows = pl.ds(pl.multiple_of(r * 256 + sub * 128, 128), 128)
            same = segc[rows, 0:1] == segr
            for h in range(heads):
                s = lax.dot_general(
                    qkv[h, rows, :], qkv[heads + h], (((1,), (1,)), ((), ())), preferred_element_type=F32
                )
                p = jnp.where(same, jnp.exp(s * scale), 0.0)
                total = jnp.sum(p, axis=-1, keepdims=True)
                o = jnp.dot(p.astype(BF), qkv[2 * heads + h], preferred_element_type=F32) / total
                oh[h, pl.ds(pl.multiple_of(sub * 128, 128), 128), :] = o.astype(BF)

        pack_rows(jnp.concatenate([oh[h][:, :HD] for h in range(heads)], axis=1), att.at[x, r])

    def gather_ring(r):
        def part(s, i):
            return att.at[s, r, pl.ds(half * i, half)]

        return RingGather(lambda i: part(x, i), part, lambda k: as_.at[r, k], lambda k: ar.at[r, k])

    def reduce_ring(r):
        return RingReduce(
            sbuf.at[r],
            far_in.at[r],
            main_in.at[r],
            lambda k: xs.at[r, k],
            lambda k: xr.at[r, k],
            half,
        )

    attend(0)
    gather_ring(0).start()
    for i in range(4):
        for h in range(2):
            gout.second_far(h, i)
    attend(1)
    gather_ring(0).relay()
    gather_ring(1).start()
    for h in range(2):
        merg.first_near(h)
    attend(2)
    gather_ring(1).relay()
    gather_ring(2).start()
    for h in range(2):
        merg.first_far(h)
    attend(3)
    gather_ring(2).relay()
    gather_ring(3).start()
    unpack_all(gout, oslots, no, wof)
    for i in range(4):
        for h in range(2):
            merg.second_near(h, i)
    save = pltpu.make_async_copy(wps, wpg, lsem.at[0])
    tiles = [(n, min(256, 1664 - n)) for n in range(0, 1664, 256)]
    @pl.loop(0, 6)
    def _(r):
        @pl.when(r < 4)
        def _():
            rg = gather_ring(r)
            rg.wait_near()
            rg.wait_far()
            attf[...] = jnp.concatenate([unpack_rows(att.at[b, r]) for b in range(4)], axis=1)
            for n, w in tiles:
                acc = lax.dot_general(
                    attf[...], wof[n : n + w, :], (((1,), (1,)), ((), ())), preferred_element_type=F32
                )
                after[:, n : n + w] = acc + toks[r, :, n : n + w].astype(F32) + ob[:, n : n + w]

            @pl.when(r == 0)
            def _():
                gather_ring(3).relay()
                load[0].wait()

            @pl.when(r > 0)
            def _():
                reduce_ring(r - 1).relay()

            @pl.when(r == 2)
            def _():
                for i in range(4):
                    for h in range(2):
                        merg.second_far(h, i)

            norm_rows(after, h2, gain2, bias2, 256)
            for j in range(4):

                @pl.when(x == j)
                def _():
                    pack_rows(after[:, 416 * j : 416 * j + 416] + b2[:, 416 * j : 416 * j + 416], own.at[r])

            for j in range(8):
                cols = slice(256 * j, 256 * j + 256)
                v = jnp.dot(h2[...], w1[:, cols], preferred_element_type=F32) + b1[:, cols]
                hid[:, cols] = gelu(v).astype(BF)

            @pl.when(r == 0)
            def _():
                load[1].wait()

            for n, w in tiles:
                after[:, n : n + w] = jnp.dot(hid[...], w2[:, n : n + w], preferred_element_type=F32)
            for j in range(4):
                piece = after[:, 416 * j : 416 * j + 416]
                pack_rows(piece.astype(BF), sbuf.at[r, j])

                @pl.when(x == j)
                def _():
                    pack_rows(piece, mine)
                    own[r] += mine[...]

            reduce_ring(r).start()

        @pl.when(r == 4)
        def _():
            reduce_ring(3).relay()
            load[2].wait()
            for h in range(2):
                for k in range(4):
                    merg.wait_cross(h, k)
            save.start()

        @pl.when(r > 1)
        def _():
            q = r - 2
            rg = reduce_ring(q)
            rg.wait()
            total = own[q] + main_in[q, 0].astype(F32) + main_in[q, 1].astype(F32)
            lo[q] = total.astype(BF)
            rg.finish()
            gather_ring(q).finish()

    save.wait()
    for d in wo_send:
        d.wait_send()
    ring.finish()
    gath.finish()
    gout.finish()
    merg.finish()


def column(rows):
    n, m = rows.shape
    return jnp.concatenate([rows, jnp.zeros((128 - n, m), F32)], axis=0).T


def k_merge(
    lo, gain3, bias3, mi, seg, owners, wpg_h, pb, out,
    wpg, rows_f, fin, gb, sbuf, own, far_in, main_in, st, placed, obuf, lsem, ss, sr, xs, xr, ts, tr
):
    x, y, z, c = position()
    t = lax.axis_index("tok")
    n_tok = out.shape[0]
    slot = out.shape[1]
    merged = mi.shape[1]
    n_loc = wpg.shape[2]
    load = pltpu.make_async_copy(wpg_h, wpg, lsem.at[0])
    load.start()
    bar = pltpu.get_barrier_semaphore()

    @pl.loop(1, n_tok)
    def _(i):
        pl.semaphore_signal(bar, inc=1, device_id={"tok": (t + i) % n_tok}, device_id_type=MESH_ID)

    @pl.loop(1, 4)
    def _(i):
        pl.semaphore_signal(bar, inc=1, device_id=x_dev(x, i), device_id_type=MESH_ID)

    @pl.loop(0, 4)
    def _(i):
        rows = pl.ds(pl.multiple_of(i * 256, 256), 256)
        v = unpack_rows(lo.at[i]).astype(F32)
        rows_f[rows, :] = v
        mean = jnp.mean(v, axis=-1, keepdims=True)
        d = v - mean
        m2 = jnp.sum(d * d, axis=-1, keepdims=True)
        lane = lax.broadcasted_iota(jnp.int32, (256, 128), 1)
        both = jnp.where(lane == 0, mean, jnp.where(lane == 1, m2, 0.0))
        st[x, :, rows] = both.T[:8]

    pl.semaphore_wait(bar, n_tok + 2)
    sends = [rcopy(st.at[x], st.at[x], ss.at[k], sr.at[k], x_dev(x, k + 1)) for k in range(3)]
    for d in sends:
        d.start()
    for j in range(4):

        @pl.when(x == j)
        def _():
            gb[0:1, :] = gain3[n_loc * j : n_loc * j + n_loc].reshape(1, n_loc)
            gb[1:2, :] = bias3[n_loc * j : n_loc * j + n_loc].reshape(1, n_loc)

    idx = column(mi[...].astype(F32))
    toks = lax.broadcasted_iota(jnp.int32, (merged, 1024), 1).astype(F32)
    seg_of = jnp.sum(jnp.where(idx[:, 0:1] == toks, seg[...].astype(F32), 0.0), axis=1, keepdims=True)
    names = lax.broadcasted_iota(jnp.int32, (merged, n_tok), 1).astype(F32)
    owner = jnp.sum(jnp.where(seg_of == names, owners[...].astype(F32), 0.0), axis=1, keepdims=True)
    mine = (owner == names).astype(F32)
    below = lax.broadcasted_iota(jnp.int32, (merged, merged), 1) < lax.broadcasted_iota(
        jnp.int32, (merged, merged), 0
    )
    before = jnp.dot(
        jnp.where(below, 1.0, 0.0).astype(BF), mine.astype(BF), preferred_element_type=F32
    )
    rank = jnp.sum(before * mine, axis=1, keepdims=True)
    target = jnp.broadcast_to(owner * slot + rank, (merged, 128)).T[0:1]
    spots = lax.broadcasted_iota(jnp.int32, (n_tok * slot, merged), 0).astype(F32)
    placed[...] = jnp.where(spots == target, 1.0, 0.0).astype(BF)
    for d in sends:
        d.wait_recv()
    means = [st[s, 0:1, :] for s in range(4)]
    mean = 0.25 * (means[0] + means[1] + means[2] + means[3])
    m2 = st[0, 1:2, :] + st[1, 1:2, :] + st[2, 1:2, :] + st[3, 1:2, :]
    for s in range(4):
        d = means[s] - mean
        m2 = m2 + n_loc * (d * d)
    rstd = lax.rsqrt(m2 * (1.0 / (4 * n_loc)) + EPS)
    for i in range(8):
        sl = slice(128 * i, 128 * i + 128)
        row = lax.broadcasted_iota(jnp.int32, (128, 128), 0)
        cols = jnp.where(row == 0, mean[:, sl], jnp.where(row == 1, rstd[:, sl], 0.0)).T
        v = rows_f[sl, :]
        fin[sl, :] = ((v - cols[:, 0:1]) * cols[:, 1:2] * gb[0:1, :] + gb[1:2, :]).astype(BF)
    load.wait()
    got = []
    for k in range(4):
        pick = jnp.where(idx[:, k : k + 1] == toks, 1.0, 0.0).astype(BF)
        got.append(jnp.dot(pick, fin[...], preferred_element_type=F32).astype(BF))
    for j in range(4):
        acc = jnp.dot(got[0], wpg[j], preferred_element_type=F32)
        for k in range(1, 4):
            acc += jnp.dot(got[k], wpg[k * 4 + j], preferred_element_type=F32)
        pack_rows(acc, own.at[j])
        sbuf[j] = own[j].astype(BF)
    rg = RingReduce(sbuf, far_in, main_in, lambda k: xs.at[k], lambda k: xr.at[k], sbuf.shape[1] // 2)
    rg.start()
    rg.relay()
    rg.wait()
    own[x] += main_in[0].astype(F32) + main_in[1].astype(F32)
    total = unpack_rows(own.at[x]) + pb[...]
    going = jnp.dot(placed[...], total.astype(BF), preferred_element_type=F32).astype(BF)
    obuf[...] = going.reshape(n_tok, slot, n_loc)

    def slot_copy(i):
        to = (t + i) % n_tok
        return rcopy(obuf.at[to], out.at[t], ts.at[i], tr.at[i], {"tok": to})

    @pl.loop(1, n_tok)
    def _(i):
        slot_copy(i).start()

    keep = pltpu.make_async_copy(obuf.at[t], out.at[t], lsem.at[1])
    keep.start()
    rg.finish()
    for d in sends:
        d.wait_send()
    keep.wait()

    @pl.loop(1, n_tok)
    def _(i):
        slot_copy(i).wait()


def kernel_call(body, name, cid, ins, outs, out_specs, scratch, args):
    return pl.pallas_call(
        body,
        name=name,
        out_shape=outs,
        in_specs=ins,
        out_specs=out_specs,
        scratch_shapes=scratch,
        compiler_params=pltpu.CompilerParams(
            collective_id=cid, has_side_effects=True, vmem_limit_bytes=VLIM
        ),
    )(*args)


def sds(shape, dtype):
    return jax.ShapeDtypeStruct(shape, dtype)


DMA = pltpu.SemaphoreType.DMA


def body(
    tokens,
    segment_ids,
    merge_index,
    segment_owner,
    ln1_gain,
    ln1_bias,
    w_qkv,
    qkv_bias,
    w_out,
    out_bias,
    ln2_gain,
    ln2_bias,
    w_fc1,
    fc1_bias,
    w_fc2,
    fc2_bias,
    ln3_gain,
    ln3_bias,
    w_proj,
    proj_bias,
):
    tok = tokens[0]
    width = tok.shape[1]
    part_w = w_qkv.shape[2]
    depth = w_qkv.shape[1]
    heads = part_w // HD
    cols = 3 * heads * HPAD

    def tall(n):
        return 16 * (-(-(n // 128) * depth // 16))

    hidden = w_fc1.shape[1]
    flat = 256 * part_w // 128
    perm = []
    for bx in range(4):
        for t in range(32):
            ty, tz, tc = t // 8, (t // 2) % 4, t % 2
            perm.append((bx * 32 + t, tz * 32 + (ty * 4 + bx) * 2 + tc))
    wp = lax.ppermute(w_proj, ("blk", "tok"), perm)
    lo, wpg = kernel_call(
        k_layer,
        "layer",
        1,
        [VM] * 10 + [ANY, VM, ANY, VM, VM],
        [sds((4, flat, 128), BF), sds((32, 208, part_w), BF)],
        [VM, ANY],
        [
            pltpu.VMEM((tall(cols), 128), BF),
            pltpu.VMEM((tall(width), 128), BF),
            pltpu.VMEM((8, hidden), F32),
            pltpu.VMEM((1, cols), F32),
            pltpu.VMEM((4, depth, part_w), BF),
            pltpu.VMEM((4, 256, width), BF),
            pltpu.VMEM((3 * heads, 1024, HPAD), BF),
            pltpu.VMEM((32, tall(cols), 128), BF),
            pltpu.VMEM((32, tall(width), 128), BF),
            pltpu.VMEM((32, 208, part_w), BF),
            pltpu.VMEM((width, width), BF),
            pltpu.VMEM((4, 256, width), BF),
            pltpu.VMEM((width, hidden), BF),
            pltpu.VMEM((hidden, width), BF),
            pltpu.VMEM((4, 4, flat, 128), BF),
            pltpu.VMEM((heads, 256, HPAD), BF),
            pltpu.VMEM((1024, 128), F32),
            pltpu.VMEM((256, width), F32),
            pltpu.VMEM((256, hidden), BF),
            pltpu.VMEM((4, flat, 128), F32),
            pltpu.VMEM((4, 4, flat, 128), BF),
            pltpu.VMEM((4, 2, flat // 2, 128), BF),
            pltpu.VMEM((4, 2, flat, 128), BF),
            DMA((6,)),
            DMA((6,)),
            DMA((6,)),
            DMA((3,)),
            DMA((3,)),
            DMA((4, 6)),
            DMA((4, 6)),
            DMA((4, 6)),
            DMA((4, 6)),
        ]
        + TOK_SEMS * 3,
        (
            tok, w_qkv, w_out.T, ln1_gain, ln1_bias, qkv_bias, segment_ids, out_bias, ln2_gain,
            ln2_bias, w_fc1, fc1_bias, w_fc2, fc2_bias, wp,
        ),
    )
    merged_count = merge_index.shape[1]
    n_tok = lax.axis_size("tok")
    slot = 2 * merged_count // n_tok
    arrived = kernel_call(
        k_merge,
        "merge",
        3,
        [VM] * 6 + [ANY, VM],
        [sds((n_tok, slot, part_w), BF)],
        [VM],
        [
            pltpu.VMEM((16, part_w, part_w), BF),
            pltpu.VMEM((1024, part_w), F32),
            pltpu.VMEM((1024, part_w), BF),
            pltpu.VMEM((2, part_w), F32),
            pltpu.VMEM((4, flat, 128), BF),
            pltpu.VMEM((4, flat, 128), F32),
            pltpu.VMEM((2, flat // 2, 128), BF),
            pltpu.VMEM((2, flat, 128), BF),
            pltpu.VMEM((4, 8, 1024), F32),
            pltpu.VMEM((n_tok * slot, merged_count), BF),
            pltpu.VMEM((n_tok, slot, part_w), BF),
            DMA((2,)),
            DMA((3,)),
            DMA((3,)),
            DMA((6,)),
            DMA((6,)),
            DMA((n_tok,)),
            DMA((n_tok,)),
        ],
        (
            lo,
            ln3_gain,
            ln3_bias,
            merge_index[0].T,
            segment_ids,
            segment_owner,
            wpg.reshape(16, part_w, part_w),
            proj_bias,
        ),
    )[0]
    return arrived[None]


def solution(mesh):
    placed = (
        P("tok", "blk", None),
        P("tok", None),
        P("tok", None, None),
        P("tok", None),
        P(),
        P(),
        P(None, "tok", "blk"),
        P(None, "blk"),
        P("blk", "tok"),
        P(),
        P(),
        P(),
        P(None, "blk"),
        P("blk"),
        P("blk", None),
        P(),
        P(),
        P(),
        P("tok", "blk"),
        P("blk"),
    )
    return jax.shard_map(
        body, mesh=mesh, in_specs=placed, out_specs=P("tok", None, None, "blk"), check_vma=False
    )
```
